32 devices in a mesh: seq: 8 (over z, y), head: 4 (over x, core).
Axes of the slice: x: 2, y: 2, z: 4, core: 2. Of those that a mesh axis runs over, the one named last changes fastest.
Arguments:
- layer_input: bfloat16 [4096, 768], P('seq', 'head'), may hold values from -6 to 6
- ln1_gain: float32 [768], replicated, may hold values from 0.5 to 1.5
- ln1_bias: float32 [768], replicated, may hold values from -3 to 3
- w_query: bfloat16 [768, 768], P(None, 'head'), may hold values from -0.21875 to 0.21875
- b_query: float32 [768], P('head'), may hold values from -3 to 3
- w_key: bfloat16 [768, 768], P(None, 'head'), may hold values from -0.3125 to 0.3125
- w_value: bfloat16 [768, 768], P(None, 'head'), may hold values from -0.21875 to 0.21875
- b_value: float32 [768], P('head'), may hold values from -1.2 to 1.2
- sub_gain: float32 [768], P('head'), may hold values from 0.5 to 1.5
- sub_bias: float32 [768], P('head'), may hold values from -3 to 3
- w_out: bfloat16 [768, 768], P('head'), may hold values from -0.21875 to 0.21875
- b_out: float32 [768], replicated, may hold values from -3 to 3
- ln2_gain: float32 [768], replicated, may hold values from 0.5 to 1.5
- ln2_bias: float32 [768], replicated, may hold values from -3 to 3
- w_up: bfloat16 [768, 3072], P(None, 'head'), may hold values from -0.21875 to 0.21875
- b_up: float32 [3072], P('head'), may hold values from -3 to 3
- w_down: bfloat16 [3072, 768], P('head'), may hold values from -0.109375 to 0.109375
- b_down: float32 [768], replicated, may hold values from -3 to 3
- cotangent: bfloat16 [4096, 768], P('seq', 'head'), may hold values from -6 to 6
- row_lengths: int32 [6], replicated, may hold values from 1 to 3072, 4096 in all
Outputs:
- layer_output: bfloat16 [4096, 768], P('seq', 'head')
- grad_input: float32 [4096, 768], P('seq', 'head')
- grad_ln1_gain: float32 [768], replicated
- grad_ln1_bias: float32 [768], replicated
- grad_w_query: float32 [768, 768], P(None, 'head')
- grad_b_query: float32 [768], P('head')
- grad_w_key: float32 [768, 768], P(None, 'head')
- grad_w_value: float32 [768, 768], P(None, 'head')
- grad_b_value: float32 [768], P('head')
- grad_sub_gain: float32 [768], P('head')
- grad_sub_bias: float32 [768], P('head')
- grad_w_out: float32 [768, 768], P('head')
- grad_b_out: float32 [768], replicated
- grad_ln2_gain: float32 [768], replicated
- grad_ln2_bias: float32 [768], replicated
- grad_w_up: float32 [768, 3072], P(None, 'head')
- grad_b_up: float32 [3072], P('head')
- grad_w_down: float32 [3072, 768], P('head')
- grad_b_down: float32 [768], replicated
The draws below stay inside these ranges and needn't reach their ends.
Inputs may be any that keep to these rules, and one draw needn't show every extreme that they name: `row_lengths`: the 6 row lengths sum to 4096, and the longest is exactly 3072.
All inputs are finite; a program needn't handle non-finite values.
Results may differ from the reference program's by a relative error of at most 0.018.
Values may be sent and summed in bfloat16 or wider, within the bound.
No kernel may reach another device: no remote copies, remote signals or barrier semaphores. Data moves between devices by JAX's collectives and lax.ppermute only.
A program may use at most 256 MiB of HBM per device.

```python
import math
import jax
import jax.numpy as jnp
import numpy as np
from jax import lax

D = 768
HEADS = 12
HEAD_DIM = 64
FF = 3072
SEG = 2048
NSEQ = 6
TOKENS = 4096


def block_scale(own_key, extent, pieces, smallest, high):
    gain = 1.0
    for position, shards_of in pieces:
        steps = jax.random.uniform(jax.random.fold_in(jax.random.fold_in(own_key, 6), position), (shards_of,), jnp.float32, smallest / len(pieces), high / len(pieces))
        gain = gain * jnp.repeat(jnp.exp(steps), extent[position] // shards_of).reshape((-1,) + (1,) * (len(extent) - 1 - position))
    return gain


def profile(number_of, total, bound, lean):
    loads = [(1 << 20) // math.isqrt(rank ** lean) + 1 for rank in range(2, number_of + 1)]
    spare, counts = total - bound - (number_of - 1), [1] * (number_of - 1)
    while spare > 0:
        movable = [i for i in range(number_of - 1) if counts[i] < bound]
        whole, remaining = sum([loads[i] for i in movable]), spare
        for i in movable:
            extra = min(bound - counts[i], max(1, remaining * loads[i] // whole), spare)
            counts[i] = counts[i] + extra
            spare = spare - extra
    return np.array([bound] + counts)


def ragged_sizes(key, count, total, reach, slope):
    if count == 2:
        one = jax.random.randint(key, (), max(1, total - reach), min(reach, total - 1) + 1)
        return jnp.stack([one, total - one])
    sizes = jnp.asarray(profile(count, total, reach, slope), jnp.int32)
    twos = (count - 1) // 2
    giver, sink = sizes[1:1 + 2 * twos:2], sizes[2:2 + 2 * twos:2]
    room = jnp.minimum(giver - 1, reach - sink)
    passed = jax.random.randint(jax.random.fold_in(key, 1), (twos,), 0, 1 << 20) % (room + 1)
    sizes = sizes.at[1:1 + 2 * twos:2].set(giver - passed).at[2:2 + 2 * twos:2].set(sink + passed)
    return sizes[jax.random.permutation(jax.random.fold_in(key, 2), count)]


def bell_draw(key, dims, scale, limit, split=(), kind=jnp.bfloat16):
    drawn = jax.random.normal(key, dims, jnp.float32) * scale
    if len(split) > 0:
        drawn = block_scale(key, dims, split, -0.22, 0.18) * drawn
    return jnp.clip(drawn, min=-limit, max=limit).astype(kind)


def setup_inputs(seed: int = 0) -> dict:
    streams_of = jax.random.split(jax.random.key(seed), 21)
    return {
        "layer_input": bell_draw(streams_of[0], (TOKENS, D), 1.0, 6.0, ((0, 8), (1, 4))),
        "ln1_gain": jnp.clip(1.0 + 0.1 * jax.random.normal(streams_of[1], (D,), jnp.float32), 0.5, 1.5),
        "ln1_bias": bell_draw(streams_of[2], (D,), 0.5, 3.0, (), jnp.float32),
        "w_query": bell_draw(streams_of[3], (D, D), D ** -0.5, 0.21875, ((1, 4),)),
        "b_query": bell_draw(streams_of[4], (D,), 0.5, 3.0, ((0, 4),), jnp.float32),
        "w_key": bell_draw(streams_of[5], (D, D), (D // 2) ** -0.5, 0.3125, ((1, 4),)),
        "w_value": bell_draw(streams_of[6], (D, D), D ** -0.5, 0.21875, ((1, 4),)),
        "b_value": bell_draw(streams_of[7], (D,), 0.2, 1.2, ((0, 4),), jnp.float32),
        "sub_gain": jnp.clip(1.0 + 0.1 * jax.random.normal(streams_of[8], (D,), jnp.float32), 0.5, 1.5),
        "sub_bias": bell_draw(streams_of[9], (D,), 0.5, 3.0, ((0, 4),), jnp.float32),
        "w_out": bell_draw(streams_of[10], (D, D), D ** -0.5, 0.21875, ((0, 4),)),
        "b_out": bell_draw(streams_of[11], (D,), 0.5, 3.0, (), jnp.float32),
        "ln2_gain": jnp.clip(1.0 + 0.1 * jax.random.normal(streams_of[12], (D,), jnp.float32), 0.5, 1.5),
        "ln2_bias": bell_draw(streams_of[13], (D,), 0.5, 3.0, (), jnp.float32),
        "w_up": bell_draw(streams_of[14], (D, FF), D ** -0.5, 0.21875, ((1, 4),)),
        "b_up": bell_draw(streams_of[15], (FF,), 0.5, 3.0, ((0, 4),), jnp.float32),
        "w_down": bell_draw(streams_of[16], (FF, D), FF ** -0.5, 0.109375, ((0, 4),)),
        "b_down": bell_draw(streams_of[17], (D,), 0.5, 3.0, (), jnp.float32),
        "cotangent": bell_draw(streams_of[18], (TOKENS, D), 1.0, 6.0, ((0, 8), (1, 4))),
        "row_lengths": ragged_sizes(streams_of[19], NSEQ, TOKENS, TOKENS * 3 // 4, 2).astype(jnp.int32),
    }


@jax.custom_vjp
def low(v):
    return lax.optimization_barrier(v.astype(jnp.bfloat16)).astype(jnp.float32)

@jax.custom_vjp
def low_back(v):
    return v

def low_keep(v):
    return (low(v), None)

def low_pass(kept, grad):
    return (grad,)

def back_keep(v):
    return (v, None)

def back_low(kept, grad):
    return (low(grad),)
low.defvjp(low_keep, low_pass)
low_back.defvjp(back_keep, back_low)
eps = 1e-05
segment_scales = (1, 2, 4, 8, 16)
dilation_steps = (1, 2, 4, 6, 12)

def layer_norm(inputs, norm_gain, norm_bias):
    center = inputs - lax.optimization_barrier(jnp.mean(inputs, axis=-1, keepdims=True))
    spread = lax.optimization_barrier(jnp.mean(center * center, axis=-1, keepdims=True))
    return center * lax.rsqrt(spread + eps) * norm_gain + norm_bias

def sub_norm(inputs, norm_gain, norm_bias):
    mean_value = lax.optimization_barrier(jnp.mean(inputs, axis=-1, keepdims=True))
    square_mean = lax.optimization_barrier(jnp.mean(inputs * inputs, axis=-1, keepdims=True))
    return (inputs - mean_value) * lax.rsqrt(square_mean - mean_value * mean_value + eps) * norm_gain + norm_bias

def token_places(positions, lengths):
    row_ends = jnp.cumsum(lengths).astype(jnp.int32)
    starts = row_ends - lengths
    row_of = lax.optimization_barrier(jnp.sum((positions[:, None] >= row_ends[None, :]).astype(jnp.int32), axis=1)).astype(jnp.int32)
    onehot = (row_of[:, None] == jnp.arange(lengths.shape[0], dtype=jnp.int32)[None, :]).astype(jnp.int32)
    row_place = (positions - lax.optimization_barrier(jnp.sum(onehot * starts[None, :], axis=1))).astype(jnp.int32)
    return (row_of, row_place)

def pattern_count(head_ids, query_row, query_place, key_row, key_place):
    allowed = (query_row[:, None] == key_row[None, :]) & (key_place[None, :] <= query_place[:, None])
    counted = jnp.zeros((head_ids.shape[0], query_row.shape[0], key_row.shape[0]), jnp.float32)
    for scale_factor, step_size in zip(segment_scales, dilation_steps):
        seg_width = SEG * scale_factor
        same_seg = allowed & (query_place[:, None] // seg_width == key_place[None, :] // seg_width)
        offset = head_ids % step_size
        query_on = (query_place % seg_width % step_size)[None, :] == offset[:, None]
        key_on = (key_place % seg_width % step_size)[None, :] == offset[:, None]
        counted = counted + (same_seg[None] & query_on[:, :, None] & key_on[:, None, :]).astype(jnp.float32)
    return counted

def forward(layer_input, ln1_gain, ln1_bias, w_query, b_query, w_key, w_value, b_value, sub_gain, sub_bias, w_out, b_out, ln2_gain, ln2_bias, w_up, b_up, w_down, b_down, row_of, row_place):
    precise = lax.Precision.HIGHEST
    tokens = layer_input.shape[0]
    normed = low(layer_norm(layer_input, ln1_gain, ln1_bias))
    queries = low_back(low(jnp.dot(normed, w_query, precision=precise) + b_query)).reshape(tokens, HEADS, HEAD_DIM)
    key_rows = low_back(low(jnp.dot(normed, w_key, precision=precise))).reshape(tokens, HEADS, HEAD_DIM)
    values = low_back(low(jnp.dot(normed, w_value, precision=precise) + b_value)).reshape(tokens, HEADS, HEAD_DIM)
    head_ids = jnp.arange(HEADS, dtype=jnp.int32)
    block_rows = min(tokens, 512)

    def attend(first_row):
        query_blk = lax.dynamic_slice_in_dim(queries, first_row, block_rows, 0)
        query_row = lax.dynamic_slice_in_dim(row_of, first_row, block_rows, 0)
        query_place = lax.dynamic_slice_in_dim(row_place, first_row, block_rows, 0)
        scores = low_back(jnp.einsum('qhd,khd->hqk', query_blk, key_rows, precision=precise) * HEAD_DIM ** (-0.5))
        counted = pattern_count(head_ids, query_row, query_place, row_of, row_place)
        is_live = counted > 0
        masked = jnp.where(is_live, scores, -1e+30)
        highest = lax.optimization_barrier(jnp.max(masked, axis=-1, keepdims=True))
        weights = counted * jnp.exp(masked - highest)
        weights_norm = weights / lax.optimization_barrier(jnp.sum(weights, axis=-1, keepdims=True))
        return jnp.einsum('hqk,khd->qhd', low(weights_norm), values, precision=precise)
    starts = jnp.arange(0, tokens, block_rows, dtype=jnp.int32)
    mixed_heads = lax.map(jax.checkpoint(attend), starts).reshape(tokens, HEADS * HEAD_DIM)
    mixed_heads = low_back(mixed_heads)
    sub_out = low(sub_norm(mixed_heads, sub_gain, sub_bias))
    branch = low_back(jnp.dot(sub_out, w_out, precision=precise) + b_out)
    middle = layer_input + branch
    normed_mid = low(layer_norm(middle, ln2_gain, ln2_bias))
    inner_act = low_back(jnp.dot(normed_mid, w_up, precision=precise) + b_up)
    active = low(jax.nn.gelu(inner_act, approximate=False))
    return middle + (jnp.dot(active, w_down, precision=precise) + b_down)

def reference(layer_input, ln1_gain, ln1_bias, w_query, b_query, w_key, w_value, b_value, sub_gain, sub_bias, w_out, b_out, ln2_gain, ln2_bias, w_up, b_up, w_down, b_down, cotangent, row_lengths):
    floats = tuple((a.astype(jnp.float32) for a in (layer_input, ln1_gain, ln1_bias, w_query, b_query, w_key, w_value, b_value, sub_gain, sub_bias, w_out, b_out, ln2_gain, ln2_bias, w_up, b_up, w_down, b_down)))
    positions = jnp.arange(layer_input.shape[0], dtype=jnp.int32)
    row_of, row_place = token_places(positions, row_lengths.astype(jnp.int32))

    def whole(*params):
        return forward(*params, row_of, row_place)
    result, pull_back = jax.vjp(whole, *floats)
    gradients = pull_back(cotangent.astype(jnp.float32))
    return (result.astype(jnp.bfloat16), gradients[0], gradients[1], gradients[2], gradients[3], gradients[4], gradients[5], gradients[6], gradients[7], gradients[8], gradients[9], gradients[10], gradients[11], gradients[12], gradients[13], gradients[14], gradients[15], gradients[16], gradients[17])
```

```python
import functools
import math

import jax
import jax.numpy as jnp
import numpy as np
from jax import lax
from jax.experimental import pallas as pl
from jax.experimental.pallas import tpu as pltpu
from jax.sharding import PartitionSpec as P

HEAD_DIM = 64
SEG = 2048


eps = 1e-05
segment_scales = (1, 2, 4, 8, 16)
dilation_steps = (1, 2, 4, 6, 12)


def layer_norm(inputs, norm_gain, norm_bias):
    center = inputs - jnp.mean(inputs, axis=-1, keepdims=True)
    spread = jnp.mean(center * center, axis=-1, keepdims=True)
    return center * lax.rsqrt(spread + eps) * norm_gain + norm_bias


bf=jnp.bfloat16; f32=jnp.float32
scales=(1,2,4,8,16); steps=(1,2,4,6,12)
NT=(((1,),(1,)),((),()))
NN=(((1,),(0,)),((),()))
def dot(a,b,dims=NN): return lax.dot_general(a,b,dims,preferred_element_type=f32)

def features(total, lengths, head_ids, nh):
    nrow=lengths.shape[0]
    pos=jnp.arange(total,dtype=jnp.int32)
    tri=np.tril(np.ones((nrow,nrow),np.int32))
    ends=jnp.sum(tri*lengths[None,:],axis=1); starts=ends-lengths
    past=(pos[:,None]>=ends[None,:])
    row_start=jnp.sum(jnp.where(past,lengths[None,:],0),axis=1)
    place=pos-row_start
    sizes=[nrow+total//(SEG*s) for s in scales]
    nf=sum(sizes); width=-(-nh*nf//128)*128
    lane=np.arange(width); lh=lane//nf; lf=lane%nf
    jl=jnp.sum(jnp.where(lh[None,:]==np.arange(nh)[:,None],head_ids[:,None],0),axis=0)
    out=jnp.zeros((total,width),jnp.bool_); off=0
    for s,r,n in zip(scales,steps,sizes):
        w=SEG*s
        nseg=(lengths+(w-1))//w
        base=jnp.sum(jnp.where(past,nseg[None,:],0),axis=1)
        sg=base+place//w+off
        pm=place%w%r
        lanek=(lf>=off)&(lf<off+n)&(lh<nh)
        fl=jnp.where(lanek,lf,-1); jm=jnp.where(lanek,jl%r,-1)
        out=out|((sg[:,None]==fl[None,:])&(pm[:,None]==jm[None,:]))
        off+=n
    return out.astype(bf), nf

def head_pad(x,h,hi):
    part=x[:,64*h:64*h+64]; z=jnp.zeros_like(part)
    return jnp.concatenate([z,part] if hi else [part,z],axis=1)

def tile_needed(sc,i,n,bk):
    gb=sc[i]; own=sc[n]; st=sc[n+1]
    return gb, own, (gb<=own)&((gb+1)*bk>st)

def count_tile(fk,fq,h,nf,gb,own,bk,tq):
    lane=lax.broadcasted_iota(jnp.int32,fq.shape,1)
    fqh=jnp.where((lane>=h*nf)&(lane<(h+1)*nf),fq.astype(f32),0.0).astype(bf)
    c=dot(fk,fqh,NT)
    ks=gb*bk+lax.broadcasted_iota(jnp.int32,(bk,1),0); qs=own*tq+lax.broadcasted_iota(jnp.int32,(1,tq),1)
    return jnp.where(ks<=qs,c,0.0)

def fwd_kernel(nh,nf,n,sc,q,fq,kv,fk,out,lse,acc,m,l):
    i=pl.program_id(0); bk=kv.shape[1]; tq=q.shape[0]
    @pl.when(i==0)
    def _():
        acc[...]=jnp.zeros_like(acc); m[...]=jnp.full_like(m,-1e30); l[...]=jnp.zeros_like(l)
    gb,own,need=tile_needed(sc,i,n,bk)
    @pl.when(need)
    def _():
        kvT=kv[0].astype(f32).T.astype(bf)
        qs=(q[...].astype(f32)*0.125).astype(bf)
        for h in range(nh):
            kvh=kv[0,:,128*h:128*h+128]
            s=dot(kvh,head_pad(qs,h,0),NT)
            c=count_tile(fk[...],fq[...],h,nf,gb,own,bk,tq)
            s=jnp.where(c>0,s,-1e30)
            mo=m[h:h+1,:]; mn=jnp.maximum(mo,jnp.max(s,axis=0,keepdims=True))
            p=c*jnp.exp(s-mn)
            al=jnp.exp(mo-mn)
            l[h:h+1,:]=l[h:h+1,:]*al+jnp.sum(p,axis=0,keepdims=True)
            o=dot(kvT[128*h:128*h+128],p.astype(bf))
            acc[64*h:64*h+64,:]=acc[64*h:64*h+64,:]*al+o[64:,:]
            m[h:h+1,:]=mn
    @pl.when(i==n-1)
    def _():
        for h in range(nh):
            acc[64*h:64*h+64,:]=acc[64*h:64*h+64,:]/l[h:h+1,:]
        out[...]=acc[...].T
        lse[...]=m[...]+jnp.log(jnp.maximum(l[...],1e-30))

def bwd_kernel(nh,nf,n,sc,q,fq,do,att,lse,kv,fk,dq,dkv,dqT,dterm):
    i=pl.program_id(0); bk=kv.shape[1]; tq=q.shape[0]
    @pl.when(i==0)
    def _():
        dqT[...]=jnp.zeros_like(dqT)
        prod=do[...].astype(f32)*att[...]
        r=lax.broadcasted_iota(jnp.int32,(8,prod.shape[1]),0); c=lax.broadcasted_iota(jnp.int32,(8,prod.shape[1]),1)
        sel=jnp.where(c//64==r,1.0,0.0).astype(f32)
        dterm[...]=lax.dot_general(sel,prod,NT,precision=lax.Precision.HIGHEST,preferred_element_type=f32)
    gb,own,need=tile_needed(sc,i,n,bk)
    @pl.when(jnp.logical_not(need))
    def _(): dkv[...]=jnp.zeros_like(dkv)
    @pl.when(need)
    def _():
        kvT=kv[0].astype(f32).T.astype(bf)
        qs=(q[...].astype(f32)*0.125).astype(bf)
        for h in range(nh):
            kvh=kv[0,:,128*h:128*h+128]
            qh=head_pad(qs,h,0); doh=head_pad(do[...],h,1)
            s=dot(kvh,qh,NT)
            c=count_tile(fk[...],fq[...],h,nf,gb,own,bk,tq)
            p=c*jnp.exp(jnp.minimum(s-lse[h:h+1,:],1.0))
            ds=p*(dot(kvh,doh,NT)-dterm[h:h+1,:])
            pb=p.astype(bf); dsb=ds.astype(bf)
            dkv[0,:,128*h:128*h+128]=(dot(dsb,qh)+dot(pb,doh)).astype(dkv.dtype)
            o=dot(kvT[128*h:128*h+128],dsb)
            dqT[64*h:64*h+64,:]+=o[:64,:]
    @pl.when(i==n-1)
    def _(): dq[...]=(dqT[...].T*0.125).astype(dq.dtype)

def attend_fwd(q,F,nf,own,kv,sc,n):
    tq,wd=q.shape; nh=wd//64; bk=kv.shape[1]; W=F.shape[1]
    full=lambda a,b: pl.BlockSpec((a,b),lambda i,s:(0,0))
    gs=pltpu.PrefetchScalarGridSpec(num_scalar_prefetch=1,grid=(n,),
      in_specs=[full(tq,wd),pl.BlockSpec((tq,W),lambda i,s:(s[n],0)),pl.BlockSpec((1,bk,2*wd),lambda i,s:(i,0,0)),pl.BlockSpec((bk,W),lambda i,s:(s[i],0))],
      out_specs=[full(tq,wd),full(8,tq)],
      scratch_shapes=[pltpu.VMEM((wd,tq),f32),pltpu.VMEM((8,tq),f32),pltpu.VMEM((8,tq),f32)])
    return pl.pallas_call(functools.partial(fwd_kernel,nh,nf,n),grid_spec=gs,
      out_shape=[jax.ShapeDtypeStruct((tq,wd),f32),jax.ShapeDtypeStruct((8,tq),f32)],
      compiler_params=pltpu.CompilerParams(dimension_semantics=("arbitrary",),vmem_limit_bytes=48<<20),name="attend_fwd")(sc,q,F,kv,F)

def attend_bwd(q,F,nf,do,att,lse,kv,sc,n):
    tq,wd=q.shape; nh=wd//64; bk=kv.shape[1]; W=F.shape[1]
    full=lambda a,b: pl.BlockSpec((a,b),lambda i,s:(0,0))
    gs=pltpu.PrefetchScalarGridSpec(num_scalar_prefetch=1,grid=(n,),
      in_specs=[full(tq,wd),pl.BlockSpec((tq,W),lambda i,s:(s[n],0)),full(tq,wd),full(tq,wd),full(8,tq),pl.BlockSpec((1,bk,2*wd),lambda i,s:(i,0,0)),pl.BlockSpec((bk,W),lambda i,s:(s[i],0))],
      out_specs=[full(tq,wd),pl.BlockSpec((1,bk,2*wd),lambda i,s:(i,0,0))],
      scratch_shapes=[pltpu.VMEM((wd,tq),f32),pltpu.VMEM((8,tq),f32)])
    return pl.pallas_call(functools.partial(bwd_kernel,nh,nf,n),grid_spec=gs,
      out_shape=[jax.ShapeDtypeStruct((tq,wd),bf),jax.ShapeDtypeStruct(kv.shape,bf)],
      compiler_params=pltpu.CompilerParams(dimension_semantics=("arbitrary",),vmem_limit_bytes=48<<20),name="attend_bwd")(sc,q,F,do,att,lse,kv,F)

RING=(0,2,4,6,7,5,3,1)
FWD=[(RING[i],RING[(i+1)%8]) for i in range(8)]
BWD=[(b,a) for a,b in FWD]

def ring_gather(x):
    a=b=x; got=[x]; h=x.shape[0]//2
    for _ in range(3):
        a=lax.ppermute(a,"seq",FWD); b=lax.ppermute(b,"seq",BWD); got+=[a,b]
    got.append(jnp.concatenate([lax.ppermute(a[:h],"seq",FWD),lax.ppermute(b[h:],"seq",BWD)],axis=0))
    return got

def ring_order(seq_pos):
    ring=jnp.asarray(RING,jnp.int32)
    pos=jnp.sum(jnp.where(ring==seq_pos,jnp.arange(8,dtype=jnp.int32),0))
    return ring[(pos+jnp.asarray([0,-1,1,-2,2,-3,3,4],jnp.int32))%8]

def ring_scatter(t):
    add=lambda u,v:(u.astype(jnp.float32)+v.astype(jnp.float32)).astype(u.dtype)
    h=t[0].shape[0]//2
    a=lax.ppermute(t[7][:h],"seq",FWD); b=lax.ppermute(t[7][h:],"seq",BWD)
    a=jnp.concatenate([add(t[6][:h],a),t[6][h:]],axis=0); b=jnp.concatenate([t[5][:h],add(t[5][h:],b)],axis=0)
    a=lax.ppermute(a,"seq",FWD); b=lax.ppermute(b,"seq",BWD)
    a=add(t[4],a); b=add(t[3],b)
    a=lax.ppermute(a,"seq",FWD); b=lax.ppermute(b,"seq",BWD)
    a=add(t[2],a); b=add(t[1],b)
    a=lax.ppermute(a,"seq",FWD); b=lax.ppermute(b,"seq",BWD)
    return t[0].astype(jnp.float32)+a.astype(jnp.float32)+b.astype(jnp.float32)

def shards(
    layer_input,
    ln1_gain,
    ln1_bias,
    w_query,
    b_query,
    w_key,
    w_value,
    b_value,
    sub_gain,
    sub_bias,
    w_out,
    b_out,
    ln2_gain,
    ln2_bias,
    w_up,
    b_up,
    w_down,
    b_down,
    cotangent,
    row_lengths,
):
    rows_local = layer_input.shape[0]
    slice_width = layer_input.shape[1]
    head_share = w_query.shape[1]
    local_heads = head_share // HEAD_DIM
    head_pos = lax.axis_index("head")
    seq_pos = lax.axis_index("seq")
    full_width = head_share * lax.axis_size("head")
    head_ids = head_pos * local_heads + jnp.arange(local_heads, dtype=jnp.int32)
    input_whole = lax.all_gather(layer_input, "head", axis=1, tiled=True).astype(jnp.float32)
    normed = layer_norm(input_whole, ln1_gain, ln1_bias).astype(jnp.bfloat16)
    queries = (jnp.dot(normed, w_query, preferred_element_type=jnp.float32) + b_query).astype(
        jnp.bfloat16
    )
    key_rows = jnp.dot(normed, w_key, preferred_element_type=jnp.float32).astype(jnp.bfloat16)
    values = (jnp.dot(normed, w_value, preferred_element_type=jnp.float32) + b_value).astype(
        jnp.bfloat16
    )
    total=rows_local*lax.axis_size("seq")
    F,nf=features(total,row_lengths,head_ids,local_heads)
    first=seq_pos*rows_local
    run_ends=jnp.sum(np.tril(np.ones((row_lengths.shape[0],)*2,np.int32))*row_lengths[None,:],axis=1)
    row_begin=jnp.sum(jnp.where(first>=run_ends,row_lengths,0))
    kv=jnp.stack([key_rows.reshape(rows_local,local_heads,HEAD_DIM),values.reshape(rows_local,local_heads,HEAD_DIM)],axis=2).reshape(rows_local,2*head_share)
    n_seq=lax.axis_size("seq")
    if n_seq==8:
        kv_tiles=jnp.stack(ring_gather(kv),axis=0); order=ring_order(seq_pos)
    else:
        kv_tiles=lax.all_gather(kv,"seq",axis=0); order=jnp.arange(n_seq,dtype=jnp.int32)
    sc=jnp.concatenate([order,jnp.stack([seq_pos,row_begin]).astype(jnp.int32)])
    mixed_heads,lse=attend_fwd(queries,F,nf,None,kv_tiles,sc,n_seq)
    row_sum, row_square = lax.psum(
        (jnp.sum(mixed_heads, axis=1), jnp.sum(mixed_heads * mixed_heads, axis=1)), "head"
    )
    mean_value = row_sum / full_width
    inv_std = lax.rsqrt(row_square / full_width - mean_value * mean_value + eps)
    centered = (mixed_heads - mean_value[:, None]) * inv_std[:, None]
    sub_out = (centered * sub_gain + sub_bias).astype(jnp.bfloat16)
    projected = lax.psum_scatter(
        jnp.dot(sub_out, w_out, preferred_element_type=jnp.float32).astype(jnp.bfloat16),
        "head",
        scatter_dimension=1,
        tiled=True,
    ).astype(jnp.float32)
    out_bias_share = lax.dynamic_slice_in_dim(b_out, head_pos * slice_width, slice_width, 0)
    middle = layer_input.astype(jnp.float32) + (projected + out_bias_share)
    middle_whole = lax.all_gather(middle.astype(jnp.bfloat16), "head", axis=1, tiled=True).astype(
        middle.dtype
    )
    normed_mid = layer_norm(middle_whole, ln2_gain, ln2_bias).astype(jnp.bfloat16)
    inner_act = jnp.dot(normed_mid, w_up, preferred_element_type=jnp.float32) + b_up
    active = jax.nn.gelu(inner_act, approximate=False).astype(jnp.bfloat16)
    ffn_out = lax.psum_scatter(
        jnp.dot(active, w_down, preferred_element_type=jnp.float32).astype(jnp.bfloat16),
        "head",
        scatter_dimension=1,
        tiled=True,
    ).astype(jnp.float32)
    down_bias_share = lax.dynamic_slice_in_dim(b_down, head_pos * slice_width, slice_width, 0)
    layer_output = (middle + (ffn_out + down_bias_share)).astype(jnp.bfloat16)
    grad_whole = lax.all_gather(cotangent, "head", axis=1, tiled=True)
    grad_float = grad_whole.astype(jnp.float32)
    grad_w_down = jnp.dot(active.T, grad_whole, preferred_element_type=jnp.float32)
    grad_b_down = jnp.sum(grad_float, axis=0)
    grad_active = jnp.dot(grad_whole, w_down.T, preferred_element_type=jnp.float32)
    unused, gelu_back = jax.vjp(lambda inputs: jax.nn.gelu(inputs, approximate=False), inner_act)
    grad_inner = gelu_back(grad_active)[0].astype(jnp.bfloat16)
    grad_w_up = jnp.dot(normed_mid.T, grad_inner, preferred_element_type=jnp.float32)
    grad_b_up = jnp.sum(grad_inner.astype(jnp.float32), axis=0)
    grad_norm_mid = lax.psum(
        jnp.dot(grad_inner, w_up.T, preferred_element_type=jnp.float32).astype(jnp.bfloat16), "head"
    ).astype(jnp.float32)
    unused, mid_back = jax.vjp(layer_norm, middle_whole, ln2_gain, ln2_bias)
    grad_mid_norm, grad_ln2_gain, grad_ln2_bias = mid_back(grad_norm_mid)
    grad_middle = grad_float + grad_mid_norm
    grad_branch = grad_middle.astype(jnp.bfloat16)
    grad_b_out = jnp.sum(grad_branch.astype(jnp.float32), axis=0)
    grad_w_out = jnp.dot(sub_out.T, grad_branch, preferred_element_type=jnp.float32)
    grad_sub = jnp.dot(grad_branch, w_out.T, preferred_element_type=jnp.float32)
    grad_sub_gain = jnp.sum(grad_sub * centered, axis=0)
    grad_sub_bias = jnp.sum(grad_sub, axis=0)
    grad_hat = grad_sub * sub_gain
    hat_sum, hat_cross = lax.psum(
        (jnp.sum(grad_hat, axis=1), jnp.sum(grad_hat * centered, axis=1)), "head"
    )
    grad_mixed = inv_std[:, None] * (
        grad_hat - hat_sum[:, None] / full_width - centered * hat_cross[:, None] / full_width
    )
    grad_queries,dkv=attend_bwd(queries,F,nf,grad_mixed.astype(jnp.bfloat16),mixed_heads,lse,kv_tiles,sc,n_seq)
    if n_seq==8:
        kv_grads=ring_scatter([dkv[i] for i in range(8)])
    else:
        kv_grads=lax.psum_scatter(dkv,"seq",scatter_dimension=0,tiled=False).astype(jnp.float32)
    kv_grads=kv_grads.reshape(rows_local,local_heads,2,HEAD_DIM)
    grad_keys=kv_grads[:,:,0].reshape(rows_local,head_share).astype(jnp.bfloat16)
    grad_values=kv_grads[:,:,1].reshape(rows_local,head_share).astype(jnp.bfloat16)
    grad_w_query = jnp.dot(normed.T, grad_queries, preferred_element_type=jnp.float32)
    grad_b_query = jnp.sum(grad_queries.astype(jnp.float32), axis=0)
    grad_w_key = jnp.dot(normed.T, grad_keys, preferred_element_type=jnp.float32)
    grad_w_value = jnp.dot(normed.T, grad_values, preferred_element_type=jnp.float32)
    grad_b_value = jnp.sum(grad_values.astype(jnp.float32), axis=0)
    grad_normed = (
        jnp.dot(grad_queries, w_query.T, preferred_element_type=jnp.float32)
        + jnp.dot(grad_keys, w_key.T, preferred_element_type=jnp.float32)
        + jnp.dot(grad_values, w_value.T, preferred_element_type=jnp.float32)
    )
    grad_normed = lax.psum(grad_normed.astype(jnp.bfloat16), "head").astype(jnp.float32)
    unused, input_back = jax.vjp(layer_norm, input_whole, ln1_gain, ln1_bias)
    grad_in_norm, grad_ln1_gain, grad_ln1_bias = input_back(grad_normed)
    grad_input_whole = grad_middle + grad_in_norm
    grad_input = lax.dynamic_slice_in_dim(grad_input_whole, head_pos * slice_width, slice_width, 1)
    summed = lax.psum(
        (
            grad_ln1_gain,
            grad_ln1_bias,
            grad_w_query,
            grad_b_query,
            grad_w_key,
            grad_w_value,
            grad_b_value,
            grad_sub_gain,
            grad_sub_bias,
            grad_w_out,
            grad_b_out,
            grad_ln2_gain,
            grad_ln2_bias,
            grad_w_up,
            grad_b_up,
            grad_w_down,
            grad_b_down,
        ),
        "seq",
    )
    return (layer_output, grad_input) + tuple(summed)


def solution(mesh):
    in_specs = (
        P("seq", "head"),
        P(),
        P(),
        P(None, "head"),
        P("head"),
        P(None, "head"),
        P(None, "head"),
        P("head"),
        P("head"),
        P("head"),
        P("head", None),
        P(),
        P(),
        P(),
        P(None, "head"),
        P("head"),
        P("head", None),
        P(),
        P("seq", "head"),
        P(),
    )
    out_specs = (
        P("seq", "head"),
        P("seq", "head"),
        P(),
        P(),
        P(None, "head"),
        P("head"),
        P(None, "head"),
        P(None, "head"),
        P("head"),
        P("head"),
        P("head"),
        P("head", None),
        P(),
        P(),
        P(),
        P(None, "head"),
        P("head"),
        P("head", None),
        P(),
    )
    return jax.shard_map(shards, mesh=mesh, in_specs=in_specs, out_specs=out_specs, check_vma=False)
```

```python
import functools

import jax
import jax.numpy as jnp
import numpy as np
from jax import lax
from jax.experimental import pallas as pl
from jax.experimental.pallas import tpu as pltpu
from jax.sharding import PartitionSpec as P

HEAD_DIM = 64
SEG = 2048
eps = 1e-05
segment_scales = (1, 2, 4, 8, 16)
dilation_steps = (1, 2, 4, 6, 12)
bf16 = jnp.bfloat16
f32 = jnp.float32
NT = (((1,), (1,)), ((), ()))
NN = (((1,), (0,)), ((), ()))
TN = (((0,), (0,)), ((), ()))
VMEM_LIMIT = 56 << 20

RING = (0, 2, 4, 6, 7, 5, 3, 1)
FWD = [(RING[i], RING[(i + 1) % 8]) for i in range(8)]
BWD = [(b, a) for a, b in FWD]
CORE = [(0, 1), (1, 0), (2, 3), (3, 2)]
CROSS = [(0, 2), (2, 0), (1, 3), (3, 1)]
BOTH = [(0, 3), (3, 0), (1, 2), (2, 1)]


def dot(a, b, dims=NN):
    return lax.dot_general(a, b, dims, preferred_element_type=f32)


def add_low(u, v):
    return (u.astype(f32) + v.astype(f32)).astype(u.dtype)


def ring_order(seq_pos):
    ring = jnp.asarray(RING, jnp.int32)
    pos = jnp.sum(jnp.where(ring == seq_pos, jnp.arange(8, dtype=jnp.int32), 0))
    return ring[(pos + jnp.asarray([0, -1, 1, -2, 2, -3, 3, 4], jnp.int32)) % 8]


def exchange(step):
    return [(i, i ^ step) for i in range(8)]


def halve_double(x):
    idx = lax.axis_index("seq")
    for step in (1, 2, 4):
        half = x.shape[0] // 2
        bit = (idx // step) % 2
        keep = lax.dynamic_slice_in_dim(x, bit * half, half, 0)
        send = lax.dynamic_slice_in_dim(x, (1 - bit) * half, half, 0)
        x = add_low(keep, lax.ppermute(send, "seq", exchange(step)))
    for step in (4, 2, 1):
        bit = (idx // step) % 2
        r = lax.ppermute(x, "seq", exchange(step))
        x = jnp.where(bit == 0, jnp.concatenate([x, r], axis=0), jnp.concatenate([r, x], axis=0))
    return x


def head_pieces(own, core, cross, both):
    return (
        own,
        lax.ppermute(core, "head", CORE),
        lax.ppermute(cross, "head", CROSS),
        lax.ppermute(both, "head", BOTH),
    )


def head_whole(x):
    p = lax.ppermute(x, "head", CROSS)
    return x, lax.ppermute(x, "head", CORE), p, lax.ppermute(p, "head", CORE)


def features(total, lengths, head_ids, nh):
    nrow = lengths.shape[0]
    pos = jnp.arange(total, dtype=jnp.int32)
    ends = jnp.sum(np.tril(np.ones((nrow, nrow), np.int32)) * lengths[None, :], axis=1)
    past = pos[:, None] >= ends[None, :]
    place = pos - jnp.sum(jnp.where(past, lengths[None, :], 0), axis=1)
    sizes = [nrow + total // (SEG * s) for s in segment_scales]
    nf = sum(sizes)
    width = -(-nh * nf // 128) * 128
    lane = np.arange(width)
    lane_head, lane_feature = lane // nf, lane % nf
    head_of = jnp.sum(
        jnp.where(lane_head[None, :] == np.arange(nh)[:, None], head_ids[:, None], 0), axis=0
    )
    out = jnp.zeros((total, width), jnp.bool_)
    first = 0
    for scale, step, size in zip(segment_scales, dilation_steps, sizes):
        seg_width = SEG * scale
        pieces = (lengths + (seg_width - 1)) // seg_width
        seg = jnp.sum(jnp.where(past, pieces[None, :], 0), axis=1) + place // seg_width + first
        residue = place % seg_width % step
        here = (lane_feature >= first) & (lane_feature < first + size) & (lane_head < nh)
        lane_seg = jnp.where(here, lane_feature, -1)
        lane_res = jnp.where(here, head_of % step, -1)
        out = out | ((seg[:, None] == lane_seg[None, :]) & (residue[:, None] == lane_res[None, :]))
        first += size
    return out.astype(bf16), nf


def head_pad(x, h, upper):
    part = x[:, HEAD_DIM * h : HEAD_DIM * (h + 1)]
    zero = jnp.zeros_like(part)
    return jnp.concatenate([zero, part] if upper else [part, zero], axis=1)


def count_tile(fk, fq, h, nf, first_key, first_row):
    lane = lax.broadcasted_iota(jnp.int32, fq.shape, 1)
    fqh = jnp.where((lane >= h * nf) & (lane < (h + 1) * nf), fq.astype(f32), 0.0).astype(bf16)
    count = dot(fk, fqh, NT)
    keys = first_key + lax.broadcasted_iota(jnp.int32, (count.shape[0], 1), 0)
    rows = first_row + lax.broadcasted_iota(jnp.int32, (1, count.shape[1]), 1)
    return jnp.where(keys <= rows, count, 0.0)


def fwd_tile(nh, nf, q, fq, kv, fk, first_key, first_row, acc, m, l):
    kv_t = kv[...].astype(f32).T.astype(bf16)
    qs = (q[...].astype(f32) * HEAD_DIM**-0.5).astype(bf16)
    for h in range(nh):
        s = dot(kv[:, 128 * h : 128 * h + 128], head_pad(qs, h, False), NT)
        count = count_tile(fk[...], fq[...], h, nf, first_key, first_row)
        s = jnp.where(count > 0, s, -1e30)
        old = m[h : h + 1, :]
        new = jnp.maximum(old, jnp.max(s, axis=0, keepdims=True))
        p = count * jnp.exp(s - new)
        factor = jnp.exp(old - new)
        l[h : h + 1, :] = l[h : h + 1, :] * factor + jnp.sum(p, axis=0, keepdims=True)
        o = dot(kv_t[128 * h : 128 * h + 128], p.astype(bf16))
        acc[64 * h : 64 * h + 64, :] = acc[64 * h : 64 * h + 64, :] * factor + o[64:, :]
        m[h : h + 1, :] = new


def bwd_tile(nh, nf, q, fq, do, lse, dterm, kv, fk, first_key, first_row, dq_t):
    kv_t = kv[...].astype(f32).T.astype(bf16)
    qs = (q[...].astype(f32) * HEAD_DIM**-0.5).astype(bf16)
    out = []
    for h in range(nh):
        kvh = kv[:, 128 * h : 128 * h + 128]
        qh = head_pad(qs, h, False)
        doh = head_pad(do[...], h, True)
        count = count_tile(fk[...], fq[...], h, nf, first_key, first_row)
        p = count * jnp.exp(jnp.minimum(dot(kvh, qh, NT) - lse[h : h + 1, :], 1.0))
        ds = (p * (dot(kvh, doh, NT) - dterm[h : h + 1, :])).astype(bf16)
        out.append((dot(ds, qh) + dot(p.astype(bf16), doh)).astype(bf16))
        o = dot(kv_t[128 * h : 128 * h + 128], ds)
        dq_t[64 * h : 64 * h + 64, :] += o[:64, :]
    return out


def fwd_start(acc, m, l):
    acc[...] = jnp.zeros_like(acc)
    m[...] = jnp.full_like(m, -1e30)
    l[...] = jnp.zeros_like(l)


def fwd_end(nh, quarters, acc, m, l, out, lse, msgs):
    for h in range(nh):
        out[:, 64 * h : 64 * h + 64] = (acc[64 * h : 64 * h + 64, :] / l[h : h + 1, :]).T
    lse[...] = m[...] + jnp.log(jnp.maximum(l[...], 1e-30))
    rows = msgs[0].shape[0]
    for at, msg in zip(quarters, msgs):
        msg[...] = out[pl.ds(pl.multiple_of(at * rows, rows), rows), :].astype(bf16)


def bwd_start(nh, quarters, pieces, att, do, dterm, dq_t):
    dq_t[...] = jnp.zeros_like(dq_t)
    rows = pieces[0].shape[0]
    for at, piece in zip(quarters, pieces):
        do[pl.ds(pl.multiple_of(at * rows, rows), rows), :] = piece[...]
    prod = do[...].astype(f32) * att[...]
    r = lax.broadcasted_iota(jnp.int32, (8, prod.shape[1]), 0)
    c = lax.broadcasted_iota(jnp.int32, (8, prod.shape[1]), 1)
    pick = jnp.where(c // HEAD_DIM == r, 1.0, 0.0).astype(f32)
    dterm[...] = lax.dot_general(
        pick, prod, NT, precision=lax.Precision.HIGHEST, preferred_element_type=f32
    )


def tile_needed(tile, sc, bk):
    return (tile <= sc[0]) & ((tile + 1) * bk > sc[1])


SC = 6


def fwd_grid(nh, nf, n, sc, q, fq, kv, fk, out, lse, m0, m1, m2, m3, acc, m, l):
    i = pl.program_id(0)
    bk = kv.shape[1]

    @pl.when(i == 0)
    def _():
        fwd_start(acc, m, l)

    @pl.when(tile_needed(sc[SC + i], sc, bk))
    def _():
        fwd_tile(nh, nf, q, fq, kv.at[0], fk, sc[SC + i] * bk, sc[0] * q.shape[0], acc, m, l)

    @pl.when(i == n - 1)
    def _():
        fwd_end(nh, [sc[2 + r] for r in range(4)], acc, m, l, out, lse, (m0, m1, m2, m3))


def bwd_grid(nh, nf, n, sc, q, fq, d0, d1, d2, d3, att, lse, kv, fk, dq, dkv, do, dterm, dq_t):
    i = pl.program_id(0)
    bk = kv.shape[1]

    @pl.when(i == 0)
    def _():
        bwd_start(nh, [sc[2 + r] for r in range(4)], (d0, d1, d2, d3), att, do, dterm, dq_t)

    need = tile_needed(sc[SC + i], sc, bk)

    @pl.when(jnp.logical_not(need))
    def _():
        dkv[...] = jnp.zeros_like(dkv)

    @pl.when(need)
    def _():
        out = bwd_tile(
            nh, nf, q, fq, do, lse, dterm, kv.at[0], fk, sc[SC + i] * bk, sc[0] * q.shape[0], dq_t
        )
        for h in range(nh):
            dkv[0, :, 128 * h : 128 * h + 128] = out[h]

    @pl.when(i == n - 1)
    def _():
        dq[...] = (dq_t[...].T * HEAD_DIM**-0.5).astype(dq.dtype)


def whole_block(*shape):
    return pl.BlockSpec(shape, lambda i, s: (0,) * len(shape))


def struct(shape, dtype):
    return jax.ShapeDtypeStruct(shape, dtype)


def params():
    return pltpu.CompilerParams(
        dimension_semantics=("arbitrary",), vmem_limit_bytes=VMEM_LIMIT
    )


def fwd_outs(tq, wd):
    return [struct((tq, wd), f32), struct((8, tq), f32)] + [struct((tq // 4, wd), bf16)] * 4


def attend_fwd(q, feats, nf, kv, sc, n):
    tq, wd = q.shape
    bk, width = kv.shape[1], feats.shape[1]
    outs = fwd_outs(tq, wd)
    return pl.pallas_call(
        functools.partial(fwd_grid, wd // HEAD_DIM, nf, n),
        grid_spec=pltpu.PrefetchScalarGridSpec(
            num_scalar_prefetch=1,
            grid=(n,),
            in_specs=[
                whole_block(tq, wd),
                pl.BlockSpec((tq, width), lambda i, s: (s[0], 0)),
                pl.BlockSpec((1, bk, 2 * wd), lambda i, s: (i, 0, 0)),
                pl.BlockSpec((bk, width), lambda i, s: (s[SC + i], 0)),
            ],
            out_specs=[whole_block(*o.shape) for o in outs],
            scratch_shapes=[
                pltpu.VMEM((wd, tq), f32),
                pltpu.VMEM((8, tq), f32),
                pltpu.VMEM((8, tq), f32),
            ],
        ),
        out_shape=outs,
        compiler_params=params(),
        name="attend_fwd",
    )(sc, q, feats, kv, feats)


def attend_bwd(q, feats, nf, pieces, att, lse, kv, sc, n):
    tq, wd = q.shape
    bk, width = kv.shape[1], feats.shape[1]
    return pl.pallas_call(
        functools.partial(bwd_grid, wd // HEAD_DIM, nf, n),
        grid_spec=pltpu.PrefetchScalarGridSpec(
            num_scalar_prefetch=1,
            grid=(n,),
            in_specs=[whole_block(tq, wd), pl.BlockSpec((tq, width), lambda i, s: (s[0], 0))]
            + [whole_block(tq // 4, wd)] * 4
            + [
                whole_block(tq, wd),
                whole_block(8, tq),
                pl.BlockSpec((1, bk, 2 * wd), lambda i, s: (i, 0, 0)),
                pl.BlockSpec((bk, width), lambda i, s: (s[SC + i], 0)),
            ],
            out_specs=[whole_block(tq, wd), pl.BlockSpec((1, bk, 2 * wd), lambda i, s: (i, 0, 0))],
            scratch_shapes=[
                pltpu.VMEM((tq, wd), bf16),
                pltpu.VMEM((8, tq), f32),
                pltpu.VMEM((wd, tq), f32),
            ],
        ),
        out_shape=[struct((tq, wd), bf16), struct(kv.shape, bf16)],
        compiler_params=params(),
        name="attend_bwd",
    )(sc, q, feats, *pieces, att, lse, kv, feats)


def fwd_part(nh, nf, tiles, bk, first, last, sc, *refs):
    q, fq = refs[:2]
    n = len(tiles)
    kvs, fks = refs[2 : 2 + n], refs[2 + n : 2 + 2 * n]
    rest = refs[2 + 2 * n :]
    if not first:
        rest = rest[3:]
    if last:
        out, lse, *msgs = rest[:6]
        acc, m, l = rest[6:9]
    else:
        acc, m, l = rest[:3]
    if first:
        fwd_start(acc, m, l)
    for (place, rows, offset), kv, fk in zip(tiles, kvs, fks):

        @pl.when(tile_needed(sc[SC + place], sc, bk))
        def _():
            fwd_tile(
                nh, nf, q, fq, kv, fk, sc[SC + place] * bk + offset, sc[0] * q.shape[0], acc, m, l
            )

    if last:
        fwd_end(nh, [sc[2 + r] for r in range(4)], acc, m, l, out, lse, msgs)


def attend_fwd_part(q, feats, nf, kvs, tiles, state, sc, last):
    tq, wd = q.shape
    width = feats.shape[1]
    n = len(tiles)
    sums = [struct((wd, tq), f32), struct((8, tq), f32), struct((8, tq), f32)]
    ins = [whole_block(tq, wd), pl.BlockSpec((tq, width), lambda i, s: (s[0], 0))]
    ins += [whole_block(*kv.shape) for kv in kvs]
    for place, rows, offset in tiles:
        at = lambda i, s, p=place, k=tq // rows, o=offset // rows: (s[SC + p] * k + o, 0)
        ins.append(pl.BlockSpec((rows, width), at))
    args = [sc, q, feats, *kvs, *([feats] * n)]
    outs = (fwd_outs(tq, wd) if last else []) + sums
    alias = {}
    if state is not None:
        ins += [whole_block(*o.shape) for o in sums]
        alias = {len(args) + k: len(outs) - 3 + k for k in range(3)}
        args += state

    def kernel(sc_ref, *refs):
        if state is not None:
            olds = refs[2 + 2 * n : 5 + 2 * n]
            news = refs[len(refs) - 3 :]
            for old, new in zip(olds, news):
                new[...] = old[...]
        fwd_part(wd // HEAD_DIM, nf, tiles, tq, state is None, last, sc_ref, *refs)

    got = pl.pallas_call(
        kernel,
        grid_spec=pltpu.PrefetchScalarGridSpec(
            num_scalar_prefetch=1,
            grid=(1,),
            in_specs=ins,
            out_specs=[whole_block(*o.shape) for o in outs],
        ),
        out_shape=outs,
        input_output_aliases=alias,
        compiler_params=params(),
        cost_estimate=pl.CostEstimate(flops=n << 31, bytes_accessed=n << 20, transcendentals=0),
        name="fwd_part",
    )(*args)
    return got[:6] if last else got


def attend_bwd_part(q, feats, nf, kvs, tiles, lse, sc, start, state, last):
    tq, wd = q.shape
    nh = wd // HEAD_DIM
    width = feats.shape[1]
    n = len(tiles)
    held = [struct((tq, wd), bf16), struct((8, tq), f32), struct((wd, tq), f32)]
    ins = [whole_block(tq, wd), pl.BlockSpec((tq, width), lambda i, s: (s[0], 0)), whole_block(8, tq)]
    ins += [whole_block(*kv.shape) for kv in kvs]
    for place, rows, offset in tiles:
        at = lambda i, s, p=place, k=tq // rows, o=offset // rows: (s[SC + p] * k + o, 0)
        ins.append(pl.BlockSpec((rows, width), at))
    args = [sc, q, feats, lse, *kvs, *([feats] * n)]
    outs = [struct(kv.shape, bf16) for kv in kvs]
    more = start if start is not None else state
    ins += [whole_block(*v.shape) for v in more]
    args += more
    if start is not None:
        outs = outs + held
    elif not last:
        outs = outs + held[2:]
    if last:
        outs = outs + [struct((tq, wd), bf16)]
    scratch = [pltpu.VMEM((wd, tq), f32)] if last else []

    def kernel(sc_ref, *refs):
        q_ref, fq, lse_ref = refs[:3]
        kv_refs, fks = refs[3 : 3 + n], refs[3 + n : 3 + 2 * n]
        given = refs[3 + 2 * n : 3 + 2 * n + len(more)]
        rest = refs[3 + 2 * n + len(more) :]
        dkvs, rest = rest[:n], rest[n:]
        if start is not None:
            do, dterm, dq_t = rest[:3]
            bwd_start(nh, [sc_ref[2 + r] for r in range(4)], given[:4], given[4], do, dterm, dq_t)
        else:
            do, dterm, old = given
            dq_t = rest[-1] if last else rest[0]
            dq_t[...] = old[...]
        for (place, rows, offset), kv, fk, dkv in zip(tiles, kv_refs, fks, dkvs):
            need = tile_needed(sc_ref[SC + place], sc_ref, tq)

            @pl.when(jnp.logical_not(need))
            def _():
                dkv[...] = jnp.zeros_like(dkv)

            @pl.when(need)
            def _():
                got = bwd_tile(
                    nh, nf, q_ref, fq, do, lse_ref, dterm, kv, fk,
                    sc_ref[SC + place] * tq + offset, sc_ref[0] * tq, dq_t,
                )
                for h in range(nh):
                    dkv[:, 128 * h : 128 * h + 128] = got[h]

        if last:
            rest[0][...] = (dq_t[...].T * HEAD_DIM**-0.5).astype(bf16)

    return pl.pallas_call(
        kernel,
        grid_spec=pltpu.PrefetchScalarGridSpec(
            num_scalar_prefetch=1,
            grid=(1,),
            in_specs=ins,
            out_specs=[whole_block(*o.shape) for o in outs],
            scratch_shapes=scratch,
        ),
        out_shape=outs,
        compiler_params=params(),
        cost_estimate=pl.CostEstimate(flops=n << 31, bytes_accessed=n << 20, transcendentals=0),
        name="bwd_part",
    )(*args)


def ring_attend(q, feats, nf, kv, sc):
    rows = kv.shape[0]
    half = rows // 2
    a = b = kv
    tiles, state = [kv], None
    whole = lambda p: (p, rows, 0)
    part = functools.partial(attend_fwd_part, q, feats, nf)
    for step in range(3):
        a2, b2 = lax.ppermute(a, "seq", FWD), lax.ppermute(b, "seq", BWD)
        if step == 0:
            state = part([kv], [whole(0)], None, sc, False)
        else:
            state = part([a, b], [whole(2 * step - 1), whole(2 * step)], state, sc, False)
        a, b = a2, b2
        tiles += [a, b]
    c, d = lax.ppermute(a[:half], "seq", FWD), lax.ppermute(b[half:], "seq", BWD)
    state = part([a, b], [whole(5), whole(6)], state, sc, False)
    tiles += [c, d]
    return part([c, d], [(7, half, 0), (7, half, half)], state, sc, True), tiles


def ring_attend_back(q, feats, nf, tiles, pieces, att, lse, sc):
    rows = tiles[0].shape[0]
    half = rows // 2
    whole = lambda p: (p, rows, 0)
    part = functools.partial(attend_bwd_part, q, feats, nf)
    c, d, do, dterm, dq_t = part(
        tiles[7:9], [(7, half, 0), (7, half, half)], lse, sc, [*pieces, att], None, False
    )
    a, b = lax.ppermute(c, "seq", FWD), lax.ppermute(d, "seq", BWD)
    for place in (5, 3, 1):
        t, u, dq_t = part(
            tiles[place : place + 2], [whole(place), whole(place + 1)], lse, sc, None, [do, dterm, dq_t], False
        )
        if place == 5:
            up = jnp.concatenate([add_low(u[:half], a), u[half:]], axis=0)
            down = jnp.concatenate([t[:half], add_low(t[half:], b)], axis=0)
        else:
            up, down = add_low(u, a), add_low(t, b)
        a, b = lax.ppermute(up, "seq", FWD), lax.ppermute(down, "seq", BWD)
    t, dq = part([tiles[0]], [whole(0)], lse, sc, None, [do, dterm, dq_t], True)
    return dq, (t.astype(f32) + a.astype(f32) + b.astype(f32)).astype(bf16)


VEC_ROWS = 16


def out_pack(w_out, b_up, sub_gain, sub_bias):
    width = w_out.shape[1]
    share = sub_gain.shape[0]
    room = width // 3
    pad = lambda v: jnp.concatenate([v, jnp.zeros((room - share,), f32)])
    vec = jnp.stack([b_up, jnp.concatenate([pad(sub_gain), pad(sub_bias), jnp.zeros((room,), f32)])])
    high = vec.astype(bf16)
    rest = vec - lax.optimization_barrier(high).astype(f32)
    middle = rest.astype(bf16)
    low = (rest - lax.optimization_barrier(middle).astype(f32)).astype(bf16)
    top = jnp.concatenate([high, middle, low, jnp.zeros((VEC_ROWS - 6, width), bf16)], axis=0)
    return jnp.concatenate([top, w_out], axis=0)


def unpack_vec(w, row):
    v = w[0:VEC_ROWS, :].astype(f32)
    return v[row : row + 1] + v[row + 2 : row + 3] + v[row + 4 : row + 5]


def sub_parts(pieces, width):
    total = sum(jnp.sum(p, axis=1, keepdims=True) for p in pieces)
    square = sum(jnp.sum(p * p, axis=1, keepdims=True) for p in pieces)
    mean = total / width
    inv = lax.rsqrt(square / width - mean * mean + eps)
    return [(p - mean) * inv for p in pieces], inv


def norm_parts(x):
    center = x - jnp.mean(x, axis=1, keepdims=True)
    rs = lax.rsqrt(jnp.mean(center * center, axis=1, keepdims=True) + eps)
    return center * rs, rs


def norm_back(g, hat, rs):
    return rs * (
        g - jnp.mean(g, axis=1, keepdims=True) - hat * jnp.mean(g * hat, axis=1, keepdims=True)
    )


def mid1_kernel(sc, p0, p1, p2, p3, w0, w1, w2, w3, x, b_out, gain2, bias2, nm, middle, sub):
    share = p0.shape[1]
    room = w0.shape[1] // 3
    cen, _ = sub_parts([p[...].astype(f32) for p in (p0, p1, p2, p3)], w0.shape[1])
    acc = x[...].astype(f32) + b_out[...]
    for r, w in enumerate((w0, w1, w2, w3)):
        vec = unpack_vec(w, 1)
        s = (cen[r] * vec[:, :share] + vec[:, room : room + share]).astype(bf16)
        sub[r] = s
        acc = acc + dot(s, w[VEC_ROWS : VEC_ROWS + share, :])
    middle[...] = acc
    hat, _ = norm_parts(acc)
    nm[...] = (hat * gain2[...] + bias2[...]).astype(bf16)


def gelu_parts(z):
    half = 0.5 * (1.0 + lax.erf(z * np.float32(np.sqrt(0.5))))
    slope = half + z * (np.float32(1.0 / np.sqrt(2.0 * np.pi)) * jnp.exp(-0.5 * z * z))
    return z * half, slope


def mid2_kernel(
    sc, p0, p1, p2, p3, w0, w1, w2, w3, nm, middle, g, b_down, gain2, *refs
):
    ups, downs, refs = refs[:4], refs[4:8], refs[8:]
    y, d_mid, dbr, d0, d1, d2, d3, vec768, vec192, wbuf, sems = refs
    share = p0.shape[1]
    width = w0.shape[1]
    copies = []
    for r in range(4):
        for k, w in enumerate((ups[r], downs[r])):
            copy = pltpu.make_async_copy(w, wbuf.at[2 * r + k], sems.at[2 * r + k])
            copy.start()
            copies.append(copy)
    nmv = nm[...]
    gb = g[...]
    out = middle[...] + b_down[...]
    dn = jnp.zeros(out.shape, f32)
    for r, w in enumerate((w0, w1, w2, w3)):
        copies[2 * r].wait()
        act, slope = gelu_parts(dot(nmv, wbuf[2 * r]) + unpack_vec(w, 0))
        copies[2 * r + 1].wait()
        out = out + dot(act.astype(bf16), wbuf[2 * r + 1])
        d_inner = (dot(gb, wbuf[2 * r + 1], NT) * slope).astype(bf16)
        dn = dn + dot(d_inner, wbuf[2 * r], NT)
    y[...] = out.astype(bf16)
    hat, rs = norm_parts(middle[...])
    vec768[0:1, :] = jnp.sum(dn * hat, axis=0, keepdims=True)
    vec768[1:2, :] = jnp.sum(dn, axis=0, keepdims=True)
    dm = gb.astype(f32) + norm_back(dn * gain2[...], hat, rs)
    d_mid[...] = dm
    branch = dm.astype(bf16)
    dbr[...] = branch
    cen, inv = sub_parts([p[...].astype(f32) for p in (p0, p1, p2, p3)], width)
    hats = []
    for r, w in enumerate((w0, w1, w2, w3)):
        ds = dot(branch, w[VEC_ROWS : VEC_ROWS + share, :], NT)
        vec192[r : r + 1, :] = jnp.sum(ds * cen[r], axis=0, keepdims=True)
        vec192[r + 4 : r + 5, :] = jnp.sum(ds, axis=0, keepdims=True)
        hats.append(ds * unpack_vec(w, 1)[:, :share])
    s1 = sum(jnp.sum(t, axis=1, keepdims=True) for t in hats) / width
    s2 = sum(jnp.sum(t * c, axis=1, keepdims=True) for t, c in zip(hats, cen)) / width
    for o, t, c in zip((d0, d1, d2, d3), hats, cen):
        o[...] = (inv * (t - s1 - c * s2)).astype(bf16)


def one_step(kernel, ins, in_specs, outs, name, flops, scratch=()):
    return pl.pallas_call(
        kernel,
        grid_spec=pltpu.PrefetchScalarGridSpec(
            num_scalar_prefetch=1,
            grid=(1,),
            in_specs=in_specs,
            out_specs=[whole_block(*o.shape) for o in outs],
            scratch_shapes=scratch,
        ),
        out_shape=outs,
        compiler_params=params(),
        cost_estimate=pl.CostEstimate(flops=flops, bytes_accessed=12 << 20, transcendentals=0),
        name=name,
    )(*ins)


def mid1(head_no, pieces, packs, x, b_out, gain2, bias2):
    quarter, share = pieces[0].shape
    rows, width = packs[0].shape
    at_quarter = pl.BlockSpec((quarter, width), lambda i, s: (s[0], 0))
    return one_step(
        mid1_kernel,
        (head_no, *pieces, *packs, x, b_out, gain2, bias2),
        [whole_block(quarter, share)] * 4
        + [whole_block(rows, width)] * 4
        + [at_quarter]
        + [whole_block(1, width)] * 3,
        [struct((quarter, width), bf16), struct((quarter, width), f32), struct((4, quarter, share), bf16)],
        "mid1",
        2 * quarter * width * width,
    )


def mid2(head_no, pieces, packs, ups, downs, nm, middle, g, b_down, gain2):
    quarter, share = pieces[0].shape
    rows, width = packs[0].shape
    at_quarter = pl.BlockSpec((quarter, width), lambda i, s: (s[0], 0))
    return one_step(
        mid2_kernel,
        (head_no, *pieces, *packs, nm, middle, g, b_down, gain2, *ups, *downs),
        [whole_block(quarter, share)] * 4
        + [whole_block(rows, width)] * 4
        + [whole_block(quarter, width)] * 2
        + [at_quarter]
        + [whole_block(1, width)] * 2
        + [pl.BlockSpec(memory_space=pl.ANY)] * 8,
        [
            struct((quarter, width), bf16),
            struct((quarter, width), f32),
            struct((quarter, width), bf16),
        ]
        + [struct((quarter, share), bf16)] * 4
        + [struct((8, width), f32), struct((8, share), f32)],
        "mid2",
        34 * quarter * width * width,
        [pltpu.VMEM((8, *ups[0].shape), bf16), pltpu.SemaphoreType.DMA((8,))],
    )


def shards(
    layer_input, ln1_gain, ln1_bias, w_query, b_query, w_key, w_value, b_value, sub_gain, sub_bias,
    w_out, b_out, ln2_gain, ln2_bias, w_up, b_up, w_down, b_down, cotangent, row_lengths,
):
    rows_local, slice_width = layer_input.shape
    head_share = w_query.shape[1]
    local_heads = head_share // HEAD_DIM
    head_pos = lax.axis_index("head")
    seq_pos = lax.axis_index("seq")
    n_seq = lax.axis_size("seq")
    width = head_share * lax.axis_size("head")
    quarter = rows_local // 4
    head_ids = head_pos * local_heads + jnp.arange(local_heads, dtype=jnp.int32)
    relative = jnp.stack([head_pos, head_pos ^ 1, head_pos ^ 2, head_pos ^ 3]).astype(jnp.int32)
    row2 = lambda v: v.reshape(1, -1)

    both = lax.all_gather(jnp.stack([layer_input, cotangent]), "head", axis=2, tiled=True)
    pack = out_pack(w_out, b_up, sub_gain, sub_bias)
    both, pack, up_in, down_in = lax.optimization_barrier((both, pack, w_up, w_down))
    input_whole, g_whole = both[0], both[1]
    packs, ups, downs = head_whole(pack), head_whole(up_in), head_whole(down_in)
    hat1, rs1 = norm_parts(input_whole.astype(f32))
    normed = (hat1 * ln1_gain + ln1_bias).astype(bf16)
    pair = lambda a, b: jnp.stack(
        [a.reshape(-1, local_heads, HEAD_DIM), b.reshape(-1, local_heads, HEAD_DIM)], axis=2
    ).reshape(-1, 2 * head_share)
    w_kv = pair(w_key, w_value)
    b_kv = pair(jnp.zeros_like(b_value), b_value)
    kv = (dot(normed, w_kv) + b_kv).astype(bf16)
    queries = (dot(normed, w_query) + b_query).astype(bf16)

    feats, nf = features(rows_local * n_seq, row_lengths, head_ids, local_heads)
    first = seq_pos * rows_local
    tri = np.tril(np.ones((row_lengths.shape[0],) * 2, np.int32))
    run_ends = jnp.sum(tri * row_lengths[None, :], axis=1)
    row_begin = jnp.sum(jnp.where(first >= run_ends, row_lengths, 0))
    order = ring_order(seq_pos) if n_seq == 8 else jnp.arange(n_seq, dtype=jnp.int32)
    sc = jnp.concatenate([jnp.stack([seq_pos, row_begin]).astype(jnp.int32), relative, order])
    if n_seq == 8:
        (att, lse, *msgs), kv_tiles = ring_attend(queries, feats, nf, kv, sc)
    else:
        kv_tiles = lax.all_gather(kv, "seq", axis=0)
        att, lse, *msgs = attend_fwd(queries, feats, nf, kv_tiles, sc, n_seq)

    pieces = head_pieces(*msgs)
    nm, middle, sub = mid1(
        relative, pieces, packs, input_whole, row2(b_out), row2(ln2_gain), row2(ln2_bias)
    )
    y, d_mid, dbr, *d_msgs, vec768, vec192 = mid2(
        relative, pieces, packs, ups, downs, nm, middle, g_whole, row2(b_down), row2(ln2_gain)
    )
    d_pieces = head_pieces(*d_msgs)

    nm_all = jnp.concatenate(head_whole(nm), axis=0)
    g_all = jnp.concatenate(
        [lax.dynamic_slice_in_dim(g_whole, relative[r] * quarter, quarter, 0) for r in range(4)], axis=0
    )
    act, slope = gelu_parts(dot(nm_all, w_up) + b_up)
    act = act.astype(bf16)
    d_inner = (dot(g_all, w_down, NT) * slope).astype(bf16)
    gw_down = dot(act, g_all, TN).astype(bf16)
    gw_up = dot(nm_all, d_inner, TN).astype(bf16)
    d_pieces, gw_up, gw_down = lax.optimization_barrier((d_pieces, gw_up, gw_down))
    gw_up, gw_down = lax.psum((gw_up, gw_down), "seq")
    gb_up = jnp.sum(d_inner.astype(f32), axis=0)
    gb_down = jnp.sum(g_whole.astype(f32), axis=0)

    back = head_whole(jnp.concatenate([dbr] + [sub[r] for r in range(4)], axis=1))
    dbr_all = jnp.concatenate([b[:, :width] for b in back], axis=0)
    sub_all = jnp.concatenate(
        [b[:, width + r * head_share : width + (r + 1) * head_share] for r, b in enumerate(back)], axis=0
    )
    gw_out = dot(sub_all, dbr_all, TN)
    gb_out = jnp.sum(dbr_all.astype(f32), axis=0)

    if n_seq == 8:
        dq, dkv = ring_attend_back(queries, feats, nf, kv_tiles, d_pieces, att, lse, sc)
    else:
        dq, dkv_tiles = attend_bwd(queries, feats, nf, d_pieces, att, lse, kv_tiles, sc, n_seq)
        dkv = lax.psum_scatter(dkv_tiles, "seq", scatter_dimension=0, tiled=False)
    dq, y = lax.optimization_barrier((dq, y))
    layer_output = lax.all_to_all(y, "head", 1, 0, tiled=True)
    gw_query = dot(normed, dq, TN)
    gw_kv = dot(normed, dkv, TN)
    gb_query = jnp.sum(dq.astype(f32), axis=0)
    gb_kv = jnp.sum(dkv.astype(f32), axis=0)
    dn = dot(dq, w_query, NT) + dot(dkv, w_kv, NT)

    late = jnp.concatenate(
        [
            jnp.concatenate([gw_query.astype(bf16), gw_kv.astype(bf16)], axis=1),
            gw_out.astype(bf16).reshape(-1, 3 * head_share),
        ],
        axis=0,
    )
    split = lambda v: jnp.sum(
        jnp.where(relative[:, None, None] == jnp.arange(4)[None, :, None], v[:, None, :], 0.0), axis=0
    ).reshape(-1)
    small = jnp.stack(
        [
            jnp.sum(dn * hat1, axis=0),
            jnp.sum(dn, axis=0),
            vec768[0],
            vec768[1],
            split(vec192[:4]),
            split(vec192[4:]),
        ]
    )
    small = small + lax.ppermute(small, "head", CORE)
    small = small + lax.ppermute(small, "head", CROSS)
    fill = lambda v: jnp.concatenate([v, jnp.zeros((width - v.shape[0],), f32)])
    small = jnp.concatenate(
        [small, jnp.stack([gb_up, gb_down, gb_out, fill(jnp.concatenate([gb_query, gb_kv]))])], axis=0
    )
    if n_seq == 8:
        for step in (1, 2, 4):
            small = small + lax.ppermute(small, "seq", exchange(step))
        late = halve_double(late)
    else:
        small = lax.psum(small, "seq")
        late = lax.psum(late, "seq")

    dn = dn.astype(bf16).reshape(2, 2, quarter, width)
    core, chip = head_pos % 2, head_pos // 2
    mine = lax.dynamic_index_in_dim(dn, core, 1, False)
    mate = lax.dynamic_index_in_dim(dn, 1 - core, 1, False)
    mine = add_low(mine, lax.ppermute(mate, "head", CORE))
    far = lax.ppermute(lax.dynamic_index_in_dim(mine, 1 - chip, 0, False), "head", CROSS)
    dn = lax.dynamic_index_in_dim(mine, chip, 0, False).astype(f32) + far.astype(f32)
    cut = lambda v: lax.dynamic_slice_in_dim(v, head_pos * quarter, quarter, 0)
    d_in = d_mid + norm_back(dn * ln1_gain, cut(hat1), cut(rs1))
    grad_input = lax.all_to_all(d_in.astype(bf16), "head", 1, 0, tiled=True).astype(f32)

    gw_query = late[:width, :head_share].astype(f32)
    gw_pair = late[:width, head_share:].astype(f32).reshape(width, local_heads, 2, HEAD_DIM)
    gw_key = gw_pair[:, :, 0].reshape(width, head_share)
    gw_value = gw_pair[:, :, 1].reshape(width, head_share)
    gw_out = late[width:].astype(f32).reshape(head_share, width)
    own = lambda v: lax.dynamic_slice_in_dim(v, head_pos * head_share, head_share, 0)
    gb_value = small[9, head_share : 3 * head_share].reshape(local_heads, 2, HEAD_DIM)[:, 1].reshape(-1)
    return (
        layer_output,
        grad_input,
        small[0],
        small[1],
        gw_query,
        small[9, :head_share],
        gw_key,
        gw_value,
        gb_value,
        own(small[4]),
        own(small[5]),
        gw_out,
        small[8],
        small[2],
        small[3],
        gw_up.astype(f32),
        small[6],
        gw_down.astype(f32),
        small[7],
    )


def solution(mesh):
    cols, rows, both, shared, vec = P(None, "head"), P("head", None), P("seq", "head"), P(), P("head")
    in_specs = (
        both, shared, shared, cols, vec, cols, cols, vec, vec, vec,
        rows, shared, shared, shared, cols, vec, rows, shared, both, shared,
    )
    out_specs = (
        both, both, shared, shared, cols, vec, cols, cols, vec, vec,
        vec, rows, shared, shared, shared, cols, vec, rows, shared,
    )
    return jax.shard_map(shards, mesh=mesh, in_specs=in_specs, out_specs=out_specs, check_vma=False)
```

```python
import functools

import jax
import jax.numpy as jnp
import numpy as np
from jax import lax
from jax.experimental import pallas as pl
from jax.experimental.pallas import tpu as pltpu
from jax.sharding import PartitionSpec as P

HEAD_DIM = 64
SEG = 2048
eps = 1e-05
segment_scales = (1, 2, 4, 8, 16)
dilation_steps = (1, 2, 4, 6, 12)
bf16 = jnp.bfloat16
f32 = jnp.float32
NT = (((1,), (1,)), ((), ()))
NN = (((1,), (0,)), ((), ()))
TN = (((0,), (0,)), ((), ()))
VMEM_LIMIT = 56 << 20

RING = (0, 2, 4, 6, 7, 5, 3, 1)
FWD = [(RING[i], RING[(i + 1) % 8]) for i in range(8)]
BWD = [(b, a) for a, b in FWD]
CORE = [(0, 1), (1, 0), (2, 3), (3, 2)]
CROSS = [(0, 2), (2, 0), (1, 3), (3, 1)]
BOTH = [(0, 3), (3, 0), (1, 2), (2, 1)]


def dot(a, b, dims=NN):
    return lax.dot_general(a, b, dims, preferred_element_type=f32)


def add_low(u, v):
    return (u.astype(f32) + v.astype(f32)).astype(u.dtype)


def ring_order(seq_pos):
    ring = jnp.asarray(RING, jnp.int32)
    pos = jnp.sum(jnp.where(ring == seq_pos, jnp.arange(8, dtype=jnp.int32), 0))
    return ring[(pos + jnp.asarray([0, -1, 1, -2, 2, -3, 3, 4], jnp.int32)) % 8]


def exchange(step):
    return [(i, i ^ step) for i in range(8)]


def halve_double(x):
    idx = lax.axis_index("seq")
    for step in (1, 2, 4):
        half = x.shape[0] // 2
        bit = (idx // step) % 2
        keep = lax.dynamic_slice_in_dim(x, bit * half, half, 0)
        send = lax.dynamic_slice_in_dim(x, (1 - bit) * half, half, 0)
        x = add_low(keep, lax.ppermute(send, "seq", exchange(step)))
    for step in (4, 2, 1):
        bit = (idx // step) % 2
        r = lax.ppermute(x, "seq", exchange(step))
        x = jnp.where(bit == 0, jnp.concatenate([x, r], axis=0), jnp.concatenate([r, x], axis=0))
    return x


def head_pieces(own, core, cross, both):
    return (
        own,
        lax.ppermute(core, "head", CORE),
        lax.ppermute(cross, "head", CROSS),
        lax.ppermute(both, "head", BOTH),
    )


def head_whole(x):
    p = lax.ppermute(x, "head", CROSS)
    return x, lax.ppermute(x, "head", CORE), p, lax.ppermute(p, "head", CORE)


def features(total, lengths, head_ids, nh):
    nrow = lengths.shape[0]
    pos = jnp.arange(total, dtype=jnp.int32)
    ends = jnp.sum(np.tril(np.ones((nrow, nrow), np.int32)) * lengths[None, :], axis=1)
    past = pos[:, None] >= ends[None, :]
    place = pos - jnp.sum(jnp.where(past, lengths[None, :], 0), axis=1)
    sizes = [nrow + total // (SEG * s) for s in segment_scales]
    nf = sum(sizes)
    width = -(-nh * nf // 128) * 128
    lane = np.arange(width)
    lane_head, lane_feature = lane // nf, lane % nf
    head_of = jnp.sum(
        jnp.where(lane_head[None, :] == np.arange(nh)[:, None], head_ids[:, None], 0), axis=0
    )
    out = jnp.zeros((total, width), jnp.bool_)
    first = 0
    for scale, step, size in zip(segment_scales, dilation_steps, sizes):
        seg_width = SEG * scale
        pieces = (lengths + (seg_width - 1)) // seg_width
        seg = jnp.sum(jnp.where(past, pieces[None, :], 0), axis=1) + place // seg_width + first
        residue = place % seg_width % step
        here = (lane_feature >= first) & (lane_feature < first + size) & (lane_head < nh)
        lane_seg = jnp.where(here, lane_feature, -1)
        lane_res = jnp.where(here, head_of % step, -1)
        out = out | ((seg[:, None] == lane_seg[None, :]) & (residue[:, None] == lane_res[None, :]))
        first += size
    return out.astype(bf16), nf


def head_pad(x, h, upper):
    part = x[:, HEAD_DIM * h : HEAD_DIM * (h + 1)]
    zero = jnp.zeros_like(part)
    return jnp.concatenate([zero, part] if upper else [part, zero], axis=1)


def count_tile(fk, fq, h, nf, first_key, first_row):
    lane = lax.broadcasted_iota(jnp.int32, fq.shape, 1)
    fqh = jnp.where((lane >= h * nf) & (lane < (h + 1) * nf), fq.astype(f32), 0.0).astype(bf16)
    count = dot(fk, fqh, NT)
    keys = first_key + lax.broadcasted_iota(jnp.int32, (count.shape[0], 1), 0)
    rows = first_row + lax.broadcasted_iota(jnp.int32, (1, count.shape[1]), 1)
    return jnp.where(keys <= rows, count, 0.0)


def fwd_tile(nh, nf, q, fq, kv, fk, first_key, first_row, acc, m, l):
    kv_t = kv[...].astype(f32).T.astype(bf16)
    qs = (q[...].astype(f32) * HEAD_DIM**-0.5).astype(bf16)
    for h in range(nh):
        s = dot(kv[:, 128 * h : 128 * h + 128], head_pad(qs, h, False), NT)
        count = count_tile(fk[...], fq[...], h, nf, first_key, first_row)
        s = jnp.where(count > 0, s, -1e30)
        old = m[h : h + 1, :]
        new = jnp.maximum(old, jnp.max(s, axis=0, keepdims=True))
        p = count * jnp.exp(s - new)
        factor = jnp.exp(old - new)
        l[h : h + 1, :] = l[h : h + 1, :] * factor + jnp.sum(p, axis=0, keepdims=True)
        o = dot(kv_t[128 * h : 128 * h + 128], p.astype(bf16))
        acc[64 * h : 64 * h + 64, :] = acc[64 * h : 64 * h + 64, :] * factor + o[64:, :]
        m[h : h + 1, :] = new


def bwd_tile(nh, nf, q, fq, do, lse, dterm, kv, fk, first_key, first_row, dq_t):
    kv_t = kv[...].astype(f32).T.astype(bf16)
    qs = (q[...].astype(f32) * HEAD_DIM**-0.5).astype(bf16)
    out = []
    for h in range(nh):
        kvh = kv[:, 128 * h : 128 * h + 128]
        qh = head_pad(qs, h, False)
        doh = head_pad(do[...], h, True)
        count = count_tile(fk[...], fq[...], h, nf, first_key, first_row)
        p = count * jnp.exp(jnp.minimum(dot(kvh, qh, NT) - lse[h : h + 1, :], 1.0))
        ds = (p * (dot(kvh, doh, NT) - dterm[h : h + 1, :])).astype(bf16)
        out.append((dot(ds, qh) + dot(p.astype(bf16), doh)).astype(bf16))
        o = dot(kv_t[128 * h : 128 * h + 128], ds)
        dq_t[64 * h : 64 * h + 64, :] += o[:64, :]
    return out


def fwd_start(acc, m, l):
    acc[...] = jnp.zeros_like(acc)
    m[...] = jnp.full_like(m, -1e30)
    l[...] = jnp.zeros_like(l)


def fwd_end(nh, quarters, acc, m, l, out, lse, msgs):
    for h in range(nh):
        out[:, 64 * h : 64 * h + 64] = (acc[64 * h : 64 * h + 64, :] / l[h : h + 1, :]).T
    lse[...] = m[...] + jnp.log(jnp.maximum(l[...], 1e-30))
    rows = msgs[0].shape[0]
    for at, msg in zip(quarters, msgs):
        msg[...] = out[pl.ds(pl.multiple_of(at * rows, rows), rows), :].astype(bf16)


def bwd_start(nh, quarters, pieces, att, do, dterm, dq_t):
    dq_t[...] = jnp.zeros_like(dq_t)
    rows = pieces[0].shape[0]
    for at, piece in zip(quarters, pieces):
        do[pl.ds(pl.multiple_of(at * rows, rows), rows), :] = piece[...]
    prod = do[...].astype(f32) * att[...]
    r = lax.broadcasted_iota(jnp.int32, (8, prod.shape[1]), 0)
    c = lax.broadcasted_iota(jnp.int32, (8, prod.shape[1]), 1)
    pick = jnp.where(c // HEAD_DIM == r, 1.0, 0.0).astype(f32)
    dterm[...] = lax.dot_general(
        pick, prod, NT, precision=lax.Precision.HIGHEST, preferred_element_type=f32
    )


def tile_needed(tile, sc, bk):
    return (tile <= sc[0]) & ((tile + 1) * bk > sc[1])


SC = 6


def fwd_grid(nh, nf, n, sc, q, fq, kv, fk, out, lse, m0, m1, m2, m3, acc, m, l):
    i = pl.program_id(0)
    bk = kv.shape[1]

    @pl.when(i == 0)
    def _():
        fwd_start(acc, m, l)

    @pl.when(tile_needed(sc[SC + i], sc, bk))
    def _():
        fwd_tile(nh, nf, q, fq, kv.at[0], fk, sc[SC + i] * bk, sc[0] * q.shape[0], acc, m, l)

    @pl.when(i == n - 1)
    def _():
        fwd_end(nh, [sc[2 + r] for r in range(4)], acc, m, l, out, lse, (m0, m1, m2, m3))


def bwd_grid(nh, nf, n, sc, q, fq, d0, d1, d2, d3, att, lse, kv, fk, dq, dkv, do, dterm, dq_t):
    i = pl.program_id(0)
    bk = kv.shape[1]

    @pl.when(i == 0)
    def _():
        bwd_start(nh, [sc[2 + r] for r in range(4)], (d0, d1, d2, d3), att, do, dterm, dq_t)

    need = tile_needed(sc[SC + i], sc, bk)

    @pl.when(jnp.logical_not(need))
    def _():
        dkv[...] = jnp.zeros_like(dkv)

    @pl.when(need)
    def _():
        out = bwd_tile(
            nh, nf, q, fq, do, lse, dterm, kv.at[0], fk, sc[SC + i] * bk, sc[0] * q.shape[0], dq_t
        )
        for h in range(nh):
            dkv[0, :, 128 * h : 128 * h + 128] = out[h]

    @pl.when(i == n - 1)
    def _():
        dq[...] = (dq_t[...].T * HEAD_DIM**-0.5).astype(dq.dtype)


def whole_block(*shape):
    return pl.BlockSpec(shape, lambda i, s: (0,) * len(shape))


def struct(shape, dtype):
    return jax.ShapeDtypeStruct(shape, dtype)


def params():
    return pltpu.CompilerParams(
        dimension_semantics=("arbitrary",), vmem_limit_bytes=VMEM_LIMIT
    )


def fwd_outs(tq, wd):
    return [struct((tq, wd), f32), struct((8, tq), f32)] + [struct((tq // 4, wd), bf16)] * 4


def attend_fwd(q, feats, nf, kv, sc, n):
    tq, wd = q.shape
    bk, width = kv.shape[1], feats.shape[1]
    outs = fwd_outs(tq, wd)
    return pl.pallas_call(
        functools.partial(fwd_grid, wd // HEAD_DIM, nf, n),
        grid_spec=pltpu.PrefetchScalarGridSpec(
            num_scalar_prefetch=1,
            grid=(n,),
            in_specs=[
                whole_block(tq, wd),
                pl.BlockSpec((tq, width), lambda i, s: (s[0], 0)),
                pl.BlockSpec((1, bk, 2 * wd), lambda i, s: (i, 0, 0)),
                pl.BlockSpec((bk, width), lambda i, s: (s[SC + i], 0)),
            ],
            out_specs=[whole_block(*o.shape) for o in outs],
            scratch_shapes=[
                pltpu.VMEM((wd, tq), f32),
                pltpu.VMEM((8, tq), f32),
                pltpu.VMEM((8, tq), f32),
            ],
        ),
        out_shape=outs,
        compiler_params=params(),
        name="attend_fwd",
    )(sc, q, feats, kv, feats)


def attend_bwd(q, feats, nf, pieces, att, lse, kv, sc, n):
    tq, wd = q.shape
    bk, width = kv.shape[1], feats.shape[1]
    return pl.pallas_call(
        functools.partial(bwd_grid, wd // HEAD_DIM, nf, n),
        grid_spec=pltpu.PrefetchScalarGridSpec(
            num_scalar_prefetch=1,
            grid=(n,),
            in_specs=[whole_block(tq, wd), pl.BlockSpec((tq, width), lambda i, s: (s[0], 0))]
            + [whole_block(tq // 4, wd)] * 4
            + [
                whole_block(tq, wd),
                whole_block(8, tq),
                pl.BlockSpec((1, bk, 2 * wd), lambda i, s: (i, 0, 0)),
                pl.BlockSpec((bk, width), lambda i, s: (s[SC + i], 0)),
            ],
            out_specs=[whole_block(tq, wd), pl.BlockSpec((1, bk, 2 * wd), lambda i, s: (i, 0, 0))],
            scratch_shapes=[
                pltpu.VMEM((tq, wd), bf16),
                pltpu.VMEM((8, tq), f32),
                pltpu.VMEM((wd, tq), f32),
            ],
        ),
        out_shape=[struct((tq, wd), bf16), struct(kv.shape, bf16)],
        compiler_params=params(),
        name="attend_bwd",
    )(sc, q, feats, *pieces, att, lse, kv, feats)


def fwd_part(nh, nf, tiles, bk, first, last, sc, *refs):
    q, fq = refs[:2]
    n = len(tiles)
    kvs, fks = refs[2 : 2 + n], refs[2 + n : 2 + 2 * n]
    rest = refs[2 + 2 * n :]
    if not first:
        rest = rest[3:]
    if last:
        out, lse, *msgs = rest[:6]
        acc, m, l = rest[6:9]
    else:
        acc, m, l = rest[:3]
    if first:
        fwd_start(acc, m, l)
    for (place, rows, offset), kv, fk in zip(tiles, kvs, fks):

        @pl.when(tile_needed(sc[SC + place], sc, bk))
        def _():
            fwd_tile(
                nh, nf, q, fq, kv, fk, sc[SC + place] * bk + offset, sc[0] * q.shape[0], acc, m, l
            )

    if last:
        fwd_end(nh, [sc[2 + r] for r in range(4)], acc, m, l, out, lse, msgs)


def attend_fwd_part(q, feats, nf, kvs, tiles, state, sc, last):
    tq, wd = q.shape
    width = feats.shape[1]
    n = len(tiles)
    sums = [struct((wd, tq), f32), struct((8, tq), f32), struct((8, tq), f32)]
    ins = [whole_block(tq, wd), pl.BlockSpec((tq, width), lambda i, s: (s[0], 0))]
    ins += [whole_block(*kv.shape) for kv in kvs]
    for place, rows, offset in tiles:
        at = lambda i, s, p=place, k=tq // rows, o=offset // rows: (s[SC + p] * k + o, 0)
        ins.append(pl.BlockSpec((rows, width), at))
    args = [sc, q, feats, *kvs, *([feats] * n)]
    outs = (fwd_outs(tq, wd) if last else []) + sums
    alias = {}
    if state is not None:
        ins += [whole_block(*o.shape) for o in sums]
        alias = {len(args) + k: len(outs) - 3 + k for k in range(3)}
        args += state

    def kernel(sc_ref, *refs):
        if state is not None:
            olds = refs[2 + 2 * n : 5 + 2 * n]
            news = refs[len(refs) - 3 :]
            for old, new in zip(olds, news):
                new[...] = old[...]
        fwd_part(wd // HEAD_DIM, nf, tiles, tq, state is None, last, sc_ref, *refs)

    got = pl.pallas_call(
        kernel,
        grid_spec=pltpu.PrefetchScalarGridSpec(
            num_scalar_prefetch=1,
            grid=(1,),
            in_specs=ins,
            out_specs=[whole_block(*o.shape) for o in outs],
        ),
        out_shape=outs,
        input_output_aliases=alias,
        compiler_params=params(),
        cost_estimate=pl.CostEstimate(flops=n << 31, bytes_accessed=n << 20, transcendentals=0),
        name="fwd_part",
    )(*args)
    return got[:6] if last else got


def attend_bwd_part(q, feats, nf, kvs, tiles, lse, sc, start, state, last):
    tq, wd = q.shape
    nh = wd // HEAD_DIM
    width = feats.shape[1]
    n = len(tiles)
    held = [struct((tq, wd), bf16), struct((8, tq), f32), struct((wd, tq), f32)]
    ins = [whole_block(tq, wd), pl.BlockSpec((tq, width), lambda i, s: (s[0], 0)), whole_block(8, tq)]
    ins += [whole_block(*kv.shape) for kv in kvs]
    for place, rows, offset in tiles:
        at = lambda i, s, p=place, k=tq // rows, o=offset // rows: (s[SC + p] * k + o, 0)
        ins.append(pl.BlockSpec((rows, width), at))
    args = [sc, q, feats, lse, *kvs, *([feats] * n)]
    outs = [struct(kv.shape, bf16) for kv in kvs]
    more = start if start is not None else state
    ins += [whole_block(*v.shape) for v in more]
    args += more
    if start is not None:
        outs = outs + held
    elif not last:
        outs = outs + held[2:]
    if last:
        outs = outs + [struct((tq, wd), bf16)]
    scratch = [pltpu.VMEM((wd, tq), f32)] if last else []

    def kernel(sc_ref, *refs):
        q_ref, fq, lse_ref = refs[:3]
        kv_refs, fks = refs[3 : 3 + n], refs[3 + n : 3 + 2 * n]
        given = refs[3 + 2 * n : 3 + 2 * n + len(more)]
        rest = refs[3 + 2 * n + len(more) :]
        dkvs, rest = rest[:n], rest[n:]
        if start is not None:
            do, dterm, dq_t = rest[:3]
            bwd_start(nh, [sc_ref[2 + r] for r in range(4)], given[:4], given[4], do, dterm, dq_t)
        else:
            do, dterm, old = given
            dq_t = rest[-1] if last else rest[0]
            dq_t[...] = old[...]
        for (place, rows, offset), kv, fk, dkv in zip(tiles, kv_refs, fks, dkvs):
            need = tile_needed(sc_ref[SC + place], sc_ref, tq)

            @pl.when(jnp.logical_not(need))
            def _():
                dkv[...] = jnp.zeros_like(dkv)

            @pl.when(need)
            def _():
                got = bwd_tile(
                    nh, nf, q_ref, fq, do, lse_ref, dterm, kv, fk,
                    sc_ref[SC + place] * tq + offset, sc_ref[0] * tq, dq_t,
                )
                for h in range(nh):
                    dkv[:, 128 * h : 128 * h + 128] = got[h]

        if last:
            rest[0][...] = (dq_t[...].T * HEAD_DIM**-0.5).astype(bf16)

    return pl.pallas_call(
        kernel,
        grid_spec=pltpu.PrefetchScalarGridSpec(
            num_scalar_prefetch=1,
            grid=(1,),
            in_specs=ins,
            out_specs=[whole_block(*o.shape) for o in outs],
            scratch_shapes=scratch,
        ),
        out_shape=outs,
        compiler_params=params(),
        cost_estimate=pl.CostEstimate(flops=n << 31, bytes_accessed=n << 20, transcendentals=0),
        name="bwd_part",
    )(*args)


def ring_attend(q, feats, nf, kv, sc, *later):
    rows = kv.shape[0]
    half = rows // 2
    a = b = kv
    tiles, state = [kv], None
    whole = lambda p: (p, rows, 0)
    part = functools.partial(attend_fwd_part, q, feats, nf)
    for step in range(3):
        a2, b2 = lax.ppermute(a, "seq", FWD), lax.ppermute(b, "seq", BWD)
        if step == 0:
            state = part([kv], [whole(0)], None, sc, False)
        else:
            state = part([a, b], [whole(2 * step - 1), whole(2 * step)], state, sc, False)
        a, b = a2, b2
        tiles += [a, b]
        if step == 0:
            a, b, *later = lax.optimization_barrier((a, b, *later))
    c, d = lax.ppermute(a[:half], "seq", FWD), lax.ppermute(b[half:], "seq", BWD)
    state = part([a, b], [whole(5), whole(6)], state, sc, False)
    tiles += [c, d]
    return part([c, d], [(7, half, 0), (7, half, half)], state, sc, True), tiles, *later


def ring_attend_back(q, feats, nf, tiles, pieces, att, lse, sc):
    rows = tiles[0].shape[0]
    half = rows // 2
    whole = lambda p: (p, rows, 0)
    part = functools.partial(attend_bwd_part, q, feats, nf)
    c, d, do, dterm, dq_t = part(
        tiles[7:9], [(7, half, 0), (7, half, half)], lse, sc, [*pieces, att], None, False
    )
    a, b = lax.ppermute(c, "seq", FWD), lax.ppermute(d, "seq", BWD)
    for place in (5, 3, 1):
        t, u, dq_t = part(
            tiles[place : place + 2], [whole(place), whole(place + 1)], lse, sc, None, [do, dterm, dq_t], False
        )
        if place == 5:
            up = jnp.concatenate([add_low(u[:half], a), u[half:]], axis=0)
            down = jnp.concatenate([t[:half], add_low(t[half:], b)], axis=0)
        else:
            up, down = add_low(u, a), add_low(t, b)
        up, down, dq_t = lax.optimization_barrier((up, down, dq_t))
        a, b = lax.ppermute(up, "seq", FWD), lax.ppermute(down, "seq", BWD)
    t, dq = part([tiles[0]], [whole(0)], lse, sc, None, [do, dterm, dq_t], True)
    return dq, (t.astype(f32) + a.astype(f32) + b.astype(f32)).astype(bf16)


VEC_ROWS = 16


def out_pack(w_out, sub_gain, sub_bias):
    width = w_out.shape[1]
    share = sub_gain.shape[0]
    room = width // 3
    pad = lambda v: jnp.concatenate([v, jnp.zeros((room - share,), f32)])
    vec = jnp.concatenate([pad(sub_gain), pad(sub_bias), jnp.zeros((room,), f32)]).reshape(1, width)
    high = vec.astype(bf16)
    rest = vec - lax.optimization_barrier(high).astype(f32)
    middle = rest.astype(bf16)
    low = (rest - lax.optimization_barrier(middle).astype(f32)).astype(bf16)
    top = jnp.concatenate([high, middle, low, jnp.zeros((VEC_ROWS - 3, width), bf16)], axis=0)
    return jnp.concatenate([top, w_out], axis=0)


def unpack_vec(w, row):
    v = w[0:VEC_ROWS, :].astype(f32)
    return v[row : row + 1] + v[row + 1 : row + 2] + v[row + 2 : row + 3]


def sub_parts(pieces, width):
    total = sum(jnp.sum(p, axis=1, keepdims=True) for p in pieces)
    square = sum(jnp.sum(p * p, axis=1, keepdims=True) for p in pieces)
    mean = total / width
    inv = lax.rsqrt(square / width - mean * mean + eps)
    return [(p - mean) * inv for p in pieces], inv


def norm_parts(x):
    center = x - jnp.mean(x, axis=1, keepdims=True)
    rs = lax.rsqrt(jnp.mean(center * center, axis=1, keepdims=True) + eps)
    return center * rs, rs


def norm_back(g, hat, rs):
    return rs * (
        g - jnp.mean(g, axis=1, keepdims=True) - hat * jnp.mean(g * hat, axis=1, keepdims=True)
    )


def mid1_kernel(sc, p0, p1, p2, p3, w0, w1, w2, w3, x, b_out, gain2, bias2, nm, middle, sub):
    share = p0.shape[1]
    room = w0.shape[1] // 3
    cen, _ = sub_parts([p[...].astype(f32) for p in (p0, p1, p2, p3)], w0.shape[1])
    acc = x[...].astype(f32) + b_out[...]
    for r, w in enumerate((w0, w1, w2, w3)):
        vec = unpack_vec(w, 0)
        s = (cen[r] * vec[:, :share] + vec[:, room : room + share]).astype(bf16)
        sub[r] = s
        acc = acc + dot(s, w[VEC_ROWS : VEC_ROWS + share, :])
    middle[...] = acc
    hat, _ = norm_parts(acc)
    nm[...] = (hat * gain2[...] + bias2[...]).astype(bf16)


def gelu_parts(z):
    half = 0.5 * (1.0 + lax.erf(z * np.float32(np.sqrt(0.5))))
    slope = half + z * (np.float32(1.0 / np.sqrt(2.0 * np.pi)) * jnp.exp(-0.5 * z * z))
    return z * half, slope


def ffn_kernel(sc, n0, n1, n2, n3, g, w_up, w_down, b_up, nm, act, d_inner, *outs):
    out_own, out_core, out_cross, dn_own, dn_core, dn_cross = outs
    rows = n0.shape[0]
    places = ((out_own, dn_own, None), (out_core, dn_core, 0), (out_cross, dn_cross, None), (out_core, dn_core, 1))
    for r, (piece, (out, dn, slot)) in enumerate(zip((n0, n1, n2, n3), places)):
        at = pl.ds(pl.multiple_of(sc[r] * rows, rows), rows)
        x = piece[...]
        nm[at, :] = x
        a, slope = gelu_parts(dot(x, w_up[...]) + b_up[...])
        a = a.astype(bf16)
        d = (dot(g[at, :], w_down[...], NT) * slope).astype(bf16)
        act[at, :] = a
        d_inner[at, :] = d
        o = dot(a, w_down[...]).astype(bf16)
        b = dot(d, w_up[...], NT).astype(bf16)
        if slot is None:
            out[...] = o
            dn[...] = b
        else:
            out[slot] = o
            dn[slot] = b


def mid2_kernel(sc, p0, p1, p2, p3, w0, w1, w2, w3, middle, g, gain2, t0, t1, t2, *refs):
    d_mid, dbr, d0, d1, d2, d3, vec768, vec192 = refs
    share = p0.shape[1]
    width = w0.shape[1]
    dn = t0[...].astype(f32) + t1[0].astype(f32) + t2[...].astype(f32)
    hat, rs = norm_parts(middle[...])
    vec768[0:1, :] = jnp.sum(dn * hat, axis=0, keepdims=True)
    vec768[1:2, :] = jnp.sum(dn, axis=0, keepdims=True)
    dm = g[...].astype(f32) + norm_back(dn * gain2[...], hat, rs)
    d_mid[...] = dm
    branch = dm.astype(bf16)
    dbr[...] = branch
    cen, inv = sub_parts([p[...].astype(f32) for p in (p0, p1, p2, p3)], width)
    hats = []
    for r, w in enumerate((w0, w1, w2, w3)):
        ds = dot(branch, w[VEC_ROWS : VEC_ROWS + share, :], NT)
        vec192[r : r + 1, :] = jnp.sum(ds * cen[r], axis=0, keepdims=True)
        vec192[r + 4 : r + 5, :] = jnp.sum(ds, axis=0, keepdims=True)
        hats.append(ds * unpack_vec(w, 0)[:, :share])
    s1 = sum(jnp.sum(t, axis=1, keepdims=True) for t in hats) / width
    s2 = sum(jnp.sum(t * c, axis=1, keepdims=True) for t, c in zip(hats, cen)) / width
    for o, t, c in zip((d0, d1, d2, d3), hats, cen):
        o[...] = (inv * (t - s1 - c * s2)).astype(bf16)


def one_step(kernel, ins, in_specs, outs, name, flops, scratch=()):
    return pl.pallas_call(
        kernel,
        grid_spec=pltpu.PrefetchScalarGridSpec(
            num_scalar_prefetch=1,
            grid=(1,),
            in_specs=in_specs,
            out_specs=[whole_block(*o.shape) for o in outs],
            scratch_shapes=scratch,
        ),
        out_shape=outs,
        compiler_params=params(),
        cost_estimate=pl.CostEstimate(flops=flops, bytes_accessed=12 << 20, transcendentals=0),
        name=name,
    )(*ins)


def mid1(head_no, pieces, packs, x, b_out, gain2, bias2):
    quarter, share = pieces[0].shape
    rows, width = packs[0].shape
    at_quarter = pl.BlockSpec((quarter, width), lambda i, s: (s[0], 0))
    return one_step(
        mid1_kernel,
        (head_no, *pieces, *packs, x, b_out, gain2, bias2),
        [whole_block(quarter, share)] * 4
        + [whole_block(rows, width)] * 4
        + [at_quarter]
        + [whole_block(1, width)] * 3,
        [struct((quarter, width), bf16), struct((quarter, width), f32), struct((4, quarter, share), bf16)],
        "mid1",
        2 * quarter * width * width,
    )


def ffn(head_no, pieces, g, w_up, w_down, b_up):
    quarter, width = pieces[0].shape
    hidden = w_up.shape[1]
    full = struct((4 * quarter, hidden), bf16)
    one, two = struct((quarter, width), bf16), struct((2, quarter, width), bf16)
    ins = (head_no, *pieces, g, w_up, w_down, b_up)
    outs = [struct((4 * quarter, width), bf16), full, full, one, two, one, one, two, one]
    flops = 32 * quarter * width * hidden
    return one_step(ffn_kernel, ins, [whole_block(*v.shape) for v in ins[1:]], outs, "ffn", flops)


def mid2(head_no, pieces, packs, middle, g, gain2, terms):
    quarter, share = pieces[0].shape
    rows, width = packs[0].shape
    at_quarter = pl.BlockSpec((quarter, width), lambda i, s: (s[0], 0))
    return one_step(
        mid2_kernel,
        (head_no, *pieces, *packs, middle, g, gain2, *terms),
        [whole_block(quarter, share)] * 4
        + [whole_block(rows, width)] * 4
        + [whole_block(quarter, width), at_quarter, whole_block(1, width)]
        + [whole_block(*t.shape) for t in terms],
        [struct((quarter, width), f32), struct((quarter, width), bf16)]
        + [struct((quarter, share), bf16)] * 4
        + [struct((8, width), f32), struct((8, share), f32)],
        "mid2",
        2 * quarter * width * width,
    )


def head_terms(own, core, cross):
    r = lax.ppermute(core, "head", CORE)
    return own, r, lax.ppermute(add_low(cross, r[1]), "head", CROSS)


def shards(
    layer_input, ln1_gain, ln1_bias, w_query, b_query, w_key, w_value, b_value, sub_gain, sub_bias,
    w_out, b_out, ln2_gain, ln2_bias, w_up, b_up, w_down, b_down, cotangent, row_lengths,
):
    rows_local, slice_width = layer_input.shape
    head_share = w_query.shape[1]
    local_heads = head_share // HEAD_DIM
    head_pos = lax.axis_index("head")
    seq_pos = lax.axis_index("seq")
    n_seq = lax.axis_size("seq")
    width = head_share * lax.axis_size("head")
    quarter = rows_local // 4
    head_ids = head_pos * local_heads + jnp.arange(local_heads, dtype=jnp.int32)
    relative = jnp.stack([head_pos, head_pos ^ 1, head_pos ^ 2, head_pos ^ 3]).astype(jnp.int32)
    row2 = lambda v: v.reshape(1, -1)

    pack = out_pack(w_out, sub_gain, sub_bias)
    input_whole = lax.all_gather(layer_input, "head", axis=1, tiled=True)
    hat1, rs1 = norm_parts(input_whole.astype(f32))
    normed = (hat1 * ln1_gain + ln1_bias).astype(bf16)
    pair = lambda a, b: jnp.stack(
        [a.reshape(-1, local_heads, HEAD_DIM), b.reshape(-1, local_heads, HEAD_DIM)], axis=2
    ).reshape(-1, 2 * head_share)
    w_kv = pair(w_key, w_value)
    b_kv = pair(jnp.zeros_like(b_value), b_value)
    kv = (dot(normed, w_kv) + b_kv).astype(bf16)
    queries = (dot(normed, w_query) + b_query).astype(bf16)

    feats, nf = features(rows_local * n_seq, row_lengths, head_ids, local_heads)
    first = seq_pos * rows_local
    tri = np.tril(np.ones((row_lengths.shape[0],) * 2, np.int32))
    run_ends = jnp.sum(tri * row_lengths[None, :], axis=1)
    row_begin = jnp.sum(jnp.where(first >= run_ends, row_lengths, 0))
    order = ring_order(seq_pos) if n_seq == 8 else jnp.arange(n_seq, dtype=jnp.int32)
    sc = jnp.concatenate([jnp.stack([seq_pos, row_begin]).astype(jnp.int32), relative, order])
    if n_seq == 8:
        (att, lse, *msgs), kv_tiles, cotangent, pack = ring_attend(queries, feats, nf, kv, sc, cotangent, pack)
    else:
        kv_tiles = lax.all_gather(kv, "seq", axis=0)
        att, lse, *msgs = attend_fwd(queries, feats, nf, kv_tiles, sc, n_seq)
    packs = head_whole(pack)
    g_whole = lax.all_gather(cotangent, "head", axis=1, tiled=True)

    pieces = head_pieces(*msgs)
    nm, middle, sub = mid1(
        relative, pieces, packs, input_whole, row2(b_out), row2(ln2_gain), row2(ln2_bias)
    )
    nm_all, act, d_inner, out0, out1, out2, *dn = ffn(
        relative, head_whole(nm), g_whole, w_up, w_down, row2(b_up)
    )
    gw_up = dot(nm_all, d_inner, TN).astype(bf16)
    gw_down = dot(act, g_whole, TN).astype(bf16)
    gb_up = jnp.sum(d_inner.astype(f32), axis=0)
    gb_down = jnp.sum(g_whole.astype(f32), axis=0)
    d_mid, dbr, *d_msgs, vec768, vec192 = mid2(
        relative, pieces, packs, middle, g_whole, row2(ln2_gain), head_terms(*dn)
    )
    d_pieces = head_pieces(*d_msgs)

    back = head_whole(jnp.concatenate([dbr] + [sub[r] for r in range(4)], axis=1))
    dbr_all = jnp.concatenate([b[:, :width] for b in back], axis=0)
    sub_all = jnp.concatenate(
        [b[:, width + r * head_share : width + (r + 1) * head_share] for r, b in enumerate(back)], axis=0
    )
    gw_out = dot(sub_all, dbr_all, TN).astype(bf16)
    gb_out = jnp.sum(dbr_all.astype(f32), axis=0)
    early = lax.psum_scatter(
        jnp.concatenate([gw_up, gw_down, gw_out], axis=0), "seq", scatter_dimension=0, tiled=True
    )

    if n_seq == 8:
        dq, dkv = ring_attend_back(queries, feats, nf, kv_tiles, d_pieces, att, lse, sc)
    else:
        dq, dkv_tiles = attend_bwd(queries, feats, nf, d_pieces, att, lse, kv_tiles, sc, n_seq)
        dkv = lax.psum_scatter(dkv_tiles, "seq", scatter_dimension=0, tiled=False)
    early, dkv = lax.optimization_barrier((early, dkv))
    early = lax.all_gather(early, "seq", axis=0, tiled=True)

    dq, out0, out1, out2 = lax.optimization_barrier((dq, out0, out1, out2))
    t0, t1, t2 = head_terms(out0, out1, out2)
    y = middle + (t0.astype(f32) + t1[0].astype(f32) + t2.astype(f32) + b_down)
    layer_output = lax.all_to_all(y.astype(bf16), "head", 1, 0, tiled=True)

    gw_query = dot(normed, dq, TN)
    gw_kv = dot(normed, dkv, TN)
    gb_query = jnp.sum(dq.astype(f32), axis=0)
    gb_kv = jnp.sum(dkv.astype(f32), axis=0)
    dn = dot(dq, w_query, NT) + dot(dkv, w_kv, NT)

    late = jnp.concatenate([gw_query.astype(bf16), gw_kv.astype(bf16)], axis=1)
    split = lambda v: jnp.sum(
        jnp.where(relative[:, None, None] == jnp.arange(4)[None, :, None], v[:, None, :], 0.0), axis=0
    ).reshape(-1)
    small = jnp.stack(
        [
            jnp.sum(dn * hat1, axis=0),
            jnp.sum(dn, axis=0),
            vec768[0],
            vec768[1],
            split(vec192[:4]),
            split(vec192[4:]),
        ]
    )
    small = small + lax.ppermute(small, "head", CORE)
    small = small + lax.ppermute(small, "head", CROSS)
    fill = lambda v: jnp.concatenate([v, jnp.zeros((width - v.shape[0],), f32)])
    small = jnp.concatenate(
        [small, jnp.stack([gb_up, gb_down, gb_out, fill(jnp.concatenate([gb_query, gb_kv]))])], axis=0
    )
    if n_seq == 8:
        for step in (1, 2, 4):
            small = small + lax.ppermute(small, "seq", exchange(step))
        late = halve_double(late)
    else:
        small = lax.psum(small, "seq")
        late = lax.psum(late, "seq")

    dn = dn.astype(bf16).reshape(2, 2, quarter, width)
    core, chip = head_pos % 2, head_pos // 2
    mine = lax.dynamic_index_in_dim(dn, core, 1, False)
    mate = lax.dynamic_index_in_dim(dn, 1 - core, 1, False)
    mine = add_low(mine, lax.ppermute(mate, "head", CORE))
    far = lax.ppermute(lax.dynamic_index_in_dim(mine, 1 - chip, 0, False), "head", CROSS)
    dn = lax.dynamic_index_in_dim(mine, chip, 0, False).astype(f32) + far.astype(f32)
    cut = lambda v: lax.dynamic_slice_in_dim(v, head_pos * quarter, quarter, 0)
    d_in = d_mid + norm_back(dn * ln1_gain, cut(hat1), cut(rs1))
    grad_input = lax.all_to_all(d_in.astype(bf16), "head", 1, 0, tiled=True).astype(f32)

    gw_query = late[:width, :head_share].astype(f32)
    gw_pair = late[:width, head_share:].astype(f32).reshape(width, local_heads, 2, HEAD_DIM)
    gw_key = gw_pair[:, :, 0].reshape(width, head_share)
    gw_value = gw_pair[:, :, 1].reshape(width, head_share)
    hidden = w_up.shape[1]
    early = early.astype(f32)
    gw_up, gw_down, gw_out = early[:width], early[width : width + hidden], early[width + hidden :]
    own = lambda v: lax.dynamic_slice_in_dim(v, head_pos * head_share, head_share, 0)
    gb_value = small[9, head_share : 3 * head_share].reshape(local_heads, 2, HEAD_DIM)[:, 1].reshape(-1)
    return (
        layer_output,
        grad_input,
        small[0],
        small[1],
        gw_query,
        small[9, :head_share],
        gw_key,
        gw_value,
        gb_value,
        own(small[4]),
        own(small[5]),
        gw_out,
        small[8],
        small[2],
        small[3],
        gw_up,
        small[6],
        gw_down,
        small[7],
    )


def solution(mesh):
    cols, rows, both, shared, vec = P(None, "head"), P("head", None), P("seq", "head"), P(), P("head")
    in_specs = (
        both, shared, shared, cols, vec, cols, cols, vec, vec, vec,
        rows, shared, shared, shared, cols, vec, rows, shared, both, shared,
    )
    out_specs = (
        both, both, shared, shared, cols, vec, cols, cols, vec, vec,
        vec, rows, shared, shared, shared, cols, vec, rows, shared,
    )
    return jax.shard_map(shards, mesh=mesh, in_specs=in_specs, out_specs=out_specs, check_vma=False)
```

```python
import functools

import jax
import jax.numpy as jnp
import numpy as np
from jax import lax
from jax.experimental import pallas as pl
from jax.experimental.pallas import tpu as pltpu
from jax.sharding import PartitionSpec as P

HEAD_DIM = 64
SEG = 2048
eps = 1e-05
segment_scales = (1, 2, 4, 8, 16)
dilation_steps = (1, 2, 4, 6, 12)
bf16 = jnp.bfloat16
f32 = jnp.float32
NT = (((1,), (1,)), ((), ()))
NN = (((1,), (0,)), ((), ()))
TN = (((0,), (0,)), ((), ()))
VMEM_LIMIT = 56 << 20

RING = (0, 2, 4, 6, 7, 5, 3, 1)
FWD = [(RING[i], RING[(i + 1) % 8]) for i in range(8)]
BWD = [(b, a) for a, b in FWD]
CORE = [(0, 1), (1, 0), (2, 3), (3, 2)]
CROSS = [(0, 2), (2, 0), (1, 3), (3, 1)]
BOTH = [(0, 3), (3, 0), (1, 2), (2, 1)]


def dot(a, b, dims=NN):
    return lax.dot_general(a, b, dims, preferred_element_type=f32)


def add_low(u, v):
    return (u.astype(f32) + v.astype(f32)).astype(u.dtype)


def exchange(step):
    return [(i, i ^ step) for i in range(8)]


def halve(x):
    idx = lax.axis_index("seq")
    for step in (1, 2, 4):
        half = x.shape[0] // 2
        bit = (idx // step) % 2
        keep = lax.dynamic_slice_in_dim(x, bit * half, half, 0)
        send = lax.dynamic_slice_in_dim(x, (1 - bit) * half, half, 0)
        x = add_low(keep, lax.ppermute(send, "seq", exchange(step)))
    return x


def ring_gather(x, later):
    half = x.shape[0] // 2
    a = b = x
    got = [x]
    for step in range(3):
        a, b = lax.ppermute(a, "seq", FWD), lax.ppermute(b, "seq", BWD)
        a, b = lax.optimization_barrier((a, b))
        got += [a, b]
    return got + [lax.ppermute(a[:half], "seq", FWD), lax.ppermute(b[half:], "seq", BWD)], later


def head_pieces(own, core, cross, both):
    return (
        own,
        lax.ppermute(core, "head", CORE),
        lax.ppermute(cross, "head", CROSS),
        lax.ppermute(both, "head", BOTH),
    )


def head_whole(x):
    p = lax.ppermute(x, "head", CROSS)
    return x, lax.ppermute(x, "head", CORE), p, lax.ppermute(p, "head", CORE)


def head_columns(got, head_pos):
    return jnp.concatenate([lax.select_n(head_pos ^ k, *got) for k in range(4)], axis=1)


SC = 6


def feature_table(total, nrow, nh, n_head):
    sizes = [nrow + total // (SEG * scale) for scale in segment_scales]
    nf = sum(sizes)
    width = -(-nh * nf // 128) * 128
    table = np.zeros((-(-(4 + n_head) // 8) * 8, width), np.int32)
    table[3] = -1
    for h in range(nh):
        lane = h * nf
        for scale, step, size in zip(segment_scales, dilation_steps, sizes):
            at = slice(lane, lane + size)
            table[0, at] = (SEG * scale).bit_length() - 1
            table[1, at] = SEG * scale - 1
            table[2, at] = lane
            table[3, at] = np.arange(lane, lane + size)
            for d in range(n_head):
                table[4 + d, at] = sum(1 << b for b in range(12) if b % step == (d * nh + h) % step)
            lane += size
    return table, nf


def feature_kernel(n, nrow, lengths, table, out, sc):
    tile = pl.program_id(0)
    bk, width = out.shape
    seq_pos, head_pos = lax.axis_index("seq"), lax.axis_index("head")
    ends, end, row_begin = [], 0, 0
    for r in range(nrow):
        end = end + lengths[r]
        ends.append(end)
        row_begin = jnp.where(end <= seq_pos * bk, end, row_begin)

    @pl.when(tile == 0)
    def _():
        sc[0] = seq_pos
        sc[1] = row_begin
        for r in range(4):
            sc[2 + r] = head_pos ^ r
        pos = sum(jnp.where(seq_pos == d, k, 0) for k, d in enumerate(RING))
        for k in range(n):
            if n == 8:
                at = (pos + (0, 7, 1, 6, 2, 5, 3, 4)[k]) & 7
                sc[SC + k] = sum(jnp.where(at == m, d, 0) for m, d in enumerate(RING))
            else:
                sc[SC + k] = k

    @pl.when((tile <= seq_pos) & ((tile + 1) * bk > row_begin))
    def _():
        shift, mask, first, own = (table[k : k + 1, :] for k in range(4))
        residues = table[pl.ds(4 + head_pos, 1), :]
        pos = tile * bk + lax.broadcasted_iota(jnp.int32, (bk, width), 0)
        begin = jnp.zeros((bk, width), jnp.int32)
        seg = jnp.broadcast_to(first, (bk, width))
        for r in range(nrow):
            past = pos >= ends[r]
            begin = jnp.where(past, ends[r], begin)
            seg = seg + jnp.where(past, (lengths[r] + mask) >> shift, 0)
        place = pos - begin
        seg = seg + (place >> shift)
        part = place & mask
        whole = ((part.astype(f32) + 0.5) * np.float32(1 / 12)).astype(jnp.int32)
        on = (residues >> (part - 12 * whole)) & 1
        out[...] = jnp.where(seg == own, on, 0).astype(f32).astype(bf16)


def features(total, lengths, nh, bk):
    n = total // bk
    nrow = lengths.shape[0]
    table, nf = feature_table(total, nrow, nh, lax.axis_size("head"))
    feats, sc = pl.pallas_call(
        functools.partial(feature_kernel, n, nrow),
        grid_spec=pltpu.PrefetchScalarGridSpec(
            num_scalar_prefetch=1,
            grid=(n,),
            in_specs=[pl.BlockSpec(table.shape, lambda i, s: (0, 0))],
            out_specs=[
                pl.BlockSpec((bk, table.shape[1]), lambda i, s: (i, 0)),
                pl.BlockSpec(memory_space=pltpu.SMEM),
            ],
        ),
        out_shape=[
            jax.ShapeDtypeStruct((total, table.shape[1]), bf16),
            jax.ShapeDtypeStruct((SC + n,), jnp.int32),
        ],
        compiler_params=pltpu.CompilerParams(dimension_semantics=("arbitrary",)),
        name="features",
    )(lengths, jnp.asarray(table))
    return feats, nf, sc


def head_pad(x, h, upper):
    part = x[:, HEAD_DIM * h : HEAD_DIM * (h + 1)]
    zero = jnp.zeros_like(part)
    return jnp.concatenate([zero, part] if upper else [part, zero], axis=1)


def count_tile(fk, fq, h, nf, first_key, first_row):
    lane = lax.broadcasted_iota(jnp.int32, fq.shape, 1)
    fqh = jnp.where((lane >= h * nf) & (lane < (h + 1) * nf), fq.astype(f32), 0.0).astype(bf16)
    count = dot(fk, fqh, NT)
    keys = first_key + lax.broadcasted_iota(jnp.int32, (count.shape[0], 1), 0)
    rows = first_row + lax.broadcasted_iota(jnp.int32, (1, count.shape[1]), 1)
    return jnp.where(keys <= rows, count, 0.0)


def fwd_tile(nh, nf, q, fq, kv, fk, first_key, first_row, acc, m, l):
    kv_t = kv[...].astype(f32).T.astype(bf16)
    qs = (q[...].astype(f32) * HEAD_DIM**-0.5).astype(bf16)
    for h in range(nh):
        s = dot(kv[:, 128 * h : 128 * h + 128], head_pad(qs, h, False), NT)
        count = count_tile(fk[...], fq[...], h, nf, first_key, first_row)
        s = jnp.where(count > 0, s, -1e30)
        old = m[h : h + 1, :]
        new = jnp.maximum(old, jnp.max(s, axis=0, keepdims=True))
        p = count * jnp.exp(s - new)
        factor = jnp.exp(old - new)
        l[h : h + 1, :] = l[h : h + 1, :] * factor + jnp.sum(p, axis=0, keepdims=True)
        o = dot(kv_t[128 * h : 128 * h + 128], p.astype(bf16))
        acc[64 * h : 64 * h + 64, :] = acc[64 * h : 64 * h + 64, :] * factor + o[64:, :]
        m[h : h + 1, :] = new


def bwd_tile(nh, nf, q, fq, do, lse, dterm, kv, fk, first_key, first_row, dq_t):
    kv_t = kv[...].astype(f32).T.astype(bf16)
    qs = (q[...].astype(f32) * HEAD_DIM**-0.5).astype(bf16)
    out = []
    for h in range(nh):
        kvh = kv[:, 128 * h : 128 * h + 128]
        qh = head_pad(qs, h, False)
        doh = head_pad(do[...], h, True)
        count = count_tile(fk[...], fq[...], h, nf, first_key, first_row)
        p = count * jnp.exp(jnp.minimum(dot(kvh, qh, NT) - lse[h : h + 1, :], 1.0))
        ds = (p * (dot(kvh, doh, NT) - dterm[h : h + 1, :])).astype(bf16)
        out.append((dot(ds, qh) + dot(p.astype(bf16), doh)).astype(bf16))
        o = dot(kv_t[128 * h : 128 * h + 128], ds)
        dq_t[64 * h : 64 * h + 64, :] += o[:64, :]
    return out


def fwd_start(acc, m, l):
    acc[...] = jnp.zeros_like(acc)
    m[...] = jnp.full_like(m, -1e30)
    l[...] = jnp.zeros_like(l)


def fwd_end(nh, quarters, acc, m, l, out, lse, msgs):
    for h in range(nh):
        out[:, 64 * h : 64 * h + 64] = (acc[64 * h : 64 * h + 64, :] / l[h : h + 1, :]).T
    lse[...] = m[...] + jnp.log(jnp.maximum(l[...], 1e-30))
    rows = msgs[0].shape[0]
    for at, msg in zip(quarters, msgs):
        msg[...] = out[pl.ds(pl.multiple_of(at * rows, rows), rows), :].astype(bf16)


def bwd_start(nh, quarters, pieces, att, do, dterm, dq_t):
    dq_t[...] = jnp.zeros_like(dq_t)
    rows = pieces[0].shape[0]
    for at, piece in zip(quarters, pieces):
        do[pl.ds(pl.multiple_of(at * rows, rows), rows), :] = piece[...]
    prod = do[...].astype(f32) * att[...]
    r = lax.broadcasted_iota(jnp.int32, (8, prod.shape[1]), 0)
    c = lax.broadcasted_iota(jnp.int32, (8, prod.shape[1]), 1)
    pick = jnp.where(c // HEAD_DIM == r, 1.0, 0.0).astype(f32)
    dterm[...] = lax.dot_general(
        pick, prod, NT, precision=lax.Precision.HIGHEST, preferred_element_type=f32
    )


def tile_needed(tile, sc, bk):
    return (tile <= sc[0]) & ((tile + 1) * bk > sc[1])


def fwd_grid(nh, nf, n, sc, q, fq, kv, fk, out, lse, m0, m1, m2, m3, acc, m, l):
    i = pl.program_id(0)
    bk = kv.shape[1]

    @pl.when(i == 0)
    def _():
        fwd_start(acc, m, l)

    @pl.when(tile_needed(sc[SC + i], sc, bk))
    def _():
        fwd_tile(nh, nf, q, fq, kv.at[0], fk, sc[SC + i] * bk, sc[0] * q.shape[0], acc, m, l)

    @pl.when(i == n - 1)
    def _():
        fwd_end(nh, [sc[2 + r] for r in range(4)], acc, m, l, out, lse, (m0, m1, m2, m3))


def bwd_grid(nh, nf, n, sc, q, fq, d0, d1, d2, d3, att, lse, kv, fk, dq, dkv, do, dterm, dq_t):
    i = pl.program_id(0)
    bk = kv.shape[1]

    @pl.when(i == 0)
    def _():
        bwd_start(nh, [sc[2 + r] for r in range(4)], (d0, d1, d2, d3), att, do, dterm, dq_t)

    need = tile_needed(sc[SC + i], sc, bk)

    @pl.when(jnp.logical_not(need))
    def _():
        dkv[...] = jnp.zeros_like(dkv)

    @pl.when(need)
    def _():
        out = bwd_tile(
            nh, nf, q, fq, do, lse, dterm, kv.at[0], fk, sc[SC + i] * bk, sc[0] * q.shape[0], dq_t
        )
        for h in range(nh):
            dkv[0, :, 128 * h : 128 * h + 128] = out[h]

    @pl.when(i == n - 1)
    def _():
        dq[...] = (dq_t[...].T * HEAD_DIM**-0.5).astype(dq.dtype)


def whole_block(*shape):
    return pl.BlockSpec(shape, lambda i, s: (0,) * len(shape))


def struct(shape, dtype):
    return jax.ShapeDtypeStruct(shape, dtype)


def params():
    return pltpu.CompilerParams(
        dimension_semantics=("arbitrary",), vmem_limit_bytes=VMEM_LIMIT
    )


def fwd_outs(tq, wd):
    return [struct((tq, wd), f32), struct((8, tq), f32)] + [struct((tq // 4, wd), bf16)] * 4


def attend_fwd(q, feats, nf, kv, sc, n):
    tq, wd = q.shape
    bk, width = kv.shape[1], feats.shape[1]
    outs = fwd_outs(tq, wd)
    return pl.pallas_call(
        functools.partial(fwd_grid, wd // HEAD_DIM, nf, n),
        grid_spec=pltpu.PrefetchScalarGridSpec(
            num_scalar_prefetch=1,
            grid=(n,),
            in_specs=[
                whole_block(tq, wd),
                pl.BlockSpec((tq, width), lambda i, s: (s[0], 0)),
                pl.BlockSpec((1, bk, 2 * wd), lambda i, s: (i, 0, 0)),
                pl.BlockSpec((bk, width), lambda i, s: (s[SC + i], 0)),
            ],
            out_specs=[whole_block(*o.shape) for o in outs],
            scratch_shapes=[
                pltpu.VMEM((wd, tq), f32),
                pltpu.VMEM((8, tq), f32),
                pltpu.VMEM((8, tq), f32),
            ],
        ),
        out_shape=outs,
        compiler_params=params(),
        name="attend_fwd",
    )(sc, q, feats, kv, feats)


def attend_bwd(q, feats, nf, pieces, att, lse, kv, sc, n):
    tq, wd = q.shape
    bk, width = kv.shape[1], feats.shape[1]
    return pl.pallas_call(
        functools.partial(bwd_grid, wd // HEAD_DIM, nf, n),
        grid_spec=pltpu.PrefetchScalarGridSpec(
            num_scalar_prefetch=1,
            grid=(n,),
            in_specs=[whole_block(tq, wd), pl.BlockSpec((tq, width), lambda i, s: (s[0], 0))]
            + [whole_block(tq // 4, wd)] * 4
            + [
                whole_block(tq, wd),
                whole_block(8, tq),
                pl.BlockSpec((1, bk, 2 * wd), lambda i, s: (i, 0, 0)),
                pl.BlockSpec((bk, width), lambda i, s: (s[SC + i], 0)),
            ],
            out_specs=[whole_block(tq, wd), pl.BlockSpec((1, bk, 2 * wd), lambda i, s: (i, 0, 0))],
            scratch_shapes=[
                pltpu.VMEM((tq, wd), bf16),
                pltpu.VMEM((8, tq), f32),
                pltpu.VMEM((wd, tq), f32),
            ],
        ),
        out_shape=[struct((tq, wd), bf16), struct(kv.shape, bf16)],
        compiler_params=params(),
        name="attend_bwd",
    )(sc, q, feats, *pieces, att, lse, kv, feats)


def fwd_part(nh, nf, tiles, bk, first, last, sc, *refs):
    q, fq = refs[:2]
    n = len(tiles)
    kvs, fks = refs[2 : 2 + n], refs[2 + n : 2 + 2 * n]
    rest = refs[2 + 2 * n :]
    if not first:
        rest = rest[3:]
    if last:
        out, lse, *msgs = rest[:6]
        acc, m, l = rest[6:9]
    else:
        acc, m, l = rest[:3]
    if first:
        fwd_start(acc, m, l)
    for (place, rows, offset), kv, fk in zip(tiles, kvs, fks):

        @pl.when(tile_needed(sc[SC + place], sc, bk))
        def _():
            fwd_tile(
                nh, nf, q, fq, kv, fk, sc[SC + place] * bk + offset, sc[0] * q.shape[0], acc, m, l
            )

    if last:
        fwd_end(nh, [sc[2 + r] for r in range(4)], acc, m, l, out, lse, msgs)


def attend_fwd_part(q, feats, nf, kvs, tiles, state, sc, last):
    tq, wd = q.shape
    width = feats.shape[1]
    n = len(tiles)
    sums = [struct((wd, tq), f32), struct((8, tq), f32), struct((8, tq), f32)]
    ins = [whole_block(tq, wd), pl.BlockSpec((tq, width), lambda i, s: (s[0], 0))]
    ins += [whole_block(*kv.shape) for kv in kvs]
    for place, rows, offset in tiles:
        at = lambda i, s, p=place, k=tq // rows, o=offset // rows: (s[SC + p] * k + o, 0)
        ins.append(pl.BlockSpec((rows, width), at))
    args = [sc, q, feats, *kvs, *([feats] * n)]
    outs = (fwd_outs(tq, wd) if last else []) + sums
    alias = {}
    if state is not None:
        ins += [whole_block(*o.shape) for o in sums]
        alias = {len(args) + k: len(outs) - 3 + k for k in range(3)}
        args += state

    def kernel(sc_ref, *refs):
        if state is not None:
            olds = refs[2 + 2 * n : 5 + 2 * n]
            news = refs[len(refs) - 3 :]
            for old, new in zip(olds, news):
                new[...] = old[...]
        fwd_part(wd // HEAD_DIM, nf, tiles, tq, state is None, last, sc_ref, *refs)

    got = pl.pallas_call(
        kernel,
        grid_spec=pltpu.PrefetchScalarGridSpec(
            num_scalar_prefetch=1,
            grid=(1,),
            in_specs=ins,
            out_specs=[whole_block(*o.shape) for o in outs],
        ),
        out_shape=outs,
        input_output_aliases=alias,
        compiler_params=params(),
        cost_estimate=pl.CostEstimate(flops=n << 31, bytes_accessed=n << 20, transcendentals=0),
        name="fwd_part",
    )(*args)
    return got[:6] if last else got


def attend_bwd_part(q, feats, nf, kvs, tiles, lse, sc, start, state, last):
    tq, wd = q.shape
    nh = wd // HEAD_DIM
    width = feats.shape[1]
    n = len(tiles)
    held = [struct((tq, wd), bf16), struct((8, tq), f32), struct((wd, tq), f32)]
    ins = [whole_block(tq, wd), pl.BlockSpec((tq, width), lambda i, s: (s[0], 0)), whole_block(8, tq)]
    ins += [whole_block(*kv.shape) for kv in kvs]
    for place, rows, offset in tiles:
        at = lambda i, s, p=place, k=tq // rows, o=offset // rows: (s[SC + p] * k + o, 0)
        ins.append(pl.BlockSpec((rows, width), at))
    args = [sc, q, feats, lse, *kvs, *([feats] * n)]
    outs = [struct(kv.shape, bf16) for kv in kvs]
    more = start if start is not None else state
    ins += [whole_block(*v.shape) for v in more]
    args += more
    if start is not None:
        outs = outs + held
    elif not last:
        outs = outs + held[2:]
    if last:
        outs = outs + [struct((tq, wd), bf16)]
    scratch = [pltpu.VMEM((wd, tq), f32)] if last else []

    def kernel(sc_ref, *refs):
        q_ref, fq, lse_ref = refs[:3]
        kv_refs, fks = refs[3 : 3 + n], refs[3 + n : 3 + 2 * n]
        given = refs[3 + 2 * n : 3 + 2 * n + len(more)]
        rest = refs[3 + 2 * n + len(more) :]
        dkvs, rest = rest[:n], rest[n:]
        if start is not None:
            do, dterm, dq_t = rest[:3]
            bwd_start(nh, [sc_ref[2 + r] for r in range(4)], given[:4], given[4], do, dterm, dq_t)
        else:
            do, dterm, old = given
            dq_t = rest[-1] if last else rest[0]
            dq_t[...] = old[...]
        for (place, rows, offset), kv, fk, dkv in zip(tiles, kv_refs, fks, dkvs):
            need = tile_needed(sc_ref[SC + place], sc_ref, tq)

            @pl.when(jnp.logical_not(need))
            def _():
                dkv[...] = jnp.zeros_like(dkv)

            @pl.when(need)
            def _():
                got = bwd_tile(
                    nh, nf, q_ref, fq, do, lse_ref, dterm, kv, fk,
                    sc_ref[SC + place] * tq + offset, sc_ref[0] * tq, dq_t,
                )
                for h in range(nh):
                    dkv[:, 128 * h : 128 * h + 128] = got[h]

        if last:
            rest[0][...] = (dq_t[...].T * HEAD_DIM**-0.5).astype(bf16)

    return pl.pallas_call(
        kernel,
        grid_spec=pltpu.PrefetchScalarGridSpec(
            num_scalar_prefetch=1,
            grid=(1,),
            in_specs=ins,
            out_specs=[whole_block(*o.shape) for o in outs],
            scratch_shapes=scratch,
        ),
        out_shape=outs,
        compiler_params=params(),
        cost_estimate=pl.CostEstimate(flops=n << 31, bytes_accessed=n << 20, transcendentals=0),
        name="bwd_part",
    )(*args)


def ring_attend(q, feats, nf, kv, sc, g, pack, head_pos):
    rows = kv.shape[0]
    half = rows // 2
    a = b = kv
    tiles, state = [kv], None
    whole = lambda p: (p, rows, 0)
    part = functools.partial(attend_fwd_part, q, feats, nf)
    for step in range(3):
        a2, b2 = lax.ppermute(a, "seq", FWD), lax.ppermute(b, "seq", BWD)
        if step == 0:
            state = part([kv], [whole(0)], None, sc, False)
        else:
            state = part([a, b], [whole(2 * step - 1), whole(2 * step)], state, sc, False)
        a, b, state = lax.optimization_barrier((a2, b2, state))
        if step == 0:
            a, b, g, pack = lax.optimization_barrier((a, b, g, pack))
            far_g, far_pack = (lax.ppermute(v, "head", CROSS) for v in (g, pack))
        if step == 2:
            a, b, far_g, far_pack = lax.optimization_barrier((a, b, far_g, far_pack))
            gs, packs = (
                [v, lax.ppermute(v, "head", CORE), w, lax.ppermute(w, "head", CORE)]
                for v, w in ((g, far_g), (pack, far_pack))
            )
        tiles += [a, b]
    c, d = lax.ppermute(a[:half], "seq", FWD), lax.ppermute(b[half:], "seq", BWD)
    g = head_columns(gs, head_pos)
    state = part([a, b], [whole(5), whole(6)], state, sc, False)
    tiles += [c, d]
    c, d, g, state = lax.optimization_barrier((c, d, g, state))
    return part([c, d], [(7, half, 0), (7, half, half)], state, sc, True), tiles, g, packs


def ring_attend_back(q, feats, nf, tiles, pieces, att, lse, sc, beside):
    rows = tiles[0].shape[0]
    half = rows // 2
    whole = lambda p: (p, rows, 0)
    part = functools.partial(attend_bwd_part, q, feats, nf)
    c, d, do, dterm, dq_t = part(
        tiles[7:9], [(7, half, 0), (7, half, half)], lse, sc, [*pieces, att], None, False
    )
    c, d, dq_t = lax.optimization_barrier((c, d, dq_t))
    a, b = lax.ppermute(c, "seq", FWD), lax.ppermute(d, "seq", BWD)
    for place in (5, 3, 1):
        t, u, dq_t = part(
            tiles[place : place + 2], [whole(place), whole(place + 1)], lse, sc, None, [do, dterm, dq_t], False
        )
        if place == 5:
            up = jnp.concatenate([add_low(u[:half], a), u[half:]], axis=0)
            down = jnp.concatenate([t[:half], add_low(t[half:], b)], axis=0)
        else:
            up, down = add_low(u, a), add_low(t, b)
        if place == 5:
            up, down, dq_t, beside = lax.optimization_barrier((up, down, dq_t, beside))
        else:
            up, down, dq_t = lax.optimization_barrier((up, down, dq_t))
        a, b = lax.ppermute(up, "seq", FWD), lax.ppermute(down, "seq", BWD)
    t, dq = part([tiles[0]], [whole(0)], lse, sc, None, [do, dterm, dq_t], True)
    return dq, (t.astype(f32) + a.astype(f32) + b.astype(f32)).astype(bf16), beside


VEC_ROWS = 16


def out_pack(w_out, sub_gain, sub_bias):
    width = w_out.shape[1]
    share = sub_gain.shape[0]
    room = width // 3
    pad = lambda v: jnp.concatenate([v, jnp.zeros((room - share,), f32)])
    vec = jnp.concatenate([pad(sub_gain), pad(sub_bias), jnp.zeros((room,), f32)]).reshape(1, width)
    high = vec.astype(bf16)
    rest = vec - lax.optimization_barrier(high).astype(f32)
    middle = rest.astype(bf16)
    low = (rest - lax.optimization_barrier(middle).astype(f32)).astype(bf16)
    top = jnp.concatenate([high, middle, low, jnp.zeros((VEC_ROWS - 3, width), bf16)], axis=0)
    return jnp.concatenate([top, w_out], axis=0)


def unpack_vec(w, row):
    v = w[0:VEC_ROWS, :].astype(f32)
    return v[row : row + 1] + v[row + 1 : row + 2] + v[row + 2 : row + 3]


def sub_parts(pieces, width):
    total = sum(jnp.sum(p, axis=1, keepdims=True) for p in pieces)
    square = sum(jnp.sum(p * p, axis=1, keepdims=True) for p in pieces)
    mean = total / width
    inv = lax.rsqrt(square / width - mean * mean + eps)
    return [(p - mean) * inv for p in pieces], inv


def norm_parts(x):
    center = x - jnp.mean(x, axis=1, keepdims=True)
    rs = lax.rsqrt(jnp.mean(center * center, axis=1, keepdims=True) + eps)
    return center * rs, rs


def norm_back(g, hat, rs):
    return rs * (
        g - jnp.mean(g, axis=1, keepdims=True) - hat * jnp.mean(g * hat, axis=1, keepdims=True)
    )


def mid1_kernel(sc, p0, p1, p2, p3, w0, w1, w2, w3, x, b_out, gain2, bias2, nm, middle, sub):
    share = p0.shape[1]
    room = w0.shape[1] // 3
    cen, _ = sub_parts([p[...].astype(f32) for p in (p0, p1, p2, p3)], w0.shape[1])
    acc = x[...].astype(f32) + b_out[...]
    for r, w in enumerate((w0, w1, w2, w3)):
        vec = unpack_vec(w, 0)
        s = (cen[r] * vec[:, :share] + vec[:, room : room + share]).astype(bf16)
        sub[r] = s
        acc = acc + dot(s, w[VEC_ROWS : VEC_ROWS + share, :])
    middle[...] = acc
    hat, _ = norm_parts(acc)
    nm[...] = (hat * gain2[...] + bias2[...]).astype(bf16)


def gelu_parts(z):
    half = 0.5 * (1.0 + lax.erf(z * np.float32(np.sqrt(0.5))))
    slope = half + z * (np.float32(1.0 / np.sqrt(2.0 * np.pi)) * jnp.exp(-0.5 * z * z))
    return z * half, slope


def ffn_kernel(sc, n0, n1, n2, n3, g, w_up, w_down, b_up, nm, act, d_inner, *outs):
    rows = n0.shape[0]
    for r, piece in enumerate((n0, n1, n2, n3)):
        at = pl.ds(pl.multiple_of(sc[r] * rows, rows), rows)
        x = piece[...]
        nm[at, :] = x
        a, slope = gelu_parts(dot(x, w_up[...]) + b_up[...])
        a = a.astype(bf16)
        d = (dot(g[at, :], w_down[...], NT) * slope).astype(bf16)
        act[at, :] = a
        d_inner[at, :] = d
        outs[r][...] = dot(a, w_down[...]).astype(bf16)
        outs[4 + r][...] = dot(d, w_up[...], NT).astype(bf16)


def mid2_kernel(sc, p0, p1, p2, p3, w0, w1, w2, w3, middle, g, gain2, t0, t1, t2, t3, *refs):
    d_mid, dbr, d0, d1, d2, d3, vec768, vec192 = refs
    share = p0.shape[1]
    width = w0.shape[1]
    dn = sum(t[...].astype(f32) for t in (t0, t1, t2, t3))
    hat, rs = norm_parts(middle[...])
    vec768[0:1, :] = jnp.sum(dn * hat, axis=0, keepdims=True)
    vec768[1:2, :] = jnp.sum(dn, axis=0, keepdims=True)
    dm = g[...].astype(f32) + norm_back(dn * gain2[...], hat, rs)
    d_mid[...] = dm
    branch = dm.astype(bf16)
    dbr[...] = branch
    cen, inv = sub_parts([p[...].astype(f32) for p in (p0, p1, p2, p3)], width)
    hats = []
    for r, w in enumerate((w0, w1, w2, w3)):
        ds = dot(branch, w[VEC_ROWS : VEC_ROWS + share, :], NT)
        vec192[r : r + 1, :] = jnp.sum(ds * cen[r], axis=0, keepdims=True)
        vec192[r + 4 : r + 5, :] = jnp.sum(ds, axis=0, keepdims=True)
        hats.append(ds * unpack_vec(w, 0)[:, :share])
    s1 = sum(jnp.sum(t, axis=1, keepdims=True) for t in hats) / width
    s2 = sum(jnp.sum(t * c, axis=1, keepdims=True) for t, c in zip(hats, cen)) / width
    for o, t, c in zip((d0, d1, d2, d3), hats, cen):
        o[...] = (inv * (t - s1 - c * s2)).astype(bf16)


def one_step(kernel, ins, in_specs, outs, name, flops, scratch=()):
    return pl.pallas_call(
        kernel,
        grid_spec=pltpu.PrefetchScalarGridSpec(
            num_scalar_prefetch=1,
            grid=(1,),
            in_specs=in_specs,
            out_specs=[whole_block(*o.shape) for o in outs],
            scratch_shapes=scratch,
        ),
        out_shape=outs,
        compiler_params=params(),
        cost_estimate=pl.CostEstimate(flops=flops, bytes_accessed=12 << 20, transcendentals=0),
        name=name,
    )(*ins)


def mid1(head_no, pieces, packs, x, b_out, gain2, bias2):
    quarter, share = pieces[0].shape
    rows, width = packs[0].shape
    at_quarter = pl.BlockSpec((quarter, width), lambda i, s: (s[0], 0))
    return one_step(
        mid1_kernel,
        (head_no, *pieces, *packs, x, b_out, gain2, bias2),
        [whole_block(quarter, share)] * 4
        + [whole_block(rows, width)] * 4
        + [at_quarter]
        + [whole_block(1, width)] * 3,
        [struct((quarter, width), bf16), struct((quarter, width), f32), struct((4, quarter, share), bf16)],
        "mid1",
        2 * quarter * width * width,
    )


def ffn(head_no, pieces, g, w_up, w_down, b_up):
    quarter, width = pieces[0].shape
    hidden = w_up.shape[1]
    full = struct((4 * quarter, hidden), bf16)
    ins = (head_no, *pieces, g, w_up, w_down, b_up)
    outs = [struct((4 * quarter, width), bf16), full, full] + [struct((quarter, width), bf16)] * 8
    flops = 32 * quarter * width * hidden
    return one_step(ffn_kernel, ins, [whole_block(*v.shape) for v in ins[1:]], outs, "ffn", flops)


def mid2(head_no, pieces, packs, middle, g, gain2, terms):
    quarter, share = pieces[0].shape
    rows, width = packs[0].shape
    at_quarter = pl.BlockSpec((quarter, width), lambda i, s: (s[0], 0))
    return one_step(
        mid2_kernel,
        (head_no, *pieces, *packs, middle, g, gain2, *terms),
        [whole_block(quarter, share)] * 4
        + [whole_block(rows, width)] * 4
        + [whole_block(quarter, width), at_quarter, whole_block(1, width)]
        + [whole_block(*t.shape) for t in terms],
        [struct((quarter, width), f32), struct((quarter, width), bf16)]
        + [struct((quarter, share), bf16)] * 4
        + [struct((8, width), f32), struct((8, share), f32)],
        "mid2",
        2 * quarter * width * width,
    )


def spread_kernel(sc, *refs):
    tiles, (gq, gk, gv, go, gu, gd, held) = refs[:9], refs[9:]
    rows = tiles[0].shape[0] // 3
    share = gq.shape[1]

    def put(out, at, value):
        out[pl.ds(pl.multiple_of(at, 8), value.shape[0]), :] = value

    def put_late(at, value):
        for k, out in enumerate((gq, gk, gv, held)):
            put(out, at, value[:, k * share : (k + 1) * share])

    for k in range(8):
        d = sc[SC + k]
        late_at = ((d & 1) * 4 + ((d >> 1) & 1) * 2 + (d >> 2)) * rows
        at = d * rows
        if k < 7:
            t = tiles[k][...].astype(f32)
            put_late(late_at, t[:rows])
            put(gu, at, t[rows : 2 * rows])
            put(gd, at, t[2 * rows :])
        else:
            half = rows // 2
            t, u = tiles[7][...].astype(f32), tiles[8][...].astype(f32)
            put_late(late_at, t[:rows])
            put(gu, at, t[rows:])
            put(gu, at + half, u[:half])
            put(gd, at, u[half:])
    go[...] = held[...].T


def spread(sc, tiles, hidden):
    width = tiles[0].shape[1]
    share = width // 4
    outs = [struct((width, share), f32)] * 3 + [
        struct((share, width), f32),
        struct((width, hidden), f32),
        struct((hidden, width), f32),
    ]
    return one_step(
        spread_kernel,
        (sc, *tiles),
        [whole_block(*t.shape) for t in tiles],
        outs,
        "spread",
        1 << 30,
        [pltpu.VMEM((width, share), f32)],
    )


def shards(
    layer_input, ln1_gain, ln1_bias, w_query, b_query, w_key, w_value, b_value, sub_gain, sub_bias,
    w_out, b_out, ln2_gain, ln2_bias, w_up, b_up, w_down, b_down, cotangent, row_lengths,
):
    rows_local, slice_width = layer_input.shape
    head_share = w_query.shape[1]
    local_heads = head_share // HEAD_DIM
    head_pos = lax.axis_index("head")
    seq_pos = lax.axis_index("seq")
    n_seq = lax.axis_size("seq")
    width = head_share * lax.axis_size("head")
    quarter = rows_local // 4
    relative = jnp.stack([head_pos, head_pos ^ 1, head_pos ^ 2, head_pos ^ 3]).astype(jnp.int32)
    row2 = lambda v: v.reshape(1, -1)

    pack = out_pack(w_out, sub_gain, sub_bias)
    input_whole = lax.all_gather(layer_input, "head", axis=1, tiled=True)
    hat1, rs1 = norm_parts(input_whole.astype(f32))
    normed = (hat1 * ln1_gain + ln1_bias).astype(bf16)
    pair = lambda a, b: jnp.stack(
        [a.reshape(-1, local_heads, HEAD_DIM), b.reshape(-1, local_heads, HEAD_DIM)], axis=2
    ).reshape(-1, 2 * head_share)
    w_kv = pair(w_key, w_value)
    b_kv = pair(jnp.zeros_like(b_value), b_value)
    kv = (dot(normed, w_kv) + b_kv).astype(bf16)
    queries = (dot(normed, w_query) + b_query).astype(bf16)

    feats, nf, sc = features(rows_local * n_seq, row_lengths, local_heads, rows_local)
    kv, cotangent, pack = lax.optimization_barrier((kv, cotangent, pack))
    if n_seq == 8:
        (att, lse, *msgs), kv_tiles, g_whole, packs = ring_attend(
            queries, feats, nf, kv, sc, cotangent, pack, head_pos
        )
    else:
        kv_tiles = lax.all_gather(kv, "seq", axis=0)
        att, lse, *msgs = attend_fwd(queries, feats, nf, kv_tiles, sc, n_seq)
        g_whole, packs = head_columns(head_whole(cotangent), head_pos), head_whole(pack)

    pieces = head_pieces(*msgs)
    nm, middle, sub = mid1(
        relative, pieces, packs, input_whole, row2(b_out), row2(ln2_gain), row2(ln2_bias)
    )
    nm_all, act, d_inner, *terms = ffn(relative, head_whole(nm), g_whole, w_up, w_down, row2(b_up))
    outs, dn = terms[:4], head_pieces(*terms[4:])
    gw_up = dot(nm_all, d_inner, TN).astype(bf16)
    gw_down = dot(act, g_whole, TN).astype(bf16)
    early = jnp.concatenate([v.reshape(8, -1, v.shape[1]) for v in (gw_up, gw_down)], axis=1)
    early = early.reshape(-1, early.shape[2])
    if n_seq == 8:
        early = lax.psum_scatter(early, "seq", scatter_dimension=0, tiled=True)
    d_mid, dbr, *d_msgs, vec768, vec192 = mid2(
        relative, pieces, packs, middle, g_whole, row2(ln2_gain), dn
    )
    d_pieces = head_pieces(*d_msgs)
    beside = (outs, dbr, sub, vec768, vec192, d_inner)
    d_pieces, beside = lax.optimization_barrier((d_pieces, beside))

    if n_seq == 8:
        dq, dkv, beside = ring_attend_back(
            queries, feats, nf, kv_tiles, d_pieces, att, lse, sc, beside
        )
    else:
        dq, dkv_tiles = attend_bwd(queries, feats, nf, d_pieces, att, lse, kv_tiles, sc, n_seq)
        dkv = lax.psum_scatter(dkv_tiles, "seq", scatter_dimension=0, tiled=False)
        early = lax.psum(early, "seq")
    outs, dbr, sub, vec768, vec192, d_inner = beside

    y = middle + (sum(t.astype(f32) for t in head_pieces(*outs)) + b_down)
    layer_output = lax.all_to_all(y.astype(bf16), "head", 1, 0, tiled=True)

    dbr_all = jnp.concatenate(head_whole(dbr), axis=0)
    sub_all = jnp.concatenate(head_pieces(*[sub[r] for r in range(4)]), axis=0)
    gw_out = dot(dbr_all, sub_all, TN).astype(bf16)
    gb_out = jnp.sum(dbr_all.astype(f32), axis=0)
    gb_up = jnp.sum(d_inner.astype(f32), axis=0)
    gb_down = jnp.sum(g_whole.astype(f32), axis=0)
    split = lambda v: jnp.sum(
        jnp.where(relative[:, None, None] == jnp.arange(4)[None, :, None], v[:, None, :], 0.0), axis=0
    ).reshape(-1)
    dkv = dkv.reshape(rows_local, local_heads, 2, HEAD_DIM)
    d_qkv = jnp.concatenate(
        [dq] + [dkv[:, :, k].reshape(rows_local, head_share) for k in range(2)], axis=1
    )
    w_qkv = jnp.concatenate([w_query, w_key, w_value], axis=1)
    late = jnp.concatenate([dot(normed, d_qkv, TN).astype(bf16), gw_out], axis=1)
    late, d_qkv = lax.optimization_barrier((late, d_qkv))
    if n_seq == 8:
        piece, early = lax.optimization_barrier((halve(late), early))
        tiles, _ = ring_gather(jnp.concatenate([piece, early], axis=0), ())
        gw_query, gw_key, gw_value, gw_out, gw_up, gw_down = spread(sc, tiles, w_up.shape[1])
    else:
        late = lax.psum(late, "seq").astype(f32)
        gw_query, gw_key, gw_value = (late[:, k * head_share : (k + 1) * head_share] for k in range(3))
        gw_out = late[:, 3 * head_share :].T
        early = early.astype(f32).reshape(8, 2, -1, width)
        gw_up, gw_down = early[:, 0].reshape(-1, width), early[:, 1].reshape(-1, width)

    dn = dot(d_qkv, w_qkv, NT)
    gb_qkv = jnp.sum(d_qkv.astype(f32), axis=0)
    fill = lambda v: jnp.concatenate([v, jnp.zeros((width - v.shape[0],), f32)])
    small = jnp.stack(
        [
            jnp.sum(dn * hat1, axis=0),
            jnp.sum(dn, axis=0),
            vec768[0],
            vec768[1],
            split(vec192[:4]),
            split(vec192[4:]),
        ]
    )
    small = small + lax.ppermute(small, "head", CORE)
    small = small + lax.ppermute(small, "head", CROSS)
    small = jnp.concatenate([small, jnp.stack([gb_up, gb_down, gb_out, fill(gb_qkv)])], axis=0)
    if n_seq == 8:
        for step in (1, 2, 4):
            small = small + lax.ppermute(small, "seq", exchange(step))
    else:
        small = lax.psum(small, "seq")

    dn = dn.astype(bf16).reshape(2, 2, quarter, width)
    core, chip = head_pos % 2, head_pos // 2
    mine = lax.dynamic_index_in_dim(dn, core, 1, False)
    mate = lax.dynamic_index_in_dim(dn, 1 - core, 1, False)
    mine = add_low(mine, lax.ppermute(mate, "head", CORE))
    far = lax.ppermute(lax.dynamic_index_in_dim(mine, 1 - chip, 0, False), "head", CROSS)
    dn = lax.dynamic_index_in_dim(mine, chip, 0, False).astype(f32) + far.astype(f32)
    cut = lambda v: lax.dynamic_slice_in_dim(v, head_pos * quarter, quarter, 0)
    d_in = d_mid + norm_back(dn * ln1_gain, cut(hat1), cut(rs1))
    grad_input = lax.all_to_all(d_in.astype(bf16), "head", 1, 0, tiled=True).astype(f32)

    gb_qkv = small[9]
    own = lambda v: lax.dynamic_slice_in_dim(v, head_pos * head_share, head_share, 0)
    gb_value = gb_qkv[2 * head_share : 3 * head_share]
    return (
        layer_output,
        grad_input,
        small[0],
        small[1],
        gw_query,
        gb_qkv[:head_share],
        gw_key,
        gw_value,
        gb_value,
        own(small[4]),
        own(small[5]),
        gw_out,
        small[8],
        small[2],
        small[3],
        gw_up,
        small[6],
        gw_down,
        small[7],
    )


def solution(mesh):
    cols, rows, both, shared, vec = P(None, "head"), P("head", None), P("seq", "head"), P(), P("head")
    in_specs = (
        both, shared, shared, cols, vec, cols, cols, vec, vec, vec,
        rows, shared, shared, shared, cols, vec, rows, shared, both, shared,
    )
    out_specs = (
        both, both, shared, shared, cols, vec, cols, cols, vec, vec,
        vec, rows, shared, shared, shared, cols, vec, rows, shared,
    )
    return jax.shard_map(shards, mesh=mesh, in_specs=in_specs, out_specs=out_specs, check_vma=False)
```

```python
import functools

import jax
import jax.numpy as jnp
import numpy as np
from jax import lax
from jax.experimental import pallas as pl
from jax.experimental.pallas import tpu as pltpu
from jax.sharding import PartitionSpec as P

HEAD_DIM = 64
SEG = 2048
eps = 1e-05
segment_scales = (1, 2, 4, 8, 16)
dilation_steps = (1, 2, 4, 6, 12)
bf16 = jnp.bfloat16
f32 = jnp.float32
NT = (((1,), (1,)), ((), ()))
NN = (((1,), (0,)), ((), ()))
TN = (((0,), (0,)), ((), ()))

RING = (0, 2, 4, 6, 7, 5, 3, 1)
FWD = [(RING[i], RING[(i + 1) % 8]) for i in range(8)]
BWD = [(b, a) for a, b in FWD]
CORE = [(0, 1), (1, 0), (2, 3), (3, 2)]
CROSS = [(0, 2), (2, 0), (1, 3), (3, 1)]
BOTH = [(0, 3), (3, 0), (1, 2), (2, 1)]


def dot(a, b, dims=NN):
    return lax.dot_general(a, b, dims, preferred_element_type=f32)


def add_low(u, v):
    return (u.astype(f32) + v.astype(f32)).astype(u.dtype)


def exchange(step):
    return [(i, i ^ step) for i in range(8)]


def halve(x, step):
    half = x.shape[0] // 2
    bit = (lax.axis_index("seq") // step) % 2
    keep = lax.dynamic_slice_in_dim(x, bit * half, half, 0)
    send = lax.dynamic_slice_in_dim(x, (1 - bit) * half, half, 0)
    return add_low(keep, lax.ppermute(send, "seq", exchange(step)))


def head_pieces(own, core, cross, both):
    return (
        own,
        lax.ppermute(core, "head", CORE),
        lax.ppermute(cross, "head", CROSS),
        lax.ppermute(both, "head", BOTH),
    )


def head_whole(x):
    p = lax.ppermute(x, "head", CROSS)
    return x, lax.ppermute(x, "head", CORE), p, lax.ppermute(p, "head", CORE)


def head_columns(got, head_pos):
    return jnp.concatenate([lax.select_n(head_pos ^ k, *got) for k in range(4)], axis=1)


SC = 6


def feature_table(total, nrow, nh, n_head):
    sizes = [nrow + total // (SEG * scale) for scale in segment_scales]
    nf = sum(sizes)
    width = -(-nh * nf // 128) * 128
    table = np.zeros((-(-(4 + n_head) // 8) * 8, width), np.int32)
    table[3] = -1
    for h in range(nh):
        lane = h * nf
        for scale, step, size in zip(segment_scales, dilation_steps, sizes):
            at = slice(lane, lane + size)
            table[0, at] = (SEG * scale).bit_length() - 1
            table[1, at] = SEG * scale - 1
            table[2, at] = lane
            table[3, at] = np.arange(lane, lane + size)
            for d in range(n_head):
                table[4 + d, at] = sum(1 << b for b in range(12) if b % step == (d * nh + h) % step)
            lane += size
    return table, nf


def feature_kernel(n, nrow, lengths, table, out, sc):
    tile = pl.program_id(0)
    bk, width = out.shape
    seq_pos, head_pos = lax.axis_index("seq"), lax.axis_index("head")
    ends, end, row_begin = [], 0, 0
    for r in range(nrow):
        end = end + lengths[r]
        ends.append(end)
        row_begin = jnp.where(end <= seq_pos * bk, end, row_begin)

    @pl.when(tile == 0)
    def _():
        sc[0] = seq_pos
        sc[1] = row_begin
        for r in range(4):
            sc[2 + r] = head_pos ^ r
        pos = sum(jnp.where(seq_pos == d, k, 0) for k, d in enumerate(RING))
        for k in range(n):
            if n == 8:
                at = (pos + (0, 7, 1, 6, 2, 5, 3, 4)[k]) & 7
                sc[SC + k] = sum(jnp.where(at == m, d, 0) for m, d in enumerate(RING))
            else:
                sc[SC + k] = k

    @pl.when((tile <= seq_pos) & ((tile + 1) * bk > row_begin))
    def _():
        shift, mask, first, own = (table[k : k + 1, :] for k in range(4))
        residues = table[pl.ds(4 + head_pos, 1), :]
        pos = tile * bk + lax.broadcasted_iota(jnp.int32, (bk, width), 0)
        begin = jnp.zeros((bk, width), jnp.int32)
        seg = jnp.broadcast_to(first, (bk, width))
        for r in range(nrow):
            past = pos >= ends[r]
            begin = jnp.where(past, ends[r], begin)
            seg = seg + jnp.where(past, (lengths[r] + mask) >> shift, 0)
        place = pos - begin
        seg = seg + (place >> shift)
        part = place & mask
        whole = ((part.astype(f32) + 0.5) * np.float32(1 / 12)).astype(jnp.int32)
        on = (residues >> (part - 12 * whole)) & 1
        out[...] = jnp.where(seg == own, on, 0).astype(f32).astype(bf16)


def features(total, lengths, nh, bk):
    n = total // bk
    nrow = lengths.shape[0]
    table, nf = feature_table(total, nrow, nh, lax.axis_size("head"))
    feats, sc = pl.pallas_call(
        functools.partial(feature_kernel, n, nrow),
        grid_spec=pltpu.PrefetchScalarGridSpec(
            num_scalar_prefetch=1,
            grid=(n,),
            in_specs=[pl.BlockSpec(table.shape, lambda i, s: (0, 0))],
            out_specs=[
                pl.BlockSpec((bk, table.shape[1]), lambda i, s: (i, 0)),
                pl.BlockSpec(memory_space=pltpu.SMEM),
            ],
        ),
        out_shape=[
            jax.ShapeDtypeStruct((total, table.shape[1]), bf16),
            jax.ShapeDtypeStruct((SC + n,), jnp.int32),
        ],
        compiler_params=pltpu.CompilerParams(dimension_semantics=("arbitrary",)),
        name="features",
    )(lengths, jnp.asarray(table))
    return feats, nf, sc


def head_pad(x, h, upper):
    part = x[:, HEAD_DIM * h : HEAD_DIM * (h + 1)]
    zero = jnp.zeros_like(part)
    return jnp.concatenate([zero, part] if upper else [part, zero], axis=1)


def count_tile(fk, fq, h, nf, first_key, first_row):
    lane = lax.broadcasted_iota(jnp.int32, fq.shape, 1)
    fqh = jnp.where((lane >= h * nf) & (lane < (h + 1) * nf), fq.astype(f32), 0.0).astype(bf16)
    count = dot(fk, fqh, NT)
    keys = first_key + lax.broadcasted_iota(jnp.int32, (count.shape[0], 1), 0)
    rows = first_row + lax.broadcasted_iota(jnp.int32, (1, count.shape[1]), 1)
    return jnp.where(keys <= rows, count, 0.0)


def fwd_tile(nh, nf, q, fq, kv, fk, first_key, first_row, acc, m, l):
    kv_t = kv[...].astype(f32).T.astype(bf16)
    qs = (q[...].astype(f32) * HEAD_DIM**-0.5).astype(bf16)
    for h in range(nh):
        s = dot(kv[:, 128 * h : 128 * h + 128], head_pad(qs, h, False), NT)
        count = count_tile(fk[...], fq[...], h, nf, first_key, first_row)
        s = jnp.where(count > 0, s, -1e30)
        old = m[h : h + 1, :]
        new = jnp.maximum(old, jnp.max(s, axis=0, keepdims=True))
        p = count * jnp.exp(s - new)
        factor = jnp.exp(old - new)
        l[h : h + 1, :] = l[h : h + 1, :] * factor + jnp.sum(p, axis=0, keepdims=True)
        o = dot(kv_t[128 * h : 128 * h + 128], p.astype(bf16))
        acc[64 * h : 64 * h + 64, :] = acc[64 * h : 64 * h + 64, :] * factor + o[64:, :]
        m[h : h + 1, :] = new


def bwd_tile(nh, nf, q, fq, do, lse, dterm, kv, fk, first_key, first_row, dq_t):
    kv_t = kv[...].astype(f32).T.astype(bf16)
    qs = (q[...].astype(f32) * HEAD_DIM**-0.5).astype(bf16)
    out = []
    for h in range(nh):
        kvh = kv[:, 128 * h : 128 * h + 128]
        qh = head_pad(qs, h, False)
        doh = head_pad(do[...], h, True)
        count = count_tile(fk[...], fq[...], h, nf, first_key, first_row)
        p = count * jnp.exp(jnp.minimum(dot(kvh, qh, NT) - lse[h : h + 1, :], 1.0))
        ds = (p * (dot(kvh, doh, NT) - dterm[h : h + 1, :])).astype(bf16)
        out.append((dot(ds, qh) + dot(p.astype(bf16), doh)).astype(bf16))
        o = dot(kv_t[128 * h : 128 * h + 128], ds)
        dq_t[64 * h : 64 * h + 64, :] += o[:64, :]
    return out


def fwd_start(acc, m, l):
    acc[...] = jnp.zeros_like(acc)
    m[...] = jnp.full_like(m, -1e30)
    l[...] = jnp.zeros_like(l)


def fwd_end(nh, quarters, acc, m, l, out, lse, msgs):
    for h in range(nh):
        out[:, 64 * h : 64 * h + 64] = (acc[64 * h : 64 * h + 64, :] / l[h : h + 1, :]).T
    lse[...] = m[...] + jnp.log(jnp.maximum(l[...], 1e-30))
    rows = msgs[0].shape[0]
    for at, msg in zip(quarters, msgs):
        msg[...] = out[pl.ds(pl.multiple_of(at * rows, rows), rows), :].astype(bf16)


def bwd_start(nh, quarters, pieces, att, do, dterm, dq_t):
    dq_t[...] = jnp.zeros_like(dq_t)
    rows = pieces[0].shape[0]
    for at, piece in zip(quarters, pieces):
        do[pl.ds(pl.multiple_of(at * rows, rows), rows), :] = piece[...]
    prod = do[...].astype(f32) * att[...]
    r = lax.broadcasted_iota(jnp.int32, (8, prod.shape[1]), 0)
    c = lax.broadcasted_iota(jnp.int32, (8, prod.shape[1]), 1)
    pick = jnp.where(c // HEAD_DIM == r, 1.0, 0.0).astype(f32)
    dterm[...] = lax.dot_general(
        pick, prod, NT, precision=lax.Precision.HIGHEST, preferred_element_type=f32
    )


def tile_needed(tile, sc, bk):
    return (tile <= sc[0]) & ((tile + 1) * bk > sc[1])


def fwd_grid(nh, nf, n, sc, q, fq, kv, fk, out, lse, m0, m1, m2, m3, acc, m, l):
    i = pl.program_id(0)
    bk = kv.shape[1]

    @pl.when(i == 0)
    def _():
        fwd_start(acc, m, l)

    @pl.when(tile_needed(sc[SC + i], sc, bk))
    def _():
        fwd_tile(nh, nf, q, fq, kv.at[0], fk, sc[SC + i] * bk, sc[0] * q.shape[0], acc, m, l)

    @pl.when(i == n - 1)
    def _():
        fwd_end(nh, [sc[2 + r] for r in range(4)], acc, m, l, out, lse, (m0, m1, m2, m3))


def bwd_grid(nh, nf, n, sc, q, fq, d0, d1, d2, d3, att, lse, kv, fk, dq, dkv, do, dterm, dq_t):
    i = pl.program_id(0)
    bk = kv.shape[1]

    @pl.when(i == 0)
    def _():
        bwd_start(nh, [sc[2 + r] for r in range(4)], (d0, d1, d2, d3), att, do, dterm, dq_t)

    need = tile_needed(sc[SC + i], sc, bk)

    @pl.when(jnp.logical_not(need))
    def _():
        dkv[...] = jnp.zeros_like(dkv)

    @pl.when(need)
    def _():
        out = bwd_tile(
            nh, nf, q, fq, do, lse, dterm, kv.at[0], fk, sc[SC + i] * bk, sc[0] * q.shape[0], dq_t
        )
        for h in range(nh):
            dkv[0, :, 128 * h : 128 * h + 128] = out[h]

    @pl.when(i == n - 1)
    def _():
        dq[...] = (dq_t[...].T * HEAD_DIM**-0.5).astype(dq.dtype)


def whole_block(*shape):
    return pl.BlockSpec(shape, lambda i, s: (0,) * len(shape))


def struct(shape, dtype):
    return jax.ShapeDtypeStruct(shape, dtype)


def params(mib=16):
    return pltpu.CompilerParams(
        dimension_semantics=("arbitrary",), vmem_limit_bytes=mib << 20
    )


def fwd_outs(tq, wd):
    return [struct((tq, wd), f32), struct((8, tq), f32)] + [struct((tq // 4, wd), bf16)] * 4


def attend_fwd(q, feats, nf, kv, sc, n):
    tq, wd = q.shape
    bk, width = kv.shape[1], feats.shape[1]
    outs = fwd_outs(tq, wd)
    return pl.pallas_call(
        functools.partial(fwd_grid, wd // HEAD_DIM, nf, n),
        grid_spec=pltpu.PrefetchScalarGridSpec(
            num_scalar_prefetch=1,
            grid=(n,),
            in_specs=[
                whole_block(tq, wd),
                pl.BlockSpec((tq, width), lambda i, s: (s[0], 0)),
                pl.BlockSpec((1, bk, 2 * wd), lambda i, s: (i, 0, 0)),
                pl.BlockSpec((bk, width), lambda i, s: (s[SC + i], 0)),
            ],
            out_specs=[whole_block(*o.shape) for o in outs],
            scratch_shapes=[
                pltpu.VMEM((wd, tq), f32),
                pltpu.VMEM((8, tq), f32),
                pltpu.VMEM((8, tq), f32),
            ],
        ),
        out_shape=outs,
        compiler_params=params(),
        name="attend_fwd",
    )(sc, q, feats, kv, feats)


def attend_bwd(q, feats, nf, pieces, att, lse, kv, sc, n):
    tq, wd = q.shape
    bk, width = kv.shape[1], feats.shape[1]
    return pl.pallas_call(
        functools.partial(bwd_grid, wd // HEAD_DIM, nf, n),
        grid_spec=pltpu.PrefetchScalarGridSpec(
            num_scalar_prefetch=1,
            grid=(n,),
            in_specs=[whole_block(tq, wd), pl.BlockSpec((tq, width), lambda i, s: (s[0], 0))]
            + [whole_block(tq // 4, wd)] * 4
            + [
                whole_block(tq, wd),
                whole_block(8, tq),
                pl.BlockSpec((1, bk, 2 * wd), lambda i, s: (i, 0, 0)),
                pl.BlockSpec((bk, width), lambda i, s: (s[SC + i], 0)),
            ],
            out_specs=[whole_block(tq, wd), pl.BlockSpec((1, bk, 2 * wd), lambda i, s: (i, 0, 0))],
            scratch_shapes=[
                pltpu.VMEM((tq, wd), bf16),
                pltpu.VMEM((8, tq), f32),
                pltpu.VMEM((wd, tq), f32),
            ],
        ),
        out_shape=[struct((tq, wd), bf16), struct(kv.shape, bf16)],
        compiler_params=params(),
        name="attend_bwd",
    )(sc, q, feats, *pieces, att, lse, kv, feats)


def fwd_part(nh, nf, tiles, bk, first, last, sc, *refs):
    q, fq = refs[:2]
    n = len(tiles)
    kvs, fks = refs[2 : 2 + n], refs[2 + n : 2 + 2 * n]
    rest = refs[2 + 2 * n :]
    if not first:
        rest = rest[3:]
    if last:
        out, lse, *msgs = rest[:6]
        acc, m, l = rest[6:9]
    else:
        acc, m, l = rest[:3]
    if first:
        fwd_start(acc, m, l)
    for (place, rows, offset), kv, fk in zip(tiles, kvs, fks):

        @pl.when(tile_needed(sc[SC + place], sc, bk))
        def _():
            fwd_tile(
                nh, nf, q, fq, kv, fk, sc[SC + place] * bk + offset, sc[0] * q.shape[0], acc, m, l
            )

    if last:
        fwd_end(nh, [sc[2 + r] for r in range(4)], acc, m, l, out, lse, msgs)


def attend_fwd_part(q, feats, nf, kvs, tiles, state, sc, last):
    tq, wd = q.shape
    width = feats.shape[1]
    n = len(tiles)
    sums = [struct((wd, tq), f32), struct((8, tq), f32), struct((8, tq), f32)]
    ins = [whole_block(tq, wd), pl.BlockSpec((tq, width), lambda i, s: (s[0], 0))]
    ins += [whole_block(*kv.shape) for kv in kvs]
    for place, rows, offset in tiles:
        at = lambda i, s, p=place, k=tq // rows, o=offset // rows: (s[SC + p] * k + o, 0)
        ins.append(pl.BlockSpec((rows, width), at))
    args = [sc, q, feats, *kvs, *([feats] * n)]
    outs = (fwd_outs(tq, wd) if last else []) + sums
    alias = {}
    if state is not None:
        ins += [whole_block(*o.shape) for o in sums]
        alias = {len(args) + k: len(outs) - 3 + k for k in range(3)}
        args += state

    def kernel(sc_ref, *refs):
        if state is not None:
            olds = refs[2 + 2 * n : 5 + 2 * n]
            news = refs[len(refs) - 3 :]
            for old, new in zip(olds, news):
                new[...] = old[...]
        fwd_part(wd // HEAD_DIM, nf, tiles, tq, state is None, last, sc_ref, *refs)

    got = pl.pallas_call(
        kernel,
        grid_spec=pltpu.PrefetchScalarGridSpec(
            num_scalar_prefetch=1,
            grid=(1,),
            in_specs=ins,
            out_specs=[whole_block(*o.shape) for o in outs],
        ),
        out_shape=outs,
        input_output_aliases=alias,
        compiler_params=params(),
        cost_estimate=pl.CostEstimate(flops=n << 31, bytes_accessed=n << 20, transcendentals=0),
        name="fwd_part",
    )(*args)
    return got[:6] if last else got


def attend_bwd_part(q, feats, nf, kvs, tiles, lse, sc, start, state, last):
    tq, wd = q.shape
    nh = wd // HEAD_DIM
    width = feats.shape[1]
    n = len(tiles)
    held = [struct((tq, wd), bf16), struct((8, tq), f32), struct((wd, tq), f32)]
    ins = [whole_block(tq, wd), pl.BlockSpec((tq, width), lambda i, s: (s[0], 0)), whole_block(8, tq)]
    ins += [whole_block(*kv.shape) for kv in kvs]
    for place, rows, offset in tiles:
        at = lambda i, s, p=place, k=tq // rows, o=offset // rows: (s[SC + p] * k + o, 0)
        ins.append(pl.BlockSpec((rows, width), at))
    args = [sc, q, feats, lse, *kvs, *([feats] * n)]
    outs = [struct(kv.shape, bf16) for kv in kvs]
    more = start if start is not None else state
    ins += [whole_block(*v.shape) for v in more]
    args += more
    if start is not None:
        outs = outs + held
    elif not last:
        outs = outs + held[2:]
    if last:
        outs = outs + [struct((tq, wd), bf16)]
    scratch = [pltpu.VMEM((wd, tq), f32)] if last else []

    def kernel(sc_ref, *refs):
        q_ref, fq, lse_ref = refs[:3]
        kv_refs, fks = refs[3 : 3 + n], refs[3 + n : 3 + 2 * n]
        given = refs[3 + 2 * n : 3 + 2 * n + len(more)]
        rest = refs[3 + 2 * n + len(more) :]
        dkvs, rest = rest[:n], rest[n:]
        if start is not None:
            do, dterm, dq_t = rest[:3]
            bwd_start(nh, [sc_ref[2 + r] for r in range(4)], given[:4], given[4], do, dterm, dq_t)
        else:
            do, dterm, old = given
            dq_t = rest[-1] if last else rest[0]
            dq_t[...] = old[...]
        for (place, rows, offset), kv, fk, dkv in zip(tiles, kv_refs, fks, dkvs):
            need = tile_needed(sc_ref[SC + place], sc_ref, tq)

            @pl.when(jnp.logical_not(need))
            def _():
                dkv[...] = jnp.zeros_like(dkv)

            @pl.when(need)
            def _():
                got = bwd_tile(
                    nh, nf, q_ref, fq, do, lse_ref, dterm, kv, fk,
                    sc_ref[SC + place] * tq + offset, sc_ref[0] * tq, dq_t,
                )
                for h in range(nh):
                    dkv[:, 128 * h : 128 * h + 128] = got[h]

        if last:
            rest[0][...] = (dq_t[...].T * HEAD_DIM**-0.5).astype(bf16)

    return pl.pallas_call(
        kernel,
        grid_spec=pltpu.PrefetchScalarGridSpec(
            num_scalar_prefetch=1,
            grid=(1,),
            in_specs=ins,
            out_specs=[whole_block(*o.shape) for o in outs],
            scratch_shapes=scratch,
        ),
        out_shape=outs,
        compiler_params=params(),
        cost_estimate=pl.CostEstimate(flops=n << 31, bytes_accessed=n << 20, transcendentals=0),
        name="bwd_part",
    )(*args)


def ring_attend(q, feats, nf, kv, sc, g, pack, head_pos):
    rows = kv.shape[0]
    half = rows // 2
    a = b = kv
    tiles, state = [kv], None
    whole = lambda p: (p, rows, 0)
    part = functools.partial(attend_fwd_part, q, feats, nf)
    for step in range(3):
        a2, b2 = lax.ppermute(a, "seq", FWD), lax.ppermute(b, "seq", BWD)
        if step == 0:
            state = part([kv], [whole(0)], None, sc, False)
        else:
            state = part([a, b], [whole(2 * step - 1), whole(2 * step)], state, sc, False)
        a, b, state = lax.optimization_barrier((a2, b2, state))
        if step == 0:
            a, b, g, pack = lax.optimization_barrier((a, b, g, pack))
            far_g, far_pack = (lax.ppermute(v, "head", CROSS) for v in (g, pack))
        if step == 2:
            a, b, far_g, far_pack = lax.optimization_barrier((a, b, far_g, far_pack))
            gs, packs = (
                [v, lax.ppermute(v, "head", CORE), w, lax.ppermute(w, "head", CORE)]
                for v, w in ((g, far_g), (pack, far_pack))
            )
        tiles += [a, b]
    c, d = lax.ppermute(a[:half], "seq", FWD), lax.ppermute(b[half:], "seq", BWD)
    g = head_columns(gs, head_pos)
    state = part([a, b], [whole(5), whole(6)], state, sc, False)
    tiles += [c, d]
    c, d, g, state = lax.optimization_barrier((c, d, g, state))
    return part([c, d], [(7, half, 0), (7, half, half)], state, sc, True), tiles, g, packs


def ring_attend_back(q, feats, nf, tiles, pieces, att, lse, sc, beside):
    rows = tiles[0].shape[0]
    half = rows // 2
    whole = lambda p: (p, rows, 0)
    part = functools.partial(attend_bwd_part, q, feats, nf)
    c, d, do, dterm, dq_t = part(
        tiles[7:9], [(7, half, 0), (7, half, half)], lse, sc, [*pieces, att], None, False
    )
    c, d, dq_t = lax.optimization_barrier((c, d, dq_t))
    a, b = lax.ppermute(c, "seq", FWD), lax.ppermute(d, "seq", BWD)
    for place in (5, 3, 1):
        given, at = tiles[place : place + 2], [whole(place), whole(place + 1)]
        if place == 3:
            t, u, own, dq_t = part(
                given + tiles[:1], at + [whole(0)], lse, sc, None, [do, dterm, dq_t], False
            )
        elif place == 5:
            t, u, dq_t = part(given, at, lse, sc, None, [do, dterm, dq_t], False)
        else:
            t, u, dq = part(given, at, lse, sc, None, [do, dterm, dq_t], True)
        if place == 5:
            up = jnp.concatenate([add_low(u[:half], a), u[half:]], axis=0)
            down = jnp.concatenate([t[:half], add_low(t[half:], b)], axis=0)
        else:
            up, down = add_low(u, a), add_low(t, b)
        if place == 3:
            up, down, dq_t, beside = lax.optimization_barrier((up, down, dq_t, beside))
        elif place == 5:
            up, down, dq_t = lax.optimization_barrier((up, down, dq_t))
        a, b = lax.ppermute(up, "seq", FWD), lax.ppermute(down, "seq", BWD)
    return dq, (own.astype(f32) + a.astype(f32) + b.astype(f32)).astype(bf16), beside


VEC_ROWS = 16


def out_pack(w_out, sub_gain, sub_bias):
    width = w_out.shape[1]
    share = sub_gain.shape[0]
    room = width // 3
    pad = lambda v: jnp.concatenate([v, jnp.zeros((room - share,), f32)])
    vec = jnp.concatenate([pad(sub_gain), pad(sub_bias), jnp.zeros((room,), f32)]).reshape(1, width)
    high = vec.astype(bf16)
    rest = vec - lax.optimization_barrier(high).astype(f32)
    middle = rest.astype(bf16)
    low = (rest - lax.optimization_barrier(middle).astype(f32)).astype(bf16)
    top = jnp.concatenate([high, middle, low, jnp.zeros((VEC_ROWS - 3, width), bf16)], axis=0)
    return jnp.concatenate([top, w_out], axis=0)


def unpack_vec(w, row):
    v = w[0:VEC_ROWS, :].astype(f32)
    return v[row : row + 1] + v[row + 1 : row + 2] + v[row + 2 : row + 3]


def sub_parts(pieces, width):
    total = sum(jnp.sum(p, axis=1, keepdims=True) for p in pieces)
    square = sum(jnp.sum(p * p, axis=1, keepdims=True) for p in pieces)
    mean = total / width
    inv = lax.rsqrt(square / width - mean * mean + eps)
    return [(p - mean) * inv for p in pieces], inv


def norm_parts(x):
    center = x - jnp.mean(x, axis=1, keepdims=True)
    rs = lax.rsqrt(jnp.mean(center * center, axis=1, keepdims=True) + eps)
    return center * rs, rs


def norm_back(g, hat, rs):
    return rs * (
        g - jnp.mean(g, axis=1, keepdims=True) - hat * jnp.mean(g * hat, axis=1, keepdims=True)
    )


def mid1_kernel(sc, p0, p1, p2, p3, w0, w1, w2, w3, x, b_out, gain2, bias2, nm, middle, sub):
    share = p0.shape[1]
    room = w0.shape[1] // 3
    cen, _ = sub_parts([p[...].astype(f32) for p in (p0, p1, p2, p3)], w0.shape[1])
    acc = x[...].astype(f32) + b_out[...]
    for r, w in enumerate((w0, w1, w2, w3)):
        vec = unpack_vec(w, 0)
        s = (cen[r] * vec[:, :share] + vec[:, room : room + share]).astype(bf16)
        sub[r] = s
        acc = acc + dot(s, w[VEC_ROWS : VEC_ROWS + share, :])
    middle[...] = acc
    hat, _ = norm_parts(acc)
    nm[...] = (hat * gain2[...] + bias2[...]).astype(bf16)


def gelu_parts(z):
    half = 0.5 * (1.0 + lax.erf(z * np.float32(np.sqrt(0.5))))
    slope = half + z * (np.float32(1.0 / np.sqrt(2.0 * np.pi)) * jnp.exp(-0.5 * z * z))
    return z * half, slope


def ffn_kernel(pair, sc, n0, n1, g, w_up, w_down, b_up, *refs):
    nm, act, d_inner, *outs = refs[len(refs) - 7 :]
    rows = n0.shape[0]
    for k, piece in enumerate((n0, n1)):
        quarter = sc[2 * pair + k]
        at = pl.ds(pl.multiple_of((quarter & 1) * rows, rows), rows)
        x = piece[...]
        nm[at, :] = x
        a, slope = gelu_parts(dot(x, w_up[...]) + b_up[...])
        a = a.astype(bf16)
        g_rows = g[pl.ds(pl.multiple_of(quarter * rows, rows), rows), :]
        d = (dot(g_rows, w_down[...], NT) * slope).astype(bf16)
        act[at, :] = a
        d_inner[at, :] = d
        outs[k][...] = dot(a, w_down[...]).astype(bf16)
        outs[2 + k][...] = dot(d, w_up[...], NT).astype(bf16)


def mid2_kernel(sc, p0, p1, p2, p3, w0, w1, w2, w3, middle, g, gain2, t0, t1, t2, t3, *refs):
    d_mid, dbr, d0, d1, d2, d3, vec768, vec192 = refs
    share = p0.shape[1]
    width = w0.shape[1]
    dn = sum(t[...].astype(f32) for t in (t0, t1, t2, t3))
    hat, rs = norm_parts(middle[...])
    vec768[0:1, :] = jnp.sum(dn * hat, axis=0, keepdims=True)
    vec768[1:2, :] = jnp.sum(dn, axis=0, keepdims=True)
    dm = g[...].astype(f32) + norm_back(dn * gain2[...], hat, rs)
    d_mid[...] = dm
    branch = dm.astype(bf16)
    dbr[...] = branch
    cen, inv = sub_parts([p[...].astype(f32) for p in (p0, p1, p2, p3)], width)
    hats = []
    for r, w in enumerate((w0, w1, w2, w3)):
        ds = dot(branch, w[VEC_ROWS : VEC_ROWS + share, :], NT)
        vec192[r : r + 1, :] = jnp.sum(ds * cen[r], axis=0, keepdims=True)
        vec192[r + 4 : r + 5, :] = jnp.sum(ds, axis=0, keepdims=True)
        hats.append(ds * unpack_vec(w, 0)[:, :share])
    s1 = sum(jnp.sum(t, axis=1, keepdims=True) for t in hats) / width
    s2 = sum(jnp.sum(t * c, axis=1, keepdims=True) for t, c in zip(hats, cen)) / width
    for o, t, c in zip((d0, d1, d2, d3), hats, cen):
        o[...] = (inv * (t - s1 - c * s2)).astype(bf16)


def one_step(kernel, ins, in_specs, outs, name, flops, scratch=()):
    return pl.pallas_call(
        kernel,
        grid_spec=pltpu.PrefetchScalarGridSpec(
            num_scalar_prefetch=1,
            grid=(1,),
            in_specs=in_specs,
            out_specs=[whole_block(*o.shape) for o in outs],
            scratch_shapes=scratch,
        ),
        out_shape=outs,
        compiler_params=params(),
        cost_estimate=pl.CostEstimate(flops=flops, bytes_accessed=12 << 20, transcendentals=0),
        name=name,
    )(*ins)


def mid1(head_no, pieces, packs, x, b_out, gain2, bias2):
    quarter, share = pieces[0].shape
    rows, width = packs[0].shape
    at_quarter = pl.BlockSpec((quarter, width), lambda i, s: (s[0], 0))
    return one_step(
        mid1_kernel,
        (head_no, *pieces, *packs, x, b_out, gain2, bias2),
        [whole_block(quarter, share)] * 4
        + [whole_block(rows, width)] * 4
        + [at_quarter]
        + [whole_block(1, width)] * 3,
        [struct((quarter, width), bf16), struct((quarter, width), f32), struct((4, quarter, share), bf16)],
        "mid1",
        2 * quarter * width * width,
    )


def ffn(head_no, pair, pieces, g, w_up, w_down, b_up, held):
    quarter, width = pieces[0].shape
    hidden = w_up.shape[1]
    ins = (head_no, *pieces, g, w_up, w_down, b_up)
    specs = [whole_block(*v.shape) for v in ins[1:]]
    outs = [struct((4 * quarter, k), bf16) for k in (width, hidden, hidden)]
    outs += [struct((quarter, width), bf16)] * 4
    at_chip = lambda k: pl.BlockSpec((2 * quarter, k), lambda i, s: (s[2 * pair] // 2, 0))
    return pl.pallas_call(
        functools.partial(ffn_kernel, pair),
        grid_spec=pltpu.PrefetchScalarGridSpec(
            num_scalar_prefetch=1,
            grid=(1,),
            in_specs=specs + [pl.BlockSpec(memory_space=pl.ANY)] * len(held),
            out_specs=[at_chip(o.shape[1]) for o in outs[:3]] + [whole_block(quarter, width)] * 4,
        ),
        out_shape=outs,
        input_output_aliases={len(ins) + k: k for k in range(len(held))},
        compiler_params=params(),
        cost_estimate=pl.CostEstimate(
            flops=16 * quarter * width * hidden, bytes_accessed=8 << 20, transcendentals=0
        ),
        name="ffn",
    )(*ins, *held)


def mid2(head_no, pieces, packs, middle, g, gain2, terms):
    quarter, share = pieces[0].shape
    rows, width = packs[0].shape
    at_quarter = pl.BlockSpec((quarter, width), lambda i, s: (s[0], 0))
    return one_step(
        mid2_kernel,
        (head_no, *pieces, *packs, middle, g, gain2, *terms),
        [whole_block(quarter, share)] * 4
        + [whole_block(rows, width)] * 4
        + [whole_block(quarter, width), at_quarter, whole_block(1, width)]
        + [whole_block(*t.shape) for t in terms],
        [struct((quarter, width), f32), struct((quarter, width), bf16)]
        + [struct((quarter, share), bf16)] * 4
        + [struct((8, width), f32), struct((8, share), f32)],
        "mid2",
        2 * quarter * width * width,
    )


def spread_kernel(sc, *refs):
    tiles, (gq, gk, gv, go, gu, gd) = refs[:9], refs[9:]
    rows = tiles[0].shape[0] // 3

    def put(out, at, value):
        out[pl.ds(pl.multiple_of(at, 8), value.shape[0]), :] = value.astype(f32)

    for k in range(8):
        d = sc[SC + k]
        at = d * rows
        which = (d & 1) * 2 + ((d >> 1) & 1)
        for m, out in enumerate((gq, gk, gv, go)):

            @pl.when(which == m)
            def _():
                put(out, (d >> 2) * rows, tiles[k][:rows])

        if k < 7:
            put(gu, at, tiles[k][rows : 2 * rows])
            put(gd, at, tiles[k][2 * rows :])
        else:
            half = rows // 2
            put(gu, at, tiles[7][rows:])
            put(gu, at + half, tiles[8][:half])
            put(gd, at, tiles[8][half:])


def spread(sc, tiles, hidden):
    width = tiles[0].shape[1]
    share = width // 4
    outs = [struct((share, width), f32)] * 4 + [
        struct((width, hidden), f32),
        struct((hidden, width), f32),
    ]
    return one_step(
        spread_kernel,
        (sc, *tiles),
        [whole_block(*t.shape) for t in tiles],
        outs,
        "spread",
        1 << 30,
    )


def shards(
    layer_input, ln1_gain, ln1_bias, w_query, b_query, w_key, w_value, b_value, sub_gain, sub_bias,
    w_out, b_out, ln2_gain, ln2_bias, w_up, b_up, w_down, b_down, cotangent, row_lengths,
):
    rows_local, slice_width = layer_input.shape
    head_share = w_query.shape[1]
    local_heads = head_share // HEAD_DIM
    head_pos = lax.axis_index("head")
    seq_pos = lax.axis_index("seq")
    n_seq = lax.axis_size("seq")
    width = head_share * lax.axis_size("head")
    quarter = rows_local // 4
    relative = jnp.stack([head_pos, head_pos ^ 1, head_pos ^ 2, head_pos ^ 3]).astype(jnp.int32)
    row2 = lambda v: v.reshape(1, -1)

    pack = out_pack(w_out, sub_gain, sub_bias)
    input_whole = lax.all_gather(layer_input, "head", axis=1, tiled=True)
    hat1, rs1 = norm_parts(input_whole.astype(f32))
    normed = (hat1 * ln1_gain + ln1_bias).astype(bf16)
    pair = lambda a, b: jnp.stack(
        [a.reshape(-1, local_heads, HEAD_DIM), b.reshape(-1, local_heads, HEAD_DIM)], axis=2
    ).reshape(-1, 2 * head_share)
    w_kv = pair(w_key, w_value)
    b_kv = pair(jnp.zeros_like(b_value), b_value)
    kv = (dot(normed, w_kv) + b_kv).astype(bf16)
    queries = (dot(normed, w_query) + b_query).astype(bf16)

    feats, nf, sc = features(rows_local * n_seq, row_lengths, local_heads, rows_local)
    kv, cotangent, pack = lax.optimization_barrier((kv, cotangent, pack))
    if n_seq == 8:
        (att, lse, *msgs), kv_tiles, g_whole, packs = ring_attend(
            queries, feats, nf, kv, sc, cotangent, pack, head_pos
        )
    else:
        kv_tiles = lax.all_gather(kv, "seq", axis=0)
        att, lse, *msgs = attend_fwd(queries, feats, nf, kv_tiles, sc, n_seq)
        g_whole, packs = head_columns(head_whole(cotangent), head_pos), head_whole(pack)

    pieces = head_pieces(*msgs)
    nm, middle, sub = mid1(
        relative, pieces, packs, input_whole, row2(b_out), row2(ln2_gain), row2(ln2_bias)
    )
    nms = head_pieces(nm, nm, nm, nm)
    *held, out0, out1, dn0, dn1 = ffn(
        relative, 0, nms[:2], g_whole, w_up, w_down, row2(b_up), []
    )
    nm_all, act, d_inner, out2, out3, dn2, dn3 = ffn(
        relative, 1, nms[2:], g_whole, w_up, w_down, row2(b_up), held
    )
    outs, dn = (out0, out1, out2, out3), head_pieces(dn0, dn1, dn2, dn3)
    gw_up = dot(nm_all, d_inner, TN).astype(bf16)
    gw_down = dot(act, g_whole, TN).astype(bf16)
    early = jnp.concatenate([v.reshape(8, -1, v.shape[1]) for v in (gw_up, gw_down)], axis=1)
    early = early.reshape(-1, early.shape[2])
    if n_seq == 8:
        early = lax.psum_scatter(early, "seq", scatter_dimension=0, tiled=True)
    d_mid, dbr, *d_msgs, vec768, vec192 = mid2(
        relative, pieces, packs, middle, g_whole, row2(ln2_gain), dn
    )
    d_pieces = head_pieces(*d_msgs)
    d_pieces, outs, dbr, sub, vec768, vec192, d_inner = lax.optimization_barrier(
        (d_pieces, outs, dbr, sub, vec768, vec192, d_inner)
    )
    dbr_all = jnp.concatenate(head_pieces(dbr, dbr, dbr, dbr), axis=0)
    sub_all = jnp.concatenate(head_pieces(*[sub[r] for r in range(4)]), axis=0)
    beside = (dbr_all, sub_all, vec768, vec192, d_inner)

    if n_seq == 8:
        dq, dkv, beside = ring_attend_back(
            queries, feats, nf, kv_tiles, d_pieces, att, lse, sc, beside
        )
    else:
        dq, dkv_tiles = attend_bwd(queries, feats, nf, d_pieces, att, lse, kv_tiles, sc, n_seq)
        dkv = lax.psum_scatter(dkv_tiles, "seq", scatter_dimension=0, tiled=False)
        early = lax.psum(early, "seq")
    dbr_all, sub_all, vec768, vec192, d_inner = beside

    gw_out = dot(sub_all, dbr_all, TN).astype(bf16)
    gw_query = dot(dq, normed, TN).astype(bf16)
    gb_out = jnp.sum(dbr_all.astype(f32), axis=0)
    gb_up = jnp.sum(d_inner.astype(f32), axis=0)
    gb_down = jnp.sum(g_whole.astype(f32), axis=0)
    gw_kv = dot(dkv, normed, TN).astype(bf16).reshape(local_heads, 2, HEAD_DIM, width)
    gw_kv = jnp.concatenate([gw_kv[:, k].reshape(head_share, width) for k in range(2)], axis=0)
    late = jnp.concatenate([gw_query, gw_kv, gw_out], axis=0)
    late, dkv = lax.optimization_barrier((late, dkv))
    dn = dot(dq, w_query, NT) + dot(dkv, w_kv, NT)
    gb_kv = jnp.sum(dkv.astype(f32), axis=0)
    gb_qkv = jnp.concatenate([jnp.sum(dq.astype(f32), axis=0), gb_kv])
    split = lambda v: jnp.sum(
        jnp.where(relative[:, None, None] == jnp.arange(4)[None, :, None], v[:, None, :], 0.0), axis=0
    ).reshape(-1)
    fill = lambda v: jnp.concatenate([v, jnp.zeros((width - v.shape[0],), f32)])
    small = jnp.stack(
        [
            jnp.sum(dn * hat1, axis=0),
            jnp.sum(dn, axis=0),
            vec768[0],
            vec768[1],
            split(vec192[:4]),
            split(vec192[4:]),
        ]
    )
    more = jnp.stack([gb_up, gb_down, gb_out, fill(gb_qkv)])
    dn = dn.astype(bf16).reshape(2, 2, quarter, width)
    core, chip = head_pos % 2, head_pos // 2
    mine = lax.dynamic_index_in_dim(dn, core, 1, False)
    mate = lax.dynamic_index_in_dim(dn, 1 - core, 1, False)
    hold = lax.optimization_barrier

    if n_seq == 8:
        late = halve(late, 1)
        late, small, mine, mate = hold((late, small, mine, mate))
        mate = lax.ppermute(mate, "head", CORE)
        late = halve(late, 2)
        mine = add_low(mine, mate)
        late, mine, small = hold((late, mine, small))
        far = lax.ppermute(lax.dynamic_index_in_dim(mine, 1 - chip, 0, False), "head", CROSS)
        late = halve(late, 4)
        a = b = jnp.concatenate([late, early], axis=0)
        tiles = [a]
        half = a.shape[0] // 2
        for step in range(3):
            a, b, outs, small, more = hold((a, b, outs, small, more))
            a, b = lax.ppermute(a, "seq", FWD), lax.ppermute(b, "seq", BWD)
            if step == 0:
                small = small + lax.ppermute(small, "head", CORE)
                small = small + lax.ppermute(small, "head", CROSS)
            elif step == 1:
                outs = head_pieces(*outs)
                small = jnp.concatenate([small, more], axis=0)
                small = small + lax.ppermute(small, "seq", exchange(1))
            else:
                small = small + lax.ppermute(small, "seq", exchange(2))
            tiles += [a, b]
        a, b, small = hold((a, b, small))
        tiles += [lax.ppermute(a[:half], "seq", FWD), lax.ppermute(b[half:], "seq", BWD)]
        small = small + lax.ppermute(small, "seq", exchange(4))
        gw_query, gw_key, gw_value, gw_out, gw_up, gw_down = spread(sc, tiles, w_up.shape[1])
    else:
        mine = add_low(mine, lax.ppermute(mate, "head", CORE))
        far = lax.ppermute(lax.dynamic_index_in_dim(mine, 1 - chip, 0, False), "head", CROSS)
        small = small + lax.ppermute(small, "head", CORE)
        small = small + lax.ppermute(small, "head", CROSS)
        small = lax.psum(jnp.concatenate([small, more], axis=0), "seq")
        outs = head_pieces(*outs)
        late = lax.psum(late, "seq").astype(f32)
        gw_query, gw_key, gw_value, gw_out = (
            late[k * head_share : (k + 1) * head_share] for k in range(4)
        )
        early = early.astype(f32).reshape(8, 2, -1, width)
        gw_up, gw_down = early[:, 0].reshape(-1, width), early[:, 1].reshape(-1, width)

    y = middle + (sum(t.astype(f32) for t in outs) + b_down)
    dn = lax.dynamic_index_in_dim(mine, chip, 0, False).astype(f32) + far.astype(f32)
    cut = lambda v: lax.dynamic_slice_in_dim(v, head_pos * quarter, quarter, 0)
    d_in = d_mid + norm_back(dn * ln1_gain, cut(hat1), cut(rs1))
    both = lax.all_to_all(jnp.stack([y, d_in]).astype(bf16), "head", 2, 1, tiled=True)
    layer_output, grad_input = both[0], both[1].astype(f32)

    gb_qkv = small[9]
    own = lambda v: lax.dynamic_slice_in_dim(v, head_pos * head_share, head_share, 0)
    gb_value = gb_qkv[head_share : 3 * head_share].reshape(local_heads, 2, HEAD_DIM)[:, 1].reshape(-1)
    return (
        layer_output,
        grad_input,
        small[0],
        small[1],
        gw_query.T,
        gb_qkv[:head_share],
        gw_key.T,
        gw_value.T,
        gb_value,
        own(small[4]),
        own(small[5]),
        gw_out,
        small[8],
        small[2],
        small[3],
        gw_up,
        small[6],
        gw_down,
        small[7],
    )


def solution(mesh):
    cols, rows, both, shared, vec = P(None, "head"), P("head", None), P("seq", "head"), P(), P("head")
    in_specs = (
        both, shared, shared, cols, vec, cols, cols, vec, vec, vec,
        rows, shared, shared, shared, cols, vec, rows, shared, both, shared,
    )
    out_specs = (
        both, both, shared, shared, cols, vec, cols, cols, vec, vec,
        vec, rows, shared, shared, shared, cols, vec, rows, shared,
    )
    return jax.shard_map(shards, mesh=mesh, in_specs=in_specs, out_specs=out_specs, check_vma=False)
```

```python
import functools

import jax
import jax.numpy as jnp
import numpy as np
from jax import lax
from jax.experimental import pallas as pl
from jax.experimental.pallas import tpu as pltpu
from jax.sharding import PartitionSpec as P

HEAD_DIM = 64
SEG = 2048
eps = 1e-05
segment_scales = (1, 2, 4, 8, 16)
dilation_steps = (1, 2, 4, 6, 12)
bf16 = jnp.bfloat16
f32 = jnp.float32
NT = (((1,), (1,)), ((), ()))
NN = (((1,), (0,)), ((), ()))
TN = (((0,), (0,)), ((), ()))

RING = (0, 2, 4, 6, 7, 5, 3, 1)
FWD = [(RING[i], RING[(i + 1) % 8]) for i in range(8)]
BWD = [(b, a) for a, b in FWD]
CORE = [(0, 1), (1, 0), (2, 3), (3, 2)]
CROSS = [(0, 2), (2, 0), (1, 3), (3, 1)]
BOTH = [(0, 3), (3, 0), (1, 2), (2, 1)]


def dot(a, b, dims=NN):
    return lax.dot_general(a, b, dims, preferred_element_type=f32)


def add_low(u, v):
    return (u.astype(f32) + v.astype(f32)).astype(u.dtype)


def exchange(step):
    return [(i, i ^ step) for i in range(8)]


def halve(x, step):
    half = x.shape[0] // 2
    bit = (lax.axis_index("seq") // step) % 2
    keep = lax.dynamic_slice_in_dim(x, bit * half, half, 0)
    send = lax.dynamic_slice_in_dim(x, (1 - bit) * half, half, 0)
    return add_low(keep, lax.ppermute(send, "seq", exchange(step)))


def head_pieces(own, core, cross, both):
    return (
        own,
        lax.ppermute(core, "head", CORE),
        lax.ppermute(cross, "head", CROSS),
        lax.ppermute(both, "head", BOTH),
    )


def head_whole(x):
    p = lax.ppermute(x, "head", CROSS)
    return x, lax.ppermute(x, "head", CORE), p, lax.ppermute(p, "head", CORE)


def head_columns(got, head_pos):
    return jnp.concatenate([lax.select_n(head_pos ^ k, *got) for k in range(4)], axis=1)


SC = 6


def feature_table(total, nrow, nh, n_head):
    sizes = [nrow + total // (SEG * scale) for scale in segment_scales]
    nf = sum(sizes)
    width = -(-nh * nf // 128) * 128
    table = np.zeros((-(-(4 + n_head) // 8) * 8, width), np.int32)
    table[3] = -1
    for h in range(nh):
        lane = h * nf
        for scale, step, size in zip(segment_scales, dilation_steps, sizes):
            at = slice(lane, lane + size)
            table[0, at] = (SEG * scale).bit_length() - 1
            table[1, at] = SEG * scale - 1
            table[2, at] = lane
            table[3, at] = np.arange(lane, lane + size)
            for d in range(n_head):
                table[4 + d, at] = sum(1 << b for b in range(12) if b % step == (d * nh + h) % step)
            lane += size
    return table, nf


def feature_kernel(n, nrow, bk, lengths, table, out, sc, seg_ref, place_ref):
    block = pl.program_id(0)
    width = out.shape[1]
    seq_pos, head_pos = lax.axis_index("seq"), lax.axis_index("head")
    ends, end, row_begin = [], 0, 0
    for r in range(nrow):
        end = end + lengths[r]
        ends.append(end)
        row_begin = jnp.where(end <= seq_pos * bk, end, row_begin)

    @pl.when(block == 0)
    def _():
        sc[0] = seq_pos
        sc[1] = row_begin
        for r in range(4):
            sc[2 + r] = head_pos ^ r
        pos = sum(jnp.where(seq_pos == d, k, 0) for k, d in enumerate(RING))
        for k in range(n):
            if n == 8:
                at = (pos + (0, 7, 1, 6, 2, 5, 3, 4)[k]) & 7
                sc[SC + k] = sum(jnp.where(at == m, d, 0) for m, d in enumerate(RING))
            else:
                sc[SC + k] = k

    shift, mask, first, own = (table[k : k + 1, :] for k in range(4))
    residues = table[pl.ds(4 + head_pos, 1), :]
    pieces = [(lengths[r] + mask) >> shift for r in range(nrow)]

    def one(k, carry):
        tile = block * (out.shape[0] // bk) + k

        @pl.when((tile <= seq_pos) & ((tile + 1) * bk > row_begin))
        def _():
            pos = tile * bk + lax.broadcasted_iota(jnp.int32, (bk, width), 0)
            start, base = 0, first
            for r in range(nrow):
                passed = ends[r] <= tile * bk
                start = jnp.where(passed, ends[r], start)
                base = base + jnp.where(passed, pieces[r], 0)
            seg_ref[...] = jnp.broadcast_to(base, (bk, width))
            place_ref[...] = pos - start
            for r in range(nrow):

                @pl.when((ends[r] > tile * bk) & (ends[r] < (tile + 1) * bk))
                def _():
                    past = pos >= ends[r]
                    place_ref[...] = jnp.where(past, pos - ends[r], place_ref[...])
                    seg_ref[...] += jnp.where(past, pieces[r], 0)

            place = place_ref[...]
            seg = seg_ref[...] + (place >> shift)
            part = place & mask
            whole = ((part.astype(f32) + 0.5) * np.float32(1 / 12)).astype(jnp.int32)
            on = (residues >> (part - 12 * whole)) & 1
            out[pl.ds(pl.multiple_of(k * bk, bk), bk), :] = (
                jnp.where(seg == own, on, 0).astype(f32).astype(bf16)
            )

        return carry

    lax.fori_loop(0, out.shape[0] // bk, one, 0)


def features(total, lengths, nh, bk):
    n = total // bk
    nrow = lengths.shape[0]
    table, nf = feature_table(total, nrow, nh, lax.axis_size("head"))
    width = table.shape[1]
    block = 8 * bk if n % 8 == 0 else bk
    feats, sc = pl.pallas_call(
        functools.partial(feature_kernel, n, nrow, bk),
        grid_spec=pltpu.PrefetchScalarGridSpec(
            num_scalar_prefetch=1,
            grid=(total // block,),
            in_specs=[pl.BlockSpec(table.shape, lambda i, s: (0, 0))],
            out_specs=[
                pl.BlockSpec((block, width), lambda i, s: (i, 0)),
                pl.BlockSpec(memory_space=pltpu.SMEM),
            ],
            scratch_shapes=[pltpu.VMEM((bk, width), jnp.int32)] * 2,
        ),
        out_shape=[
            jax.ShapeDtypeStruct((total, width), bf16),
            jax.ShapeDtypeStruct((SC + n,), jnp.int32),
        ],
        compiler_params=pltpu.CompilerParams(
            dimension_semantics=("arbitrary",), vmem_limit_bytes=16 << 20
        ),
        name="features",
    )(lengths, jnp.asarray(table))
    return feats, nf, sc


def head_pad(x, h, upper):
    part = x[:, HEAD_DIM * h : HEAD_DIM * (h + 1)]
    zero = jnp.zeros_like(part)
    return jnp.concatenate([zero, part] if upper else [part, zero], axis=1)


def count_tile(fk, fq, h, nf, first_key, first_row):
    lane = lax.broadcasted_iota(jnp.int32, fq.shape, 1)
    fqh = jnp.where((lane >= h * nf) & (lane < (h + 1) * nf), fq.astype(f32), 0.0).astype(bf16)
    count = dot(fk, fqh, NT)
    keys = first_key + lax.broadcasted_iota(jnp.int32, (count.shape[0], 1), 0)
    rows = first_row + lax.broadcasted_iota(jnp.int32, (1, count.shape[1]), 1)
    return jnp.where(keys <= rows, count, 0.0)


def fwd_tile(nh, nf, q, fq, kv, fk, first_key, first_row, acc, m, l):
    kv_t = kv[...].astype(f32).T.astype(bf16)
    qs = (q[...].astype(f32) * HEAD_DIM**-0.5).astype(bf16)
    for h in range(nh):
        s = dot(kv[:, 128 * h : 128 * h + 128], head_pad(qs, h, False), NT)
        count = count_tile(fk[...], fq[...], h, nf, first_key, first_row)
        s = jnp.where(count > 0, s, -1e30)
        old = m[h : h + 1, :]
        new = jnp.maximum(old, jnp.max(s, axis=0, keepdims=True))
        p = count * jnp.exp(s - new)
        factor = jnp.exp(old - new)
        l[h : h + 1, :] = l[h : h + 1, :] * factor + jnp.sum(p, axis=0, keepdims=True)
        o = dot(kv_t[128 * h : 128 * h + 128], p.astype(bf16))
        acc[64 * h : 64 * h + 64, :] = acc[64 * h : 64 * h + 64, :] * factor + o[64:, :]
        m[h : h + 1, :] = new


def bwd_tile(nh, nf, q, fq, do, lse, dterm, kv, fk, first_key, first_row, dq_t):
    kv_t = kv[...].astype(f32).T.astype(bf16)
    qs = (q[...].astype(f32) * HEAD_DIM**-0.5).astype(bf16)
    out = []
    for h in range(nh):
        kvh = kv[:, 128 * h : 128 * h + 128]
        qh = head_pad(qs, h, False)
        doh = head_pad(do[...], h, True)
        count = count_tile(fk[...], fq[...], h, nf, first_key, first_row)
        p = count * jnp.exp(jnp.minimum(dot(kvh, qh, NT) - lse[h : h + 1, :], 1.0))
        ds = (p * (dot(kvh, doh, NT) - dterm[h : h + 1, :])).astype(bf16)
        out.append((dot(ds, qh) + dot(p.astype(bf16), doh)).astype(bf16))
        o = dot(kv_t[128 * h : 128 * h + 128], ds)
        dq_t[64 * h : 64 * h + 64, :] += o[:64, :]
    return out


def fwd_start(acc, m, l):
    acc[...] = jnp.zeros_like(acc)
    m[...] = jnp.full_like(m, -1e30)
    l[...] = jnp.zeros_like(l)


def fwd_end(nh, quarters, acc, m, l, out, lse, msgs):
    for h in range(nh):
        out[:, 64 * h : 64 * h + 64] = (acc[64 * h : 64 * h + 64, :] / l[h : h + 1, :]).T
    lse[...] = m[...] + jnp.log(jnp.maximum(l[...], 1e-30))
    rows = msgs[0].shape[0]
    for at, msg in zip(quarters, msgs):
        msg[...] = out[pl.ds(pl.multiple_of(at * rows, rows), rows), :].astype(bf16)


def bwd_start(nh, quarters, pieces, att, do, dterm, dq_t):
    dq_t[...] = jnp.zeros_like(dq_t)
    rows = pieces[0].shape[0]
    for at, piece in zip(quarters, pieces):
        do[pl.ds(pl.multiple_of(at * rows, rows), rows), :] = piece[...]
    prod = do[...].astype(f32) * att[...]
    r = lax.broadcasted_iota(jnp.int32, (8, prod.shape[1]), 0)
    c = lax.broadcasted_iota(jnp.int32, (8, prod.shape[1]), 1)
    pick = jnp.where(c // HEAD_DIM == r, 1.0, 0.0).astype(f32)
    dterm[...] = lax.dot_general(
        pick, prod, NT, precision=lax.Precision.HIGHEST, preferred_element_type=f32
    )


def tile_needed(tile, sc, bk):
    return (tile <= sc[0]) & ((tile + 1) * bk > sc[1])


def fwd_grid(nh, nf, n, sc, q, fq, kv, fk, out, lse, m0, m1, m2, m3, acc, m, l):
    i = pl.program_id(0)
    bk = kv.shape[1]

    @pl.when(i == 0)
    def _():
        fwd_start(acc, m, l)

    @pl.when(tile_needed(sc[SC + i], sc, bk))
    def _():
        fwd_tile(nh, nf, q, fq, kv.at[0], fk, sc[SC + i] * bk, sc[0] * q.shape[0], acc, m, l)

    @pl.when(i == n - 1)
    def _():
        fwd_end(nh, [sc[2 + r] for r in range(4)], acc, m, l, out, lse, (m0, m1, m2, m3))


def bwd_grid(nh, nf, n, sc, q, fq, d0, d1, d2, d3, att, lse, kv, fk, dq, dkv, do, dterm, dq_t):
    i = pl.program_id(0)
    bk = kv.shape[1]

    @pl.when(i == 0)
    def _():
        bwd_start(nh, [sc[2 + r] for r in range(4)], (d0, d1, d2, d3), att, do, dterm, dq_t)

    need = tile_needed(sc[SC + i], sc, bk)

    @pl.when(jnp.logical_not(need))
    def _():
        dkv[...] = jnp.zeros_like(dkv)

    @pl.when(need)
    def _():
        out = bwd_tile(
            nh, nf, q, fq, do, lse, dterm, kv.at[0], fk, sc[SC + i] * bk, sc[0] * q.shape[0], dq_t
        )
        for h in range(nh):
            dkv[0, :, 128 * h : 128 * h + 128] = out[h]

    @pl.when(i == n - 1)
    def _():
        dq[...] = (dq_t[...].T * HEAD_DIM**-0.5).astype(dq.dtype)


def whole_block(*shape):
    return pl.BlockSpec(shape, lambda i, s: (0,) * len(shape))


def struct(shape, dtype):
    return jax.ShapeDtypeStruct(shape, dtype)


def params(mib=16):
    return pltpu.CompilerParams(
        dimension_semantics=("arbitrary",), vmem_limit_bytes=mib << 20
    )


def fwd_outs(tq, wd):
    return [struct((tq, wd), f32), struct((8, tq), f32)] + [struct((tq // 4, wd), bf16)] * 4


def attend_fwd(q, feats, nf, kv, sc, n):
    tq, wd = q.shape
    bk, width = kv.shape[1], feats.shape[1]
    outs = fwd_outs(tq, wd)
    return pl.pallas_call(
        functools.partial(fwd_grid, wd // HEAD_DIM, nf, n),
        grid_spec=pltpu.PrefetchScalarGridSpec(
            num_scalar_prefetch=1,
            grid=(n,),
            in_specs=[
                whole_block(tq, wd),
                pl.BlockSpec((tq, width), lambda i, s: (s[0], 0)),
                pl.BlockSpec((1, bk, 2 * wd), lambda i, s: (i, 0, 0)),
                pl.BlockSpec((bk, width), lambda i, s: (s[SC + i], 0)),
            ],
            out_specs=[whole_block(*o.shape) for o in outs],
            scratch_shapes=[
                pltpu.VMEM((wd, tq), f32),
                pltpu.VMEM((8, tq), f32),
                pltpu.VMEM((8, tq), f32),
            ],
        ),
        out_shape=outs,
        compiler_params=params(),
        name="attend_fwd",
    )(sc, q, feats, kv, feats)


def attend_bwd(q, feats, nf, pieces, att, lse, kv, sc, n):
    tq, wd = q.shape
    bk, width = kv.shape[1], feats.shape[1]
    return pl.pallas_call(
        functools.partial(bwd_grid, wd // HEAD_DIM, nf, n),
        grid_spec=pltpu.PrefetchScalarGridSpec(
            num_scalar_prefetch=1,
            grid=(n,),
            in_specs=[whole_block(tq, wd), pl.BlockSpec((tq, width), lambda i, s: (s[0], 0))]
            + [whole_block(tq // 4, wd)] * 4
            + [
                whole_block(tq, wd),
                whole_block(8, tq),
                pl.BlockSpec((1, bk, 2 * wd), lambda i, s: (i, 0, 0)),
                pl.BlockSpec((bk, width), lambda i, s: (s[SC + i], 0)),
            ],
            out_specs=[whole_block(tq, wd), pl.BlockSpec((1, bk, 2 * wd), lambda i, s: (i, 0, 0))],
            scratch_shapes=[
                pltpu.VMEM((tq, wd), bf16),
                pltpu.VMEM((8, tq), f32),
                pltpu.VMEM((wd, tq), f32),
            ],
        ),
        out_shape=[struct((tq, wd), bf16), struct(kv.shape, bf16)],
        compiler_params=params(),
        name="attend_bwd",
    )(sc, q, feats, *pieces, att, lse, kv, feats)


def fwd_part(nh, nf, tiles, bk, first, last, sc, *refs):
    q, fq = refs[:2]
    n = len(tiles)
    kvs, fks = refs[2 : 2 + n], refs[2 + n : 2 + 2 * n]
    rest = refs[2 + 2 * n :]
    if not first:
        rest = rest[3:]
    if last:
        out, lse, *msgs = rest[:6]
        acc, m, l = rest[6:9]
    else:
        acc, m, l = rest[:3]
    if first:
        fwd_start(acc, m, l)
    for (place, rows, offset), kv, fk in zip(tiles, kvs, fks):

        @pl.when(tile_needed(sc[SC + place], sc, bk))
        def _():
            fwd_tile(
                nh, nf, q, fq, kv, fk, sc[SC + place] * bk + offset, sc[0] * q.shape[0], acc, m, l
            )

    if last:
        fwd_end(nh, [sc[2 + r] for r in range(4)], acc, m, l, out, lse, msgs)


def attend_fwd_part(q, feats, nf, kvs, tiles, state, sc, last):
    tq, wd = q.shape
    width = feats.shape[1]
    n = len(tiles)
    sums = [struct((wd, tq), f32), struct((8, tq), f32), struct((8, tq), f32)]
    ins = [whole_block(tq, wd), pl.BlockSpec((tq, width), lambda i, s: (s[0], 0))]
    ins += [whole_block(*kv.shape) for kv in kvs]
    for place, rows, offset in tiles:
        at = lambda i, s, p=place, k=tq // rows, o=offset // rows: (s[SC + p] * k + o, 0)
        ins.append(pl.BlockSpec((rows, width), at))
    args = [sc, q, feats, *kvs, *([feats] * n)]
    outs = (fwd_outs(tq, wd) if last else []) + sums
    alias = {}
    if state is not None:
        ins += [whole_block(*o.shape) for o in sums]
        alias = {len(args) + k: len(outs) - 3 + k for k in range(3)}
        args += state

    def kernel(sc_ref, *refs):
        if state is not None:
            olds = refs[2 + 2 * n : 5 + 2 * n]
            news = refs[len(refs) - 3 :]
            for old, new in zip(olds, news):
                new[...] = old[...]
        fwd_part(wd // HEAD_DIM, nf, tiles, tq, state is None, last, sc_ref, *refs)

    got = pl.pallas_call(
        kernel,
        grid_spec=pltpu.PrefetchScalarGridSpec(
            num_scalar_prefetch=1,
            grid=(1,),
            in_specs=ins,
            out_specs=[whole_block(*o.shape) for o in outs],
        ),
        out_shape=outs,
        input_output_aliases=alias,
        compiler_params=params(),
        cost_estimate=pl.CostEstimate(flops=n << 31, bytes_accessed=n << 20, transcendentals=0),
        name="fwd_part",
    )(*args)
    return got[:6] if last else got


def attend_bwd_part(q, feats, nf, kvs, tiles, lse, sc, start, state, last):
    tq, wd = q.shape
    nh = wd // HEAD_DIM
    width = feats.shape[1]
    n = len(tiles)
    held = [struct((tq, wd), bf16), struct((8, tq), f32), struct((wd, tq), f32)]
    ins = [whole_block(tq, wd), pl.BlockSpec((tq, width), lambda i, s: (s[0], 0)), whole_block(8, tq)]
    ins += [whole_block(*kv.shape) for kv in kvs]
    for place, rows, offset in tiles:
        at = lambda i, s, p=place, k=tq // rows, o=offset // rows: (s[SC + p] * k + o, 0)
        ins.append(pl.BlockSpec((rows, width), at))
    args = [sc, q, feats, lse, *kvs, *([feats] * n)]
    outs = [struct(kv.shape, bf16) for kv in kvs]
    more = start if start is not None else state
    ins += [whole_block(*v.shape) for v in more]
    args += more
    if start is not None:
        outs = outs + held
    elif not last:
        outs = outs + held[2:]
    if last:
        outs = outs + [struct((tq, wd), bf16)]
    scratch = [pltpu.VMEM((wd, tq), f32)] if last else []

    def kernel(sc_ref, *refs):
        q_ref, fq, lse_ref = refs[:3]
        kv_refs, fks = refs[3 : 3 + n], refs[3 + n : 3 + 2 * n]
        given = refs[3 + 2 * n : 3 + 2 * n + len(more)]
        rest = refs[3 + 2 * n + len(more) :]
        dkvs, rest = rest[:n], rest[n:]
        if start is not None:
            do, dterm, dq_t = rest[:3]
            bwd_start(nh, [sc_ref[2 + r] for r in range(4)], given[:4], given[4], do, dterm, dq_t)
        else:
            do, dterm, old = given
            dq_t = rest[-1] if last else rest[0]
            dq_t[...] = old[...]
        for (place, rows, offset), kv, fk, dkv in zip(tiles, kv_refs, fks, dkvs):
            need = tile_needed(sc_ref[SC + place], sc_ref, tq)

            @pl.when(jnp.logical_not(need))
            def _():
                dkv[...] = jnp.zeros_like(dkv)

            @pl.when(need)
            def _():
                got = bwd_tile(
                    nh, nf, q_ref, fq, do, lse_ref, dterm, kv, fk,
                    sc_ref[SC + place] * tq + offset, sc_ref[0] * tq, dq_t,
                )
                for h in range(nh):
                    dkv[:, 128 * h : 128 * h + 128] = got[h]

        if last:
            rest[0][...] = (dq_t[...].T * HEAD_DIM**-0.5).astype(bf16)

    return pl.pallas_call(
        kernel,
        grid_spec=pltpu.PrefetchScalarGridSpec(
            num_scalar_prefetch=1,
            grid=(1,),
            in_specs=ins,
            out_specs=[whole_block(*o.shape) for o in outs],
            scratch_shapes=scratch,
        ),
        out_shape=outs,
        compiler_params=params(56 if start is not None else 16),
        cost_estimate=pl.CostEstimate(flops=n << 31, bytes_accessed=n << 20, transcendentals=0),
        name="bwd_part",
    )(*args)


def ring_attend(q, feats, nf, kv, sc, g, pack_in, head_pos):
    rows = kv.shape[0]
    half = rows // 2
    a = b = kv
    tiles, state = [kv], None
    whole = lambda p: (p, rows, 0)
    part = functools.partial(attend_fwd_part, q, feats, nf)
    for step in range(3):
        a2, b2 = lax.ppermute(a, "seq", FWD), lax.ppermute(b, "seq", BWD)
        if step == 0:
            state = part([kv], [whole(0)], None, sc, False)
        else:
            state = part([a, b], [whole(2 * step - 1), whole(2 * step)], state, sc, False)
        a, b, state = lax.optimization_barrier((a2, b2, state))
        if step == 0:
            a, b, g, pack_in = lax.optimization_barrier((a, b, g, pack_in))
            pack = out_pack(*pack_in)
            far_g, far_pack = (lax.ppermute(v, "head", CROSS) for v in (g, pack))
        if step == 2:
            a, b, far_g, far_pack = lax.optimization_barrier((a, b, far_g, far_pack))
            gs, packs = (
                [v, lax.ppermute(v, "head", CORE), w, lax.ppermute(w, "head", CORE)]
                for v, w in ((g, far_g), (pack, far_pack))
            )
        tiles += [a, b]
    c, d = lax.ppermute(a[:half], "seq", FWD), lax.ppermute(b[half:], "seq", BWD)
    g = head_columns(gs, head_pos)
    state = part([a, b], [whole(5), whole(6)], state, sc, False)
    tiles += [c, d]
    c, d, g, state = lax.optimization_barrier((c, d, g, state))
    return part([c, d], [(7, half, 0), (7, half, half)], state, sc, True), tiles, g, packs


def ring_attend_back(q, feats, nf, tiles, pieces, att, lse, sc, beside):
    rows = tiles[0].shape[0]
    half = rows // 2
    whole = lambda p: (p, rows, 0)
    part = functools.partial(attend_bwd_part, q, feats, nf)
    c, d, do, dterm, dq_t = part(
        tiles[7:9], [(7, half, 0), (7, half, half)], lse, sc, [*pieces, att], None, False
    )
    c, d, dq_t, (dbr, sub) = lax.optimization_barrier((c, d, dq_t, beside))
    a, b = lax.ppermute(c, "seq", FWD), lax.ppermute(d, "seq", BWD)
    for place in (5, 3, 1):
        given, at = tiles[place : place + 2], [whole(place), whole(place + 1)]
        if place == 3:
            t, u, own, dq_t = part(
                given + tiles[:1], at + [whole(0)], lse, sc, None, [do, dterm, dq_t], False
            )
        elif place == 5:
            t, u, dq_t = part(given, at, lse, sc, None, [do, dterm, dq_t], False)
        else:
            t, u, dq = part(given, at, lse, sc, None, [do, dterm, dq_t], True)
        if place == 5:
            up = jnp.concatenate([add_low(u[:half], a), u[half:]], axis=0)
            down = jnp.concatenate([t[:half], add_low(t[half:], b)], axis=0)
        else:
            up, down = add_low(u, a), add_low(t, b)
        if place == 1:
            up, down, beside = lax.optimization_barrier((up, down, beside))
        elif place == 3:
            up, down, dq_t = lax.optimization_barrier((up, down, dq_t))
        else:
            up, down, dq_t = lax.optimization_barrier((up, down, dq_t))
            beside = head_whole(dbr), head_pieces(*sub)
        a, b = lax.ppermute(up, "seq", FWD), lax.ppermute(down, "seq", BWD)
    return dq, (own.astype(f32) + a.astype(f32) + b.astype(f32)).astype(bf16), beside


VEC_ROWS = 16


def out_pack(w_out, sub_gain, sub_bias):
    width = w_out.shape[1]
    share = sub_gain.shape[0]
    room = width // 3
    pad = lambda v: jnp.concatenate([v, jnp.zeros((room - share,), f32)])
    vec = jnp.concatenate([pad(sub_gain), pad(sub_bias), jnp.zeros((room,), f32)]).reshape(1, width)
    high = vec.astype(bf16)
    rest = vec - lax.optimization_barrier(high).astype(f32)
    middle = rest.astype(bf16)
    low = (rest - lax.optimization_barrier(middle).astype(f32)).astype(bf16)
    top = jnp.concatenate([high, middle, low, jnp.zeros((VEC_ROWS - 3, width), bf16)], axis=0)
    return jnp.concatenate([top, w_out], axis=0)


def unpack_vec(w, row):
    v = w[0:VEC_ROWS, :].astype(f32)
    return v[row : row + 1] + v[row + 1 : row + 2] + v[row + 2 : row + 3]


def sub_parts(pieces, width):
    total = sum(jnp.sum(p, axis=1, keepdims=True) for p in pieces)
    square = sum(jnp.sum(p * p, axis=1, keepdims=True) for p in pieces)
    mean = total / width
    inv = lax.rsqrt(square / width - mean * mean + eps)
    return [(p - mean) * inv for p in pieces], inv


def norm_parts(x):
    center = x - jnp.mean(x, axis=1, keepdims=True)
    rs = lax.rsqrt(jnp.mean(center * center, axis=1, keepdims=True) + eps)
    return center * rs, rs


def norm_back(g, hat, rs):
    return rs * (
        g - jnp.mean(g, axis=1, keepdims=True) - hat * jnp.mean(g * hat, axis=1, keepdims=True)
    )


def mid1_kernel(sc, p0, p1, p2, p3, w0, w1, w2, w3, x, b_out, gain2, bias2, nm, middle, sub):
    share = p0.shape[1]
    room = w0.shape[1] // 3
    cen, _ = sub_parts([p[...].astype(f32) for p in (p0, p1, p2, p3)], w0.shape[1])
    acc = x[...].astype(f32) + b_out[...]
    for r, w in enumerate((w0, w1, w2, w3)):
        vec = unpack_vec(w, 0)
        s = (cen[r] * vec[:, :share] + vec[:, room : room + share]).astype(bf16)
        sub[r] = s
        acc = acc + dot(s, w[VEC_ROWS : VEC_ROWS + share, :])
    middle[...] = acc
    hat, _ = norm_parts(acc)
    nm[...] = (hat * gain2[...] + bias2[...]).astype(bf16)


def gelu_parts(z):
    half = 0.5 * (1.0 + lax.erf(z * np.float32(np.sqrt(0.5))))
    slope = half + z * (np.float32(1.0 / np.sqrt(2.0 * np.pi)) * jnp.exp(-0.5 * z * z))
    return z * half, slope


def ffn_kernel(pair, sc, n0, n1, g, w_up, w_down, b_up, *refs):
    nm, act, d_inner, *outs = refs[len(refs) - 7 :]
    rows = n0.shape[0]
    for k, piece in enumerate((n0, n1)):
        quarter = sc[2 * pair + k]
        at = pl.ds(pl.multiple_of((quarter & 1) * rows, rows), rows)
        x = piece[...]
        nm[at, :] = x
        a, slope = gelu_parts(dot(x, w_up[...]) + b_up[...])
        a = a.astype(bf16)
        g_rows = g[pl.ds(pl.multiple_of(quarter * rows, rows), rows), :]
        d = (dot(g_rows, w_down[...], NT) * slope).astype(bf16)
        act[at, :] = a
        d_inner[at, :] = d
        outs[k][...] = dot(a, w_down[...]).astype(bf16)
        outs[2 + k][...] = dot(d, w_up[...], NT).astype(bf16)


def mid2_kernel(sc, p0, p1, p2, p3, w0, w1, w2, w3, middle, g, gain2, t0, t1, t2, t3, *refs):
    d_mid, dbr, d0, d1, d2, d3, vec768, vec192 = refs
    share = p0.shape[1]
    width = w0.shape[1]
    dn = sum(t[...].astype(f32) for t in (t0, t1, t2, t3))
    hat, rs = norm_parts(middle[...])
    vec768[0:1, :] = jnp.sum(dn * hat, axis=0, keepdims=True)
    vec768[1:2, :] = jnp.sum(dn, axis=0, keepdims=True)
    dm = g[...].astype(f32) + norm_back(dn * gain2[...], hat, rs)
    d_mid[...] = dm
    branch = dm.astype(bf16)
    dbr[...] = branch
    cen, inv = sub_parts([p[...].astype(f32) for p in (p0, p1, p2, p3)], width)
    hats = []
    for r, w in enumerate((w0, w1, w2, w3)):
        ds = dot(branch, w[VEC_ROWS : VEC_ROWS + share, :], NT)
        vec192[r : r + 1, :] = jnp.sum(ds * cen[r], axis=0, keepdims=True)
        vec192[r + 4 : r + 5, :] = jnp.sum(ds, axis=0, keepdims=True)
        hats.append(ds * unpack_vec(w, 0)[:, :share])
    s1 = sum(jnp.sum(t, axis=1, keepdims=True) for t in hats) / width
    s2 = sum(jnp.sum(t * c, axis=1, keepdims=True) for t, c in zip(hats, cen)) / width
    for o, t, c in zip((d0, d1, d2, d3), hats, cen):
        o[...] = (inv * (t - s1 - c * s2)).astype(bf16)


def one_step(kernel, ins, in_specs, outs, name, flops, mib=16):
    return pl.pallas_call(
        kernel,
        grid_spec=pltpu.PrefetchScalarGridSpec(
            num_scalar_prefetch=1,
            grid=(1,),
            in_specs=in_specs,
            out_specs=[whole_block(*o.shape) for o in outs],
        ),
        out_shape=outs,
        compiler_params=params(mib),
        cost_estimate=pl.CostEstimate(flops=flops, bytes_accessed=12 << 20, transcendentals=0),
        name=name,
    )(*ins)


def mid1(head_no, pieces, packs, x, b_out, gain2, bias2):
    quarter, share = pieces[0].shape
    rows, width = packs[0].shape
    at_quarter = pl.BlockSpec((quarter, width), lambda i, s: (s[0], 0))
    return one_step(
        mid1_kernel,
        (head_no, *pieces, *packs, x, b_out, gain2, bias2),
        [whole_block(quarter, share)] * 4
        + [whole_block(rows, width)] * 4
        + [at_quarter]
        + [whole_block(1, width)] * 3,
        [struct((quarter, width), bf16), struct((quarter, width), f32), struct((4, quarter, share), bf16)],
        "mid1",
        2 * quarter * width * width,
    )


def ffn(head_no, pair, pieces, g, w_up, w_down, b_up, held):
    quarter, width = pieces[0].shape
    hidden = w_up.shape[1]
    ins = (head_no, *pieces, g, w_up, w_down, b_up)
    specs = [whole_block(*v.shape) for v in ins[1:]]
    outs = [struct((4 * quarter, k), bf16) for k in (width, hidden, hidden)]
    outs += [struct((quarter, width), bf16)] * 4
    at_chip = lambda k: pl.BlockSpec((2 * quarter, k), lambda i, s: (s[2 * pair] // 2, 0))
    return pl.pallas_call(
        functools.partial(ffn_kernel, pair),
        grid_spec=pltpu.PrefetchScalarGridSpec(
            num_scalar_prefetch=1,
            grid=(1,),
            in_specs=specs + [pl.BlockSpec(memory_space=pl.ANY)] * len(held),
            out_specs=[at_chip(o.shape[1]) for o in outs[:3]] + [whole_block(quarter, width)] * 4,
        ),
        out_shape=outs,
        input_output_aliases={len(ins) + k: k for k in range(len(held))},
        compiler_params=params(),
        cost_estimate=pl.CostEstimate(
            flops=16 * quarter * width * hidden, bytes_accessed=8 << 20, transcendentals=0
        ),
        name="ffn",
    )(*ins, *held)


def mid2(head_no, pieces, packs, middle, g, gain2, terms):
    quarter, share = pieces[0].shape
    rows, width = packs[0].shape
    at_quarter = pl.BlockSpec((quarter, width), lambda i, s: (s[0], 0))
    return one_step(
        mid2_kernel,
        (head_no, *pieces, *packs, middle, g, gain2, *terms),
        [whole_block(quarter, share)] * 4
        + [whole_block(rows, width)] * 4
        + [whole_block(quarter, width), at_quarter, whole_block(1, width)]
        + [whole_block(*t.shape) for t in terms],
        [struct((quarter, width), f32), struct((quarter, width), bf16)]
        + [struct((quarter, share), bf16)] * 4
        + [struct((8, width), f32), struct((8, share), f32)],
        "mid2",
        2 * quarter * width * width,
        56,
    )


def spread_kernel(sc, *refs):
    tiles, (gq, gk, gv, go, gu, gd) = refs[:9], refs[9:]
    rows = tiles[0].shape[0] // 3

    def put(out, at, value):
        out[pl.ds(pl.multiple_of(at, 8), value.shape[0]), :] = value.astype(f32)

    for k in range(8):
        d = sc[SC + k]
        at = d * rows
        which = (d & 1) * 2 + ((d >> 1) & 1)
        for m, out in enumerate((gq, gk, gv, go)):

            @pl.when(which == m)
            def _():
                put(out, (d >> 2) * rows, tiles[k][:rows])

        if k < 7:
            put(gu, at, tiles[k][rows : 2 * rows])
            put(gd, at, tiles[k][2 * rows :])
        else:
            half = rows // 2
            put(gu, at, tiles[7][rows:])
            put(gu, at + half, tiles[8][:half])
            put(gd, at, tiles[8][half:])


def spread(sc, tiles, hidden):
    width = tiles[0].shape[1]
    share = width // 4
    outs = [struct((share, width), f32)] * 4 + [
        struct((width, hidden), f32),
        struct((hidden, width), f32),
    ]
    return one_step(
        spread_kernel,
        (sc, *tiles),
        [whole_block(*t.shape) for t in tiles],
        outs,
        "spread",
        1 << 30,
    )


def shards(
    layer_input, ln1_gain, ln1_bias, w_query, b_query, w_key, w_value, b_value, sub_gain, sub_bias,
    w_out, b_out, ln2_gain, ln2_bias, w_up, b_up, w_down, b_down, cotangent, row_lengths,
):
    rows_local, slice_width = layer_input.shape
    head_share = w_query.shape[1]
    local_heads = head_share // HEAD_DIM
    head_pos = lax.axis_index("head")
    seq_pos = lax.axis_index("seq")
    n_seq = lax.axis_size("seq")
    width = head_share * lax.axis_size("head")
    quarter = rows_local // 4
    relative = jnp.stack([head_pos, head_pos ^ 1, head_pos ^ 2, head_pos ^ 3]).astype(jnp.int32)
    row2 = lambda v: v.reshape(1, -1)

    input_whole = lax.all_gather(layer_input, "head", axis=1, tiled=True)
    hat1, rs1 = norm_parts(input_whole.astype(f32))
    normed = (hat1 * ln1_gain + ln1_bias).astype(bf16)
    pair = lambda a, b: jnp.stack(
        [a.reshape(-1, local_heads, HEAD_DIM), b.reshape(-1, local_heads, HEAD_DIM)], axis=2
    ).reshape(-1, 2 * head_share)
    w_kv = pair(w_key, w_value)
    b_kv = pair(jnp.zeros_like(b_value), b_value)
    kv = (dot(normed, w_kv) + b_kv).astype(bf16)
    queries = (dot(normed, w_query) + b_query).astype(bf16)

    feats, nf, sc = features(rows_local * n_seq, row_lengths, local_heads, rows_local)
    kv, cotangent, pack_in = lax.optimization_barrier((kv, cotangent, (w_out, sub_gain, sub_bias)))
    if n_seq == 8:
        (att, lse, *msgs), kv_tiles, g_whole, packs = ring_attend(
            queries, feats, nf, kv, sc, cotangent, pack_in, head_pos
        )
    else:
        kv_tiles = lax.all_gather(kv, "seq", axis=0)
        att, lse, *msgs = attend_fwd(queries, feats, nf, kv_tiles, sc, n_seq)
        g_whole, packs = head_columns(head_whole(cotangent), head_pos), head_whole(out_pack(*pack_in))

    pieces = head_pieces(*msgs)
    nm, middle, sub = mid1(
        relative, pieces, packs, input_whole, row2(b_out), row2(ln2_gain), row2(ln2_bias)
    )
    nms = head_pieces(nm, nm, nm, nm)
    *held, out0, out1, dn0, dn1 = ffn(
        relative, 0, nms[:2], g_whole, w_up, w_down, row2(b_up), []
    )
    nm_all, act, d_inner, out2, out3, dn2, dn3 = ffn(
        relative, 1, nms[2:], g_whole, w_up, w_down, row2(b_up), held
    )
    outs, dn = (out0, out1, out2, out3), head_pieces(dn0, dn1, dn2, dn3)
    gw_up = dot(nm_all, d_inner, TN).astype(bf16)
    gw_down = dot(act, g_whole, TN).astype(bf16)
    early = jnp.concatenate([v.reshape(8, -1, v.shape[1]) for v in (gw_up, gw_down)], axis=1)
    early = early.reshape(-1, early.shape[2])
    early, dn = lax.optimization_barrier((early, dn))
    if n_seq == 8:
        early = lax.psum_scatter(early, "seq", scatter_dimension=0, tiled=True)
    d_mid, dbr, *d_msgs, vec768, vec192 = mid2(
        relative, pieces, packs, middle, g_whole, row2(ln2_gain), dn
    )
    d_pieces = head_pieces(*d_msgs)
    beside = (dbr, [sub[r] for r in range(4)])

    if n_seq == 8:
        dq, dkv, beside = ring_attend_back(
            queries, feats, nf, kv_tiles, d_pieces, att, lse, sc, beside
        )
    else:
        dq, dkv_tiles = attend_bwd(queries, feats, nf, d_pieces, att, lse, kv_tiles, sc, n_seq)
        dkv = lax.psum_scatter(dkv_tiles, "seq", scatter_dimension=0, tiled=False)
        beside = head_pieces(*[beside[0]] * 4), head_pieces(*beside[1])
        early = lax.psum(early, "seq")
    dbr_all, sub_all = (jnp.concatenate(v, axis=0) for v in beside)

    gw_out = dot(sub_all, dbr_all, TN).astype(bf16)
    gw_query = dot(dq, normed, TN).astype(bf16)
    gb_out = jnp.sum(dbr_all.astype(f32), axis=0)
    gb_up = jnp.sum(d_inner.astype(f32), axis=0)
    gb_down = jnp.sum(g_whole.astype(f32), axis=0)
    gw_kv = dot(dkv, normed, TN).astype(bf16).reshape(local_heads, 2, HEAD_DIM, width)
    gw_kv = jnp.concatenate([gw_kv[:, k].reshape(head_share, width) for k in range(2)], axis=0)
    late = jnp.concatenate([gw_query, gw_kv, gw_out], axis=0)
    late, dkv = lax.optimization_barrier((late, dkv))
    dn = dot(dq, w_query, NT) + dot(dkv, w_kv, NT)
    gb_kv = jnp.sum(dkv.astype(f32), axis=0)
    gb_qkv = jnp.concatenate([jnp.sum(dq.astype(f32), axis=0), gb_kv])
    split = lambda v: jnp.sum(
        jnp.where(relative[:, None, None] == jnp.arange(4)[None, :, None], v[:, None, :], 0.0), axis=0
    ).reshape(-1)
    fill = lambda v: jnp.concatenate([v, jnp.zeros((width - v.shape[0],), f32)])
    small = jnp.stack(
        [
            jnp.sum(dn * hat1, axis=0),
            jnp.sum(dn, axis=0),
            vec768[0],
            vec768[1],
            split(vec192[:4]),
            split(vec192[4:]),
        ]
    )
    more = jnp.stack([gb_up, gb_down, gb_out, fill(gb_qkv)])
    dn = dn.astype(bf16).reshape(2, 2, quarter, width)
    core, chip = head_pos % 2, head_pos // 2
    mine = lax.dynamic_index_in_dim(dn, core, 1, False)
    mate = lax.dynamic_index_in_dim(dn, 1 - core, 1, False)
    hold = lax.optimization_barrier

    if n_seq == 8:
        late = halve(late, 1)
        late, small, mine, mate = hold((late, small, mine, mate))
        mate = lax.ppermute(mate, "head", CORE)
        late = halve(late, 2)
        mine = add_low(mine, mate)
        late, mine, small = hold((late, mine, small))
        far = lax.ppermute(lax.dynamic_index_in_dim(mine, 1 - chip, 0, False), "head", CROSS)
        late = halve(late, 4)
        a = b = jnp.concatenate([late, early], axis=0)
        tiles = [a]
        half = a.shape[0] // 2
        for step in range(3):
            a, b, outs, small, more = hold((a, b, outs, small, more))
            a, b = lax.ppermute(a, "seq", FWD), lax.ppermute(b, "seq", BWD)
            if step == 0:
                small = small + lax.ppermute(small, "head", CORE)
                small = small + lax.ppermute(small, "head", CROSS)
            elif step == 1:
                core_terms = [lax.ppermute(outs[k], "head", CORE) for k in (1, 3)]
                cross_term = lax.ppermute(add_low(outs[2], core_terms[1]), "head", CROSS)
                outs = outs[0], core_terms[0], cross_term
                small = jnp.concatenate([small, more], axis=0)
                small = small + lax.ppermute(small, "seq", exchange(1))
            else:
                small = small + lax.ppermute(small, "seq", exchange(2))
            tiles += [a, b]
        a, b, small = hold((a, b, small))
        tiles += [lax.ppermute(a[:half], "seq", FWD), lax.ppermute(b[half:], "seq", BWD)]
        small = small + lax.ppermute(small, "seq", exchange(4))
        gw_query, gw_key, gw_value, gw_out, gw_up, gw_down = spread(sc, tiles, w_up.shape[1])
    else:
        mine = add_low(mine, lax.ppermute(mate, "head", CORE))
        far = lax.ppermute(lax.dynamic_index_in_dim(mine, 1 - chip, 0, False), "head", CROSS)
        small = small + lax.ppermute(small, "head", CORE)
        small = small + lax.ppermute(small, "head", CROSS)
        small = lax.psum(jnp.concatenate([small, more], axis=0), "seq")
        outs = head_pieces(*outs)
        late = lax.psum(late, "seq").astype(f32)
        gw_query, gw_key, gw_value, gw_out = (
            late[k * head_share : (k + 1) * head_share] for k in range(4)
        )
        early = early.astype(f32).reshape(8, 2, -1, width)
        gw_up, gw_down = early[:, 0].reshape(-1, width), early[:, 1].reshape(-1, width)

    y = middle + (sum(t.astype(f32) for t in outs) + b_down)
    dn = lax.dynamic_index_in_dim(mine, chip, 0, False).astype(f32) + far.astype(f32)
    cut = lambda v: lax.dynamic_slice_in_dim(v, head_pos * quarter, quarter, 0)
    d_in = d_mid + norm_back(dn * ln1_gain, cut(hat1), cut(rs1))
    both = lax.all_to_all(jnp.stack([y, d_in]).astype(bf16), "head", 2, 1, tiled=True)
    layer_output, grad_input = both[0], both[1].astype(f32)

    gb_qkv = small[9]
    own = lambda v: lax.dynamic_slice_in_dim(v, head_pos * head_share, head_share, 0)
    gb_value = gb_qkv[head_share : 3 * head_share].reshape(local_heads, 2, HEAD_DIM)[:, 1].reshape(-1)
    return (
        layer_output,
        grad_input,
        small[0],
        small[1],
        gw_query.T,
        gb_qkv[:head_share],
        gw_key.T,
        gw_value.T,
        gb_value,
        own(small[4]),
        own(small[5]),
        gw_out,
        small[8],
        small[2],
        small[3],
        gw_up,
        small[6],
        gw_down,
        small[7],
    )


def solution(mesh):
    cols, rows, both, shared, vec = P(None, "head"), P("head", None), P("seq", "head"), P(), P("head")
    in_specs = (
        both, shared, shared, cols, vec, cols, cols, vec, vec, vec,
        rows, shared, shared, shared, cols, vec, rows, shared, both, shared,
    )
    out_specs = (
        both, both, shared, shared, cols, vec, cols, cols, vec, vec,
        vec, rows, shared, shared, shared, cols, vec, rows, shared,
    )
    return jax.shard_map(shards, mesh=mesh, in_specs=in_specs, out_specs=out_specs, check_vma=False)
```

```python
import functools

import jax
import jax.numpy as jnp
import numpy as np
from jax import lax
from jax.experimental import pallas as pl
from jax.experimental.pallas import tpu as pltpu
from jax.sharding import PartitionSpec as P

HEAD_DIM = 64
SEG = 2048
eps = 1e-05
segment_scales = (1, 2, 4, 8, 16)
dilation_steps = (1, 2, 4, 6, 12)
bf16 = jnp.bfloat16
f32 = jnp.float32
NT = (((1,), (1,)), ((), ()))
NN = (((1,), (0,)), ((), ()))
TN = (((0,), (0,)), ((), ()))

RING = (0, 2, 4, 6, 7, 5, 3, 1)
FWD = [(RING[i], RING[(i + 1) % 8]) for i in range(8)]
BWD = [(b, a) for a, b in FWD]
CORE = [(0, 1), (1, 0), (2, 3), (3, 2)]
CROSS = [(0, 2), (2, 0), (1, 3), (3, 1)]
BOTH = [(0, 3), (3, 0), (1, 2), (2, 1)]


def dot(a, b, dims=NN):
    return lax.dot_general(a, b, dims, preferred_element_type=f32)


def add_low(u, v):
    return (u.astype(f32) + v.astype(f32)).astype(u.dtype)


def exchange(step):
    return [(i, i ^ step) for i in range(8)]


def halve(x, step):
    half = x.shape[0] // 2
    bit = (lax.axis_index("seq") // step) % 2
    keep = lax.dynamic_slice_in_dim(x, bit * half, half, 0)
    send = lax.dynamic_slice_in_dim(x, (1 - bit) * half, half, 0)
    return add_low(keep, lax.ppermute(send, "seq", exchange(step)))


def head_pieces(own, core, cross, both):
    return (
        own,
        lax.ppermute(core, "head", CORE),
        lax.ppermute(cross, "head", CROSS),
        lax.ppermute(both, "head", BOTH),
    )


def head_whole(x):
    p = lax.ppermute(x, "head", CROSS)
    return x, lax.ppermute(x, "head", CORE), p, lax.ppermute(p, "head", CORE)


def head_columns(got, head_pos):
    return jnp.concatenate([lax.select_n(head_pos ^ k, *got) for k in range(4)], axis=1)


SC = 6


def feature_table(total, nrow, nh, n_head):
    sizes = [nrow + total // (SEG * scale) for scale in segment_scales]
    nf = sum(sizes)
    width = -(-nh * nf // 128) * 128
    table = np.zeros((-(-(4 + n_head) // 8) * 8, width), np.int32)
    table[3] = -1
    for h in range(nh):
        lane = h * nf
        for scale, step, size in zip(segment_scales, dilation_steps, sizes):
            at = slice(lane, lane + size)
            table[0, at] = (SEG * scale).bit_length() - 1
            table[1, at] = SEG * scale - 1
            table[2, at] = lane
            table[3, at] = np.arange(lane, lane + size)
            for d in range(n_head):
                table[4 + d, at] = sum(1 << b for b in range(12) if b % step == (d * nh + h) % step)
            lane += size
    return table, nf


def feature_kernel(n, nrow, bk, lengths, table, out, sc, seg_ref, place_ref):
    block = pl.program_id(0)
    width = out.shape[1]
    seq_pos, head_pos = lax.axis_index("seq"), lax.axis_index("head")
    ends, end, row_begin = [], 0, 0
    for r in range(nrow):
        end = end + lengths[r]
        ends.append(end)
        row_begin = jnp.where(end <= seq_pos * bk, end, row_begin)

    @pl.when(block == 0)
    def _():
        sc[0] = seq_pos
        sc[1] = row_begin
        for r in range(4):
            sc[2 + r] = head_pos ^ r
        pos = sum(jnp.where(seq_pos == d, k, 0) for k, d in enumerate(RING))
        for k in range(n):
            if n == 8:
                at = (pos + (0, 7, 1, 6, 2, 5, 3, 4)[k]) & 7
                sc[SC + k] = sum(jnp.where(at == m, d, 0) for m, d in enumerate(RING))
            else:
                sc[SC + k] = k

    shift, mask, first, own = (table[k : k + 1, :] for k in range(4))
    residues = table[pl.ds(4 + head_pos, 1), :]
    pieces = [(lengths[r] + mask) >> shift for r in range(nrow)]

    def one(k, carry):
        tile = block * (out.shape[0] // bk) + k

        @pl.when((tile <= seq_pos) & ((tile + 1) * bk > row_begin))
        def _():
            pos = tile * bk + lax.broadcasted_iota(jnp.int32, (bk, width), 0)
            start, base = 0, first
            for r in range(nrow):
                passed = ends[r] <= tile * bk
                start = jnp.where(passed, ends[r], start)
                base = base + jnp.where(passed, pieces[r], 0)
            seg_ref[...] = jnp.broadcast_to(base, (bk, width))
            place_ref[...] = pos - start
            for r in range(nrow):

                @pl.when((ends[r] > tile * bk) & (ends[r] < (tile + 1) * bk))
                def _():
                    past = pos >= ends[r]
                    place_ref[...] = jnp.where(past, pos - ends[r], place_ref[...])
                    seg_ref[...] += jnp.where(past, pieces[r], 0)

            place = place_ref[...]
            seg = seg_ref[...] + (place >> shift)
            part = place & mask
            whole = ((part.astype(f32) + 0.5) * np.float32(1 / 12)).astype(jnp.int32)
            on = (residues >> (part - 12 * whole)) & 1
            out[pl.ds(pl.multiple_of(k * bk, bk), bk), :] = (
                jnp.where(seg == own, on, 0).astype(f32).astype(bf16)
            )

        return carry

    lax.fori_loop(0, out.shape[0] // bk, one, 0)


def features(total, lengths, nh, bk):
    n = total // bk
    nrow = lengths.shape[0]
    table, nf = feature_table(total, nrow, nh, lax.axis_size("head"))
    width = table.shape[1]
    block = 8 * bk if n % 8 == 0 else bk
    feats, sc = pl.pallas_call(
        functools.partial(feature_kernel, n, nrow, bk),
        grid_spec=pltpu.PrefetchScalarGridSpec(
            num_scalar_prefetch=1,
            grid=(total // block,),
            in_specs=[pl.BlockSpec(table.shape, lambda i, s: (0, 0))],
            out_specs=[
                pl.BlockSpec((block, width), lambda i, s: (i, 0)),
                pl.BlockSpec(memory_space=pltpu.SMEM),
            ],
            scratch_shapes=[pltpu.VMEM((bk, width), jnp.int32)] * 2,
        ),
        out_shape=[
            jax.ShapeDtypeStruct((total, width), bf16),
            jax.ShapeDtypeStruct((SC + n,), jnp.int32),
        ],
        compiler_params=pltpu.CompilerParams(
            dimension_semantics=("arbitrary",), vmem_limit_bytes=16 << 20
        ),
        name="features",
    )(lengths, jnp.asarray(table))
    return feats, nf, sc


def head_pad(x, h, upper):
    part = x[:, HEAD_DIM * h : HEAD_DIM * (h + 1)]
    zero = jnp.zeros_like(part)
    return jnp.concatenate([zero, part] if upper else [part, zero], axis=1)


def count_tile(fk, fq, h, nf, first_key, first_row):
    lane = lax.broadcasted_iota(jnp.int32, fq.shape, 1)
    fqh = jnp.where((lane >= h * nf) & (lane < (h + 1) * nf), fq.astype(f32), 0.0).astype(bf16)
    count = dot(fk, fqh, NT)
    keys = first_key + lax.broadcasted_iota(jnp.int32, (count.shape[0], 1), 0)
    rows = first_row + lax.broadcasted_iota(jnp.int32, (1, count.shape[1]), 1)
    return jnp.where(keys <= rows, count, 0.0)


def fwd_tile(nh, nf, q, fq, kv, fk, first_key, first_row, acc, m, l):
    kv_t = kv[...].astype(f32).T.astype(bf16)
    qs = (q[...].astype(f32) * HEAD_DIM**-0.5).astype(bf16)
    for h in range(nh):
        s = dot(kv[:, 128 * h : 128 * h + 128], head_pad(qs, h, False), NT)
        count = count_tile(fk[...], fq[...], h, nf, first_key, first_row)
        s = jnp.where(count > 0, s, -1e30)
        old = m[h : h + 1, :]
        new = jnp.maximum(old, jnp.max(s, axis=0, keepdims=True))
        p = count * jnp.exp(s - new)
        factor = jnp.exp(old - new)
        l[h : h + 1, :] = l[h : h + 1, :] * factor + jnp.sum(p, axis=0, keepdims=True)
        o = dot(kv_t[128 * h : 128 * h + 128], p.astype(bf16))
        acc[64 * h : 64 * h + 64, :] = acc[64 * h : 64 * h + 64, :] * factor + o[64:, :]
        m[h : h + 1, :] = new


def bwd_tile(nh, nf, q, fq, do, lse, dterm, kv, fk, first_key, first_row, dq_t):
    kv_t = kv[...].astype(f32).T.astype(bf16)
    qs = (q[...].astype(f32) * HEAD_DIM**-0.5).astype(bf16)
    out = []
    for h in range(nh):
        kvh = kv[:, 128 * h : 128 * h + 128]
        qh = head_pad(qs, h, False)
        doh = head_pad(do[...], h, True)
        count = count_tile(fk[...], fq[...], h, nf, first_key, first_row)
        p = count * jnp.exp(jnp.minimum(dot(kvh, qh, NT) - lse[h : h + 1, :], 1.0))
        ds = (p * (dot(kvh, doh, NT) - dterm[h : h + 1, :])).astype(bf16)
        out.append((dot(ds, qh) + dot(p.astype(bf16), doh)).astype(bf16))
        o = dot(kv_t[128 * h : 128 * h + 128], ds)
        dq_t[64 * h : 64 * h + 64, :] += o[:64, :]
    return out


def fwd_start(acc, m, l):
    acc[...] = jnp.zeros_like(acc)
    m[...] = jnp.full_like(m, -1e30)
    l[...] = jnp.zeros_like(l)


def fwd_end(nh, quarters, acc, m, l, out, lse, msgs):
    for h in range(nh):
        out[:, 64 * h : 64 * h + 64] = (acc[64 * h : 64 * h + 64, :] / l[h : h + 1, :]).T
    lse[...] = m[...] + jnp.log(jnp.maximum(l[...], 1e-30))
    rows = msgs[0].shape[0]
    for at, msg in zip(quarters, msgs):
        msg[...] = out[pl.ds(pl.multiple_of(at * rows, rows), rows), :].astype(bf16)


def bwd_start(nh, quarters, pieces, att, do, dterm, dq_t):
    dq_t[...] = jnp.zeros_like(dq_t)
    rows = pieces[0].shape[0]
    for at, piece in zip(quarters, pieces):
        do[pl.ds(pl.multiple_of(at * rows, rows), rows), :] = piece[...]
    prod = do[...].astype(f32) * att[...]
    r = lax.broadcasted_iota(jnp.int32, (8, prod.shape[1]), 0)
    c = lax.broadcasted_iota(jnp.int32, (8, prod.shape[1]), 1)
    pick = jnp.where(c // HEAD_DIM == r, 1.0, 0.0).astype(f32)
    dterm[...] = lax.dot_general(
        pick, prod, NT, precision=lax.Precision.HIGHEST, preferred_element_type=f32
    )


def tile_needed(tile, sc, bk):
    return (tile <= sc[0]) & ((tile + 1) * bk > sc[1])


def fwd_grid(nh, nf, n, sc, q, fq, kv, fk, out, lse, m0, m1, m2, m3, acc, m, l):
    i = pl.program_id(0)
    bk = kv.shape[1]

    @pl.when(i == 0)
    def _():
        fwd_start(acc, m, l)

    @pl.when(tile_needed(sc[SC + i], sc, bk))
    def _():
        fwd_tile(nh, nf, q, fq, kv.at[0], fk, sc[SC + i] * bk, sc[0] * q.shape[0], acc, m, l)

    @pl.when(i == n - 1)
    def _():
        fwd_end(nh, [sc[2 + r] for r in range(4)], acc, m, l, out, lse, (m0, m1, m2, m3))


def bwd_grid(nh, nf, n, sc, q, fq, d0, d1, d2, d3, att, lse, kv, fk, dq, dkv, do, dterm, dq_t):
    i = pl.program_id(0)
    bk = kv.shape[1]

    @pl.when(i == 0)
    def _():
        bwd_start(nh, [sc[2 + r] for r in range(4)], (d0, d1, d2, d3), att, do, dterm, dq_t)

    need = tile_needed(sc[SC + i], sc, bk)

    @pl.when(jnp.logical_not(need))
    def _():
        dkv[...] = jnp.zeros_like(dkv)

    @pl.when(need)
    def _():
        out = bwd_tile(
            nh, nf, q, fq, do, lse, dterm, kv.at[0], fk, sc[SC + i] * bk, sc[0] * q.shape[0], dq_t
        )
        for h in range(nh):
            dkv[0, :, 128 * h : 128 * h + 128] = out[h]

    @pl.when(i == n - 1)
    def _():
        dq[...] = (dq_t[...].T * HEAD_DIM**-0.5).astype(dq.dtype)


def whole_block(*shape):
    return pl.BlockSpec(shape, lambda i, s: (0,) * len(shape))


def struct(shape, dtype):
    return jax.ShapeDtypeStruct(shape, dtype)


def params(mib=16):
    return pltpu.CompilerParams(
        dimension_semantics=("arbitrary",), vmem_limit_bytes=mib << 20
    )


def fwd_outs(tq, wd):
    return [struct((tq, wd), f32), struct((8, tq), f32)] + [struct((tq // 4, wd), bf16)] * 4


def attend_fwd(q, feats, nf, kv, sc, n):
    tq, wd = q.shape
    bk, width = kv.shape[1], feats.shape[1]
    outs = fwd_outs(tq, wd)
    return pl.pallas_call(
        functools.partial(fwd_grid, wd // HEAD_DIM, nf, n),
        grid_spec=pltpu.PrefetchScalarGridSpec(
            num_scalar_prefetch=1,
            grid=(n,),
            in_specs=[
                whole_block(tq, wd),
                pl.BlockSpec((tq, width), lambda i, s: (s[0], 0)),
                pl.BlockSpec((1, bk, 2 * wd), lambda i, s: (i, 0, 0)),
                pl.BlockSpec((bk, width), lambda i, s: (s[SC + i], 0)),
            ],
            out_specs=[whole_block(*o.shape) for o in outs],
            scratch_shapes=[
                pltpu.VMEM((wd, tq), f32),
                pltpu.VMEM((8, tq), f32),
                pltpu.VMEM((8, tq), f32),
            ],
        ),
        out_shape=outs,
        compiler_params=params(),
        name="attend_fwd",
    )(sc, q, feats, kv, feats)


def attend_bwd(q, feats, nf, pieces, att, lse, kv, sc, n):
    tq, wd = q.shape
    bk, width = kv.shape[1], feats.shape[1]
    return pl.pallas_call(
        functools.partial(bwd_grid, wd // HEAD_DIM, nf, n),
        grid_spec=pltpu.PrefetchScalarGridSpec(
            num_scalar_prefetch=1,
            grid=(n,),
            in_specs=[whole_block(tq, wd), pl.BlockSpec((tq, width), lambda i, s: (s[0], 0))]
            + [whole_block(tq // 4, wd)] * 4
            + [
                whole_block(tq, wd),
                whole_block(8, tq),
                pl.BlockSpec((1, bk, 2 * wd), lambda i, s: (i, 0, 0)),
                pl.BlockSpec((bk, width), lambda i, s: (s[SC + i], 0)),
            ],
            out_specs=[whole_block(tq, wd), pl.BlockSpec((1, bk, 2 * wd), lambda i, s: (i, 0, 0))],
            scratch_shapes=[
                pltpu.VMEM((tq, wd), bf16),
                pltpu.VMEM((8, tq), f32),
                pltpu.VMEM((wd, tq), f32),
            ],
        ),
        out_shape=[struct((tq, wd), bf16), struct(kv.shape, bf16)],
        compiler_params=params(),
        name="attend_bwd",
    )(sc, q, feats, *pieces, att, lse, kv, feats)


def fwd_part(nh, nf, tiles, bk, first, last, sc, *refs):
    q, fq = refs[:2]
    n = len(tiles)
    kvs, fks = refs[2 : 2 + n], refs[2 + n : 2 + 2 * n]
    rest = refs[2 + 2 * n :]
    if not first:
        rest = rest[3:]
    if last:
        out, lse, *msgs = rest[:6]
        acc, m, l = rest[6:9]
    else:
        acc, m, l = rest[:3]
    if first:
        fwd_start(acc, m, l)
    for (place, rows, offset), kv, fk in zip(tiles, kvs, fks):

        @pl.when(tile_needed(sc[SC + place], sc, bk))
        def _():
            fwd_tile(
                nh, nf, q, fq, kv, fk, sc[SC + place] * bk + offset, sc[0] * q.shape[0], acc, m, l
            )

    if last:
        fwd_end(nh, [sc[2 + r] for r in range(4)], acc, m, l, out, lse, msgs)


def attend_fwd_part(q, feats, nf, kvs, tiles, state, sc, last):
    tq, wd = q.shape
    width = feats.shape[1]
    n = len(tiles)
    sums = [struct((wd, tq), f32), struct((8, tq), f32), struct((8, tq), f32)]
    ins = [whole_block(tq, wd), pl.BlockSpec((tq, width), lambda i, s: (s[0], 0))]
    ins += [whole_block(*kv.shape) for kv in kvs]
    for place, rows, offset in tiles:
        at = lambda i, s, p=place, k=tq // rows, o=offset // rows: (s[SC + p] * k + o, 0)
        ins.append(pl.BlockSpec((rows, width), at))
    args = [sc, q, feats, *kvs, *([feats] * n)]
    outs = (fwd_outs(tq, wd) if last else []) + sums
    alias = {}
    if state is not None:
        ins += [whole_block(*o.shape) for o in sums]
        alias = {len(args) + k: len(outs) - 3 + k for k in range(3)}
        args += state

    def kernel(sc_ref, *refs):
        if state is not None:
            olds = refs[2 + 2 * n : 5 + 2 * n]
            news = refs[len(refs) - 3 :]
            for old, new in zip(olds, news):
                new[...] = old[...]
        fwd_part(wd // HEAD_DIM, nf, tiles, tq, state is None, last, sc_ref, *refs)

    got = pl.pallas_call(
        kernel,
        grid_spec=pltpu.PrefetchScalarGridSpec(
            num_scalar_prefetch=1,
            grid=(1,),
            in_specs=ins,
            out_specs=[whole_block(*o.shape) for o in outs],
        ),
        out_shape=outs,
        input_output_aliases=alias,
        compiler_params=params(),
        cost_estimate=pl.CostEstimate(flops=n << 31, bytes_accessed=n << 20, transcendentals=0),
        name="fwd_part",
    )(*args)
    return got[:6] if last else got


def attend_bwd_part(q, feats, nf, kvs, tiles, lse, sc, start, state, last):
    tq, wd = q.shape
    nh = wd // HEAD_DIM
    width = feats.shape[1]
    n = len(tiles)
    held = [struct((tq, wd), bf16), struct((8, tq), f32), struct((wd, tq), f32)]
    ins = [whole_block(tq, wd), pl.BlockSpec((tq, width), lambda i, s: (s[0], 0)), whole_block(8, tq)]
    ins += [whole_block(*kv.shape) for kv in kvs]
    for place, rows, offset in tiles:
        at = lambda i, s, p=place, k=tq // rows, o=offset // rows: (s[SC + p] * k + o, 0)
        ins.append(pl.BlockSpec((rows, width), at))
    args = [sc, q, feats, lse, *kvs, *([feats] * n)]
    outs = [struct(kv.shape, bf16) for kv in kvs]
    more = start if start is not None else state
    ins += [whole_block(*v.shape) for v in more]
    args += more
    if start is not None:
        outs = outs + held
    elif not last:
        outs = outs + held[2:]
    if last:
        outs = outs + [struct((tq, wd), bf16)]
    scratch = [pltpu.VMEM((wd, tq), f32)] if last else []

    def kernel(sc_ref, *refs):
        q_ref, fq, lse_ref = refs[:3]
        kv_refs, fks = refs[3 : 3 + n], refs[3 + n : 3 + 2 * n]
        given = refs[3 + 2 * n : 3 + 2 * n + len(more)]
        rest = refs[3 + 2 * n + len(more) :]
        dkvs, rest = rest[:n], rest[n:]
        if start is not None:
            do, dterm, dq_t = rest[:3]
            bwd_start(nh, [sc_ref[2 + r] for r in range(4)], given[:4], given[4], do, dterm, dq_t)
        else:
            do, dterm, old = given
            dq_t = rest[-1] if last else rest[0]
            dq_t[...] = old[...]
        for (place, rows, offset), kv, fk, dkv in zip(tiles, kv_refs, fks, dkvs):
            need = tile_needed(sc_ref[SC + place], sc_ref, tq)

            @pl.when(jnp.logical_not(need))
            def _():
                dkv[...] = jnp.zeros_like(dkv)

            @pl.when(need)
            def _():
                got = bwd_tile(
                    nh, nf, q_ref, fq, do, lse_ref, dterm, kv, fk,
                    sc_ref[SC + place] * tq + offset, sc_ref[0] * tq, dq_t,
                )
                for h in range(nh):
                    dkv[:, 128 * h : 128 * h + 128] = got[h]

        if last:
            rest[0][...] = (dq_t[...].T * HEAD_DIM**-0.5).astype(bf16)

    return pl.pallas_call(
        kernel,
        grid_spec=pltpu.PrefetchScalarGridSpec(
            num_scalar_prefetch=1,
            grid=(1,),
            in_specs=ins,
            out_specs=[whole_block(*o.shape) for o in outs],
            scratch_shapes=scratch,
        ),
        out_shape=outs,
        compiler_params=params(56 if start is not None else 16),
        cost_estimate=pl.CostEstimate(flops=n << 31, bytes_accessed=n << 20, transcendentals=0),
        name="bwd_part",
    )(*args)


def ring_attend(q, feats, nf, kv, sc, g, pack_in, head_pos):
    rows = kv.shape[0]
    half = rows // 2
    a = b = kv
    tiles, state = [kv], None
    whole = lambda p: (p, rows, 0)
    part = functools.partial(attend_fwd_part, q, feats, nf)
    for step in range(3):
        a2, b2 = lax.ppermute(a, "seq", FWD), lax.ppermute(b, "seq", BWD)
        if step == 0:
            state = part([kv], [whole(0)], None, sc, False)
        else:
            state = part([a, b], [whole(2 * step - 1), whole(2 * step)], state, sc, False)
        a, b, state = lax.optimization_barrier((a2, b2, state))
        if step == 0:
            a, b, g, pack_in = lax.optimization_barrier((a, b, g, pack_in))
            pack = out_pack(*pack_in)
            far_g, far_pack = (lax.ppermute(v, "head", CROSS) for v in (g, pack))
        if step == 2:
            a, b, far_g, far_pack = lax.optimization_barrier((a, b, far_g, far_pack))
            gs, packs = (
                [v, lax.ppermute(v, "head", CORE), w, lax.ppermute(w, "head", CORE)]
                for v, w in ((g, far_g), (pack, far_pack))
            )
        tiles += [a, b]
    c, d = lax.ppermute(a[:half], "seq", FWD), lax.ppermute(b[half:], "seq", BWD)
    g = head_columns(gs, head_pos)
    state = part([a, b], [whole(5), whole(6)], state, sc, False)
    tiles += [c, d]
    c, d, g, state = lax.optimization_barrier((c, d, g, state))
    return part([c, d], [(7, half, 0), (7, half, half)], state, sc, True), tiles, g, packs


def ring_attend_back(q, feats, nf, tiles, pieces, att, lse, sc, beside, early):
    rows = tiles[0].shape[0]
    half = rows // 2
    under = early[0].shape[0] // 2
    whole = lambda p: (p, rows, 0)
    part = functools.partial(attend_bwd_part, q, feats, nf)
    c, d, do, dterm, dq_t = part(
        tiles[7:9], [(7, half, 0), (7, half, half)], lse, sc, [*pieces, att], None, False
    )
    c, d = jnp.concatenate([c, early[7]]), jnp.concatenate([d, early[8]])
    own_x, for_core, for_cross = beside
    c, d, dq_t, own_x = lax.optimization_barrier((c, d, dq_t, own_x))
    a, b = lax.ppermute(c, "seq", FWD), lax.ppermute(d, "seq", BWD)
    for place in (5, 3, 1):
        given, at = tiles[place : place + 2], [whole(place), whole(place + 1)]
        if place == 3:
            t, u, own, dq_t = part(
                given + tiles[:1], at + [whole(0)], lse, sc, None, [do, dterm, dq_t], False
            )
        elif place == 5:
            t, u, dq_t = part(given, at, lse, sc, None, [do, dterm, dq_t], False)
            dq_t, for_core, for_cross = lax.optimization_barrier((dq_t, for_core, for_cross))
            cross = lax.ppermute(for_cross, "head", CROSS)
            core = lax.ppermute(for_core, "head", CORE)
        else:
            t, u, dq = part(given, at, lse, sc, None, [do, dterm, dq_t], True)
        e, f = early[place], early[place + 1]
        if place == 5:
            up = [add_low(u[:half], a[:half]), u[half:], add_low(f[:under], a[half:]), f[under:]]
            down = [t[:half], add_low(t[half:], b[:half]), e[:under], add_low(e[under:], b[half:])]
        else:
            up = [add_low(u, a[:rows]), add_low(f, a[rows:])]
            down = [add_low(t, b[:rows]), add_low(e, b[rows:])]
        up, down = jnp.concatenate(up), jnp.concatenate(down)
        if place == 1:
            up, down, both = lax.optimization_barrier((up, down, both))
        elif place == 3:
            up, down, dq_t, cross, core = lax.optimization_barrier((up, down, dq_t, cross, core))
            both = lax.ppermute(cross, "head", CORE)
        else:
            up, down, dq_t = lax.optimization_barrier((up, down, dq_t))
        a, b = lax.ppermute(up, "seq", FWD), lax.ppermute(down, "seq", BWD)
    own = jnp.concatenate([own, early[0]])
    summed = (own.astype(f32) + a.astype(f32) + b.astype(f32)).astype(bf16)
    early = summed[rows:].reshape(2, -1, summed.shape[1])
    early = jnp.concatenate([early[0], early[1]], axis=1)
    return dq, summed[:rows], (own_x, core, cross, both), early


VEC_ROWS = 16


def out_pack(w_out, sub_gain, sub_bias):
    width = w_out.shape[1]
    share = sub_gain.shape[0]
    room = width // 3
    pad = lambda v: jnp.concatenate([v, jnp.zeros((room - share,), f32)])
    vec = jnp.concatenate([pad(sub_gain), pad(sub_bias), jnp.zeros((room,), f32)]).reshape(1, width)
    high = vec.astype(bf16)
    rest = vec - lax.optimization_barrier(high).astype(f32)
    middle = rest.astype(bf16)
    low = (rest - lax.optimization_barrier(middle).astype(f32)).astype(bf16)
    top = jnp.concatenate([high, middle, low, jnp.zeros((VEC_ROWS - 3, width), bf16)], axis=0)
    return jnp.concatenate([top, w_out], axis=0)


def unpack_vec(w, row):
    v = w[0:VEC_ROWS, :].astype(f32)
    return v[row : row + 1] + v[row + 1 : row + 2] + v[row + 2 : row + 3]


def sub_parts(pieces, width):
    total = sum(jnp.sum(p, axis=1, keepdims=True) for p in pieces)
    square = sum(jnp.sum(p * p, axis=1, keepdims=True) for p in pieces)
    mean = total / width
    inv = lax.rsqrt(square / width - mean * mean + eps)
    return [(p - mean) * inv for p in pieces], inv


def norm_parts(x):
    center = x - jnp.mean(x, axis=1, keepdims=True)
    rs = lax.rsqrt(jnp.mean(center * center, axis=1, keepdims=True) + eps)
    return center * rs, rs


def norm_back(g, hat, rs):
    return rs * (
        g - jnp.mean(g, axis=1, keepdims=True) - hat * jnp.mean(g * hat, axis=1, keepdims=True)
    )


def mid1_kernel(sc, p0, p1, p2, p3, w0, w1, w2, w3, x, b_out, gain2, bias2, nm, middle, sub):
    share = p0.shape[1]
    room = w0.shape[1] // 3
    cen, _ = sub_parts([p[...].astype(f32) for p in (p0, p1, p2, p3)], w0.shape[1])
    acc = x[...].astype(f32) + b_out[...]
    for r, w in enumerate((w0, w1, w2, w3)):
        vec = unpack_vec(w, 0)
        s = (cen[r] * vec[:, :share] + vec[:, room : room + share]).astype(bf16)
        sub[r] = s
        acc = acc + dot(s, w[VEC_ROWS : VEC_ROWS + share, :])
    middle[...] = acc
    hat, _ = norm_parts(acc)
    nm[...] = (hat * gain2[...] + bias2[...]).astype(bf16)


def gelu_parts(z):
    half = 0.5 * (1.0 + lax.erf(z * np.float32(np.sqrt(0.5))))
    slope = half + z * (np.float32(1.0 / np.sqrt(2.0 * np.pi)) * jnp.exp(-0.5 * z * z))
    return z * half, slope


def ffn_kernel(pair, sc, n0, n1, g, w_up, w_down, b_up, *refs):
    nm, act, d_inner, *outs = refs[len(refs) - 7 :]
    rows = n0.shape[0]
    for k, piece in enumerate((n0, n1)):
        quarter = sc[2 * pair + k]
        at = pl.ds(pl.multiple_of((quarter & 1) * rows, rows), rows)
        x = piece[...]
        nm[at, :] = x
        a, slope = gelu_parts(dot(x, w_up[...]) + b_up[...])
        a = a.astype(bf16)
        g_rows = g[pl.ds(pl.multiple_of(quarter * rows, rows), rows), :]
        d = (dot(g_rows, w_down[...], NT) * slope).astype(bf16)
        act[at, :] = a
        d_inner[at, :] = d
        outs[k][...] = dot(a, w_down[...]).astype(bf16)
        outs[2 + k][...] = dot(d, w_up[...], NT).astype(bf16)


def mid2_kernel(sc, p0, p1, p2, p3, w0, w1, w2, w3, middle, g, gain2, t0, t1, t2, t3, sub, *refs):
    d_mid, for_core, for_cross, d0, d1, d2, d3, vec768, vec192 = refs
    share = p0.shape[1]
    width = w0.shape[1]
    dn = sum(t[...].astype(f32) for t in (t0, t1, t2, t3))
    hat, rs = norm_parts(middle[...])
    vec768[0:1, :] = jnp.sum(dn * hat, axis=0, keepdims=True)
    vec768[1:2, :] = jnp.sum(dn, axis=0, keepdims=True)
    dm = g[...].astype(f32) + norm_back(dn * gain2[...], hat, rs)
    d_mid[...] = dm
    branch = dm.astype(bf16)
    for_core[:, :width] = branch
    for_core[:, width:] = sub[1]
    for_cross[:, :width] = branch
    for_cross[:, width : width + share] = sub[2]
    for_cross[:, width + share :] = sub[3]
    cen, inv = sub_parts([p[...].astype(f32) for p in (p0, p1, p2, p3)], width)
    hats = []
    for r, w in enumerate((w0, w1, w2, w3)):
        ds = dot(branch, w[VEC_ROWS : VEC_ROWS + share, :], NT)
        vec192[r : r + 1, :] = jnp.sum(ds * cen[r], axis=0, keepdims=True)
        vec192[r + 4 : r + 5, :] = jnp.sum(ds, axis=0, keepdims=True)
        hats.append(ds * unpack_vec(w, 0)[:, :share])
    s1 = sum(jnp.sum(t, axis=1, keepdims=True) for t in hats) / width
    s2 = sum(jnp.sum(t * c, axis=1, keepdims=True) for t, c in zip(hats, cen)) / width
    for o, t, c in zip((d0, d1, d2, d3), hats, cen):
        o[...] = (inv * (t - s1 - c * s2)).astype(bf16)


def one_step(kernel, ins, in_specs, outs, name, flops, mib=16):
    return pl.pallas_call(
        kernel,
        grid_spec=pltpu.PrefetchScalarGridSpec(
            num_scalar_prefetch=1,
            grid=(1,),
            in_specs=in_specs,
            out_specs=[whole_block(*o.shape) for o in outs],
        ),
        out_shape=outs,
        compiler_params=params(mib),
        cost_estimate=pl.CostEstimate(flops=flops, bytes_accessed=12 << 20, transcendentals=0),
        name=name,
    )(*ins)


def mid1(head_no, pieces, packs, x, b_out, gain2, bias2):
    quarter, share = pieces[0].shape
    rows, width = packs[0].shape
    at_quarter = pl.BlockSpec((quarter, width), lambda i, s: (s[0], 0))
    return one_step(
        mid1_kernel,
        (head_no, *pieces, *packs, x, b_out, gain2, bias2),
        [whole_block(quarter, share)] * 4
        + [whole_block(rows, width)] * 4
        + [at_quarter]
        + [whole_block(1, width)] * 3,
        [struct((quarter, width), bf16), struct((quarter, width), f32), struct((4, quarter, share), bf16)],
        "mid1",
        2 * quarter * width * width,
    )


def ffn(head_no, pair, pieces, g, w_up, w_down, b_up, held):
    quarter, width = pieces[0].shape
    hidden = w_up.shape[1]
    ins = (head_no, *pieces, g, w_up, w_down, b_up)
    specs = [whole_block(*v.shape) for v in ins[1:]]
    outs = [struct((4 * quarter, k), bf16) for k in (width, hidden, hidden)]
    outs += [struct((quarter, width), bf16)] * 4
    at_chip = lambda k: pl.BlockSpec((2 * quarter, k), lambda i, s: (s[2 * pair] // 2, 0))
    return pl.pallas_call(
        functools.partial(ffn_kernel, pair),
        grid_spec=pltpu.PrefetchScalarGridSpec(
            num_scalar_prefetch=1,
            grid=(1,),
            in_specs=specs + [pl.BlockSpec(memory_space=pl.ANY)] * len(held),
            out_specs=[at_chip(o.shape[1]) for o in outs[:3]] + [whole_block(quarter, width)] * 4,
        ),
        out_shape=outs,
        input_output_aliases={len(ins) + k: k for k in range(len(held))},
        compiler_params=params(),
        cost_estimate=pl.CostEstimate(
            flops=16 * quarter * width * hidden, bytes_accessed=8 << 20, transcendentals=0
        ),
        name="ffn",
    )(*ins, *held)


def mid2(head_no, pieces, packs, middle, g, gain2, terms, sub):
    quarter, share = pieces[0].shape
    rows, width = packs[0].shape
    at_quarter = pl.BlockSpec((quarter, width), lambda i, s: (s[0], 0))
    return one_step(
        mid2_kernel,
        (head_no, *pieces, *packs, middle, g, gain2, *terms, sub),
        [whole_block(quarter, share)] * 4
        + [whole_block(rows, width)] * 4
        + [whole_block(quarter, width), at_quarter, whole_block(1, width)]
        + [whole_block(*t.shape) for t in terms]
        + [whole_block(*sub.shape)],
        [struct((quarter, width), f32)]
        + [struct((quarter, width + k * share), bf16) for k in (1, 2)]
        + [struct((quarter, share), bf16)] * 4
        + [struct((8, width), f32), struct((8, share), f32)],
        "mid2",
        2 * quarter * width * width,
        56,
    )


def deal_kernel(sc, up, down, *outs):
    rows = up.shape[0] // 8
    cols = up.shape[1] // 2

    def piece(out, at, k, right):
        for m, ref in enumerate((up, down)):
            rows_of = pl.ds(pl.multiple_of(sc[SC + k] * rows, rows), rows)
            out[at + m * rows : at + (m + 1) * rows, :] = ref[rows_of, right * cols : (right + 1) * cols]

    for k in range(7):
        piece(outs[k], 0, k, 0)
        piece(outs[k], 2 * rows, k, 1)
    piece(outs[7], 0, 7, 0)
    piece(outs[8], 0, 7, 1)


def deal(sc, up, down):
    rows, cols = up.shape[0] // 8, up.shape[1] // 2
    return one_step(
        deal_kernel,
        (sc, up, down),
        [whole_block(*up.shape)] * 2,
        [struct((4 * rows, cols), bf16)] * 7 + [struct((2 * rows, cols), bf16)] * 2,
        "deal",
        1 << 28,
    )


def spread_kernel(sc, *refs):
    parts, (gq, gk, gv, go, gu, gd) = refs[:18], refs[18:]
    rows = 2 * parts[0].shape[0] // 3

    def put(out, at, value):
        out[pl.ds(pl.multiple_of(at, 8), value.shape[0]), :] = value

    def place(d, first, value):
        last = first + value.shape[0]
        for m in range(3):
            lo, hi = max(first, m * rows), min(last, (m + 1) * rows)
            if lo >= hi:
                continue
            some = value[lo - first : hi - first]
            if m:
                put((gu, gd)[m - 1], d * rows + lo - m * rows, some)
                continue
            which = (d & 1) * 2 + ((d >> 1) & 1)
            for k, out in enumerate((gq, gk, gv, go)):

                @pl.when(which == k)
                def _():
                    put(out, (d >> 2) * rows + lo, some)

    for k in range(7):
        for m in range(2):
            part = parts[2 * k + m]
            place(sc[SC + k], m * part.shape[0], part[...].astype(f32))
    size = parts[14].shape[0]
    for n, first in enumerate((0, 2, 1, 3)):
        place(sc[SC + 7], first * size, parts[14 + n][...].astype(f32))


def spread(sc, tiles, hidden):
    tiles = [part for tile in tiles for part in tile]
    width = tiles[0].shape[1]
    share = width // 4
    outs = [struct((share, width), f32)] * 4 + [
        struct((width, hidden), f32),
        struct((hidden, width), f32),
    ]
    return one_step(
        spread_kernel,
        (sc, *tiles),
        [whole_block(*t.shape) for t in tiles],
        outs,
        "spread",
        1 << 30,
    )


def shards(
    layer_input, ln1_gain, ln1_bias, w_query, b_query, w_key, w_value, b_value, sub_gain, sub_bias,
    w_out, b_out, ln2_gain, ln2_bias, w_up, b_up, w_down, b_down, cotangent, row_lengths,
):
    rows_local, slice_width = layer_input.shape
    head_share = w_query.shape[1]
    local_heads = head_share // HEAD_DIM
    head_pos = lax.axis_index("head")
    seq_pos = lax.axis_index("seq")
    n_seq = lax.axis_size("seq")
    width = head_share * lax.axis_size("head")
    quarter = rows_local // 4
    relative = jnp.stack([head_pos, head_pos ^ 1, head_pos ^ 2, head_pos ^ 3]).astype(jnp.int32)
    row2 = lambda v: v.reshape(1, -1)

    input_whole = lax.all_gather(layer_input, "head", axis=1, tiled=True)
    hat1, rs1 = norm_parts(input_whole.astype(f32))
    normed = (hat1 * ln1_gain + ln1_bias).astype(bf16)
    pair = lambda a, b: jnp.stack(
        [a.reshape(-1, local_heads, HEAD_DIM), b.reshape(-1, local_heads, HEAD_DIM)], axis=2
    ).reshape(-1, 2 * head_share)
    w_kv = pair(w_key, w_value)
    b_kv = pair(jnp.zeros_like(b_value), b_value)
    kv = (dot(normed, w_kv) + b_kv).astype(bf16)
    queries = (dot(normed, w_query) + b_query).astype(bf16)

    feats, nf, sc = features(rows_local * n_seq, row_lengths, local_heads, rows_local)
    kv, cotangent, pack_in = lax.optimization_barrier((kv, cotangent, (w_out, sub_gain, sub_bias)))
    if n_seq == 8:
        (att, lse, *msgs), kv_tiles, g_whole, packs = ring_attend(
            queries, feats, nf, kv, sc, cotangent, pack_in, head_pos
        )
    else:
        kv_tiles = lax.all_gather(kv, "seq", axis=0)
        att, lse, *msgs = attend_fwd(queries, feats, nf, kv_tiles, sc, n_seq)
        g_whole, packs = head_columns(head_whole(cotangent), head_pos), head_whole(out_pack(*pack_in))

    pieces = head_pieces(*msgs)
    nm, middle, sub = mid1(
        relative, pieces, packs, input_whole, row2(b_out), row2(ln2_gain), row2(ln2_bias)
    )
    nms = head_pieces(nm, nm, nm, nm)
    *held, out0, out1, dn0, dn1 = ffn(
        relative, 0, nms[:2], g_whole, w_up, w_down, row2(b_up), []
    )
    nm_all, act, d_inner, out2, out3, dn2, dn3 = ffn(
        relative, 1, nms[2:], g_whole, w_up, w_down, row2(b_up), held
    )
    outs, dn = (out0, out1, out2, out3), head_pieces(dn0, dn1, dn2, dn3)
    gw_up = dot(nm_all, d_inner, TN).astype(bf16)
    gw_down = dot(act, g_whole, TN).astype(bf16)
    early = deal(sc, gw_up, gw_down) if n_seq == 8 else (gw_up, gw_down)
    early, dn = lax.optimization_barrier((early, dn))
    d_mid, for_core, for_cross, *d_msgs, vec768, vec192 = mid2(
        relative, pieces, packs, middle, g_whole, row2(ln2_gain), dn, sub
    )
    d_pieces = head_pieces(*d_msgs)
    beside = (sub[0], for_core, for_cross)

    if n_seq == 8:
        dq, dkv, beside, early = ring_attend_back(
            queries, feats, nf, kv_tiles, d_pieces, att, lse, sc, beside, early
        )
    else:
        dq, dkv_tiles = attend_bwd(queries, feats, nf, d_pieces, att, lse, kv_tiles, sc, n_seq)
        dkv = lax.psum_scatter(dkv_tiles, "seq", scatter_dimension=0, tiled=False)
        cross = lax.ppermute(for_cross, "head", CROSS)
        beside = sub[0], lax.ppermute(for_core, "head", CORE), cross, lax.ppermute(cross, "head", CORE)
        gw_up, gw_down = lax.psum(early, "seq")
    own_sub, near, far, both = beside
    dbr_all = jnp.concatenate([for_core[:, :width]] + [v[:, :width] for v in (near, far, both)], axis=0)
    far_at, both_at = width + head_share, width + 2 * head_share
    sub_all = jnp.concatenate(
        [own_sub, near[:, width:], far[:, width:far_at], both[:, far_at:both_at]], axis=0
    )

    gw_out = dot(sub_all, dbr_all, TN).astype(bf16)
    gw_query = dot(dq, normed, TN).astype(bf16)
    gb_out = jnp.sum(dbr_all.astype(f32), axis=0)
    gb_up = jnp.sum(d_inner.astype(f32), axis=0)
    gb_down = jnp.sum(g_whole.astype(f32), axis=0)
    gw_kv = dot(dkv, normed, TN).astype(bf16).reshape(local_heads, 2, HEAD_DIM, width)
    gw_kv = jnp.concatenate([gw_kv[:, k].reshape(head_share, width) for k in range(2)], axis=0)
    late = jnp.concatenate([gw_query, gw_kv, gw_out], axis=0)
    late, dkv = lax.optimization_barrier((late, dkv))
    dn = dot(dq, w_query, NT) + dot(dkv, w_kv, NT)
    gb_kv = jnp.sum(dkv.astype(f32), axis=0)
    gb_qkv = jnp.concatenate([jnp.sum(dq.astype(f32), axis=0), gb_kv])
    split = lambda v: jnp.sum(
        jnp.where(relative[:, None, None] == jnp.arange(4)[None, :, None], v[:, None, :], 0.0), axis=0
    ).reshape(-1)
    fill = lambda v: jnp.concatenate([v, jnp.zeros((width - v.shape[0],), f32)])
    small = jnp.stack(
        [
            jnp.sum(dn * hat1, axis=0),
            jnp.sum(dn, axis=0),
            vec768[0],
            vec768[1],
            split(vec192[:4]),
            split(vec192[4:]),
        ]
    )
    more = jnp.stack([gb_up, gb_down, gb_out, fill(gb_qkv)])
    dn = dn.astype(bf16).reshape(2, 2, quarter, width)
    core, chip = head_pos % 2, head_pos // 2
    mine = lax.dynamic_index_in_dim(dn, core, 1, False)
    mate = lax.dynamic_index_in_dim(dn, 1 - core, 1, False)
    hold = lax.optimization_barrier

    if n_seq == 8:
        late = halve(late, 1)
        small = small + lax.ppermute(small, "head", CORE)
        small = small + lax.ppermute(small, "head", CROSS)
        late, small, more, mine, mate = hold((late, small, more, mine, mate))
        mate = lax.ppermute(mate, "head", CORE)
        small = jnp.concatenate([small, more], axis=0)
        small = small + lax.ppermute(small, "seq", exchange(1))
        late = halve(late, 2)
        mine = add_low(mine, mate)
        late, mine, small = hold((late, mine, small))
        far = lax.ppermute(lax.dynamic_index_in_dim(mine, 1 - chip, 0, False), "head", CROSS)
        small = small + lax.ppermute(small, "seq", exchange(2))
        late = halve(late, 4)
        tile = jnp.concatenate([late, early], axis=0)
        half = tile.shape[0] // 2
        tile, small, outs = hold((tile, small, outs))
        a = [tile[:half], tile[half:]]
        b, tiles = a, [a]
        for step in range(3):
            if step == 1:
                a[1], small, outs = hold((a[1], small, outs))
                small = small + lax.ppermute(small, "seq", exchange(4))
                core_terms = [lax.ppermute(outs[k], "head", CORE) for k in (1, 3)]
                cross_term = lax.ppermute(add_low(outs[2], core_terms[1]), "head", CROSS)
                outs = outs[0], core_terms[0], cross_term
            a = [lax.ppermute(v, "seq", FWD) for v in a]
            b = [lax.ppermute(v, "seq", BWD) for v in b]
            tiles += [a, b]
        tiles.append([lax.ppermute(v[: half // 2], "seq", FWD) for v in a])
        tiles.append([lax.ppermute(v[half // 2 :], "seq", BWD) for v in b])
        gw_query, gw_key, gw_value, gw_out, gw_up, gw_down = spread(sc, tiles, w_up.shape[1])
    else:
        mine = add_low(mine, lax.ppermute(mate, "head", CORE))
        far = lax.ppermute(lax.dynamic_index_in_dim(mine, 1 - chip, 0, False), "head", CROSS)
        small = small + lax.ppermute(small, "head", CORE)
        small = small + lax.ppermute(small, "head", CROSS)
        small = lax.psum(jnp.concatenate([small, more], axis=0), "seq")
        outs = head_pieces(*outs)
        late = lax.psum(late, "seq").astype(f32)
        gw_query, gw_key, gw_value, gw_out = (
            late[k * head_share : (k + 1) * head_share] for k in range(4)
        )
        gw_up, gw_down = gw_up.astype(f32), gw_down.astype(f32)

    y = middle + (sum(t.astype(f32) for t in outs) + b_down)
    dn = lax.dynamic_index_in_dim(mine, chip, 0, False).astype(f32) + far.astype(f32)
    cut = lambda v: lax.dynamic_slice_in_dim(v, head_pos * quarter, quarter, 0)
    d_in = d_mid + norm_back(dn * ln1_gain, cut(hat1), cut(rs1))
    both = lax.all_to_all(jnp.stack([y, d_in]).astype(bf16), "head", 2, 1, tiled=True)
    layer_output, grad_input = both[0], both[1].astype(f32)

    gb_qkv = small[9]
    own = lambda v: lax.dynamic_slice_in_dim(v, head_pos * head_share, head_share, 0)
    gb_value = gb_qkv[head_share : 3 * head_share].reshape(local_heads, 2, HEAD_DIM)[:, 1].reshape(-1)
    return (
        layer_output,
        grad_input,
        small[0],
        small[1],
        gw_query.T,
        gb_qkv[:head_share],
        gw_key.T,
        gw_value.T,
        gb_value,
        own(small[4]),
        own(small[5]),
        gw_out,
        small[8],
        small[2],
        small[3],
        gw_up,
        small[6],
        gw_down,
        small[7],
    )


def solution(mesh):
    cols, rows, both, shared, vec = P(None, "head"), P("head", None), P("seq", "head"), P(), P("head")
    in_specs = (
        both, shared, shared, cols, vec, cols, cols, vec, vec, vec,
        rows, shared, shared, shared, cols, vec, rows, shared, both, shared,
    )
    out_specs = (
        both, both, shared, shared, cols, vec, cols, cols, vec, vec,
        vec, rows, shared, shared, shared, cols, vec, rows, shared,
    )
    return jax.shard_map(shards, mesh=mesh, in_specs=in_specs, out_specs=out_specs, check_vma=False)
```

```python
import functools

import jax
import jax.numpy as jnp
import numpy as np
from jax import lax
from jax.experimental import pallas as pl
from jax.experimental.pallas import tpu as pltpu
from jax.sharding import PartitionSpec as P

HEAD_DIM = 64
SEG = 2048
eps = 1e-05
segment_scales = (1, 2, 4, 8, 16)
dilation_steps = (1, 2, 4, 6, 12)
bf16 = jnp.bfloat16
f32 = jnp.float32
NT = (((1,), (1,)), ((), ()))
NN = (((1,), (0,)), ((), ()))
TN = (((0,), (0,)), ((), ()))

RING = (0, 2, 4, 6, 7, 5, 3, 1)
FWD = [(RING[i], RING[(i + 1) % 8]) for i in range(8)]
BWD = [(b, a) for a, b in FWD]
CORE = [(0, 1), (1, 0), (2, 3), (3, 2)]
CROSS = [(0, 2), (2, 0), (1, 3), (3, 1)]
BOTH = [(0, 3), (3, 0), (1, 2), (2, 1)]


def dot(a, b, dims=NN):
    return lax.dot_general(a, b, dims, preferred_element_type=f32)


def add_low(u, v):
    return (u.astype(f32) + v.astype(f32)).astype(u.dtype)


def exchange(step):
    return [(i, i ^ step) for i in range(8)]


def halve(x, step):
    half = x.shape[0] // 2
    bit = (lax.axis_index("seq") // step) % 2
    keep = lax.dynamic_slice_in_dim(x, bit * half, half, 0)
    send = lax.dynamic_slice_in_dim(x, (1 - bit) * half, half, 0)
    return add_low(keep, lax.ppermute(send, "seq", exchange(step)))


def head_pieces(own, core, cross, both):
    return (
        own,
        lax.ppermute(core, "head", CORE),
        lax.ppermute(cross, "head", CROSS),
        lax.ppermute(both, "head", BOTH),
    )


def head_whole(x):
    p = lax.ppermute(x, "head", CROSS)
    return x, lax.ppermute(x, "head", CORE), p, lax.ppermute(p, "head", CORE)


def head_columns(got, head_pos):
    return jnp.concatenate([lax.select_n(head_pos ^ k, *got) for k in range(4)], axis=1)


SC = 6


def feature_table(total, nrow, nh, n_head):
    sizes = [nrow + total // (SEG * scale) for scale in segment_scales]
    nf = sum(sizes)
    width = -(-nh * nf // 128) * 128
    table = np.zeros((-(-(4 + n_head) // 8) * 8, width), np.int32)
    table[3] = -1
    for h in range(nh):
        lane = h * nf
        for scale, step, size in zip(segment_scales, dilation_steps, sizes):
            at = slice(lane, lane + size)
            table[0, at] = (SEG * scale).bit_length() - 1
            table[1, at] = SEG * scale - 1
            table[2, at] = lane
            table[3, at] = np.arange(lane, lane + size)
            for d in range(n_head):
                table[4 + d, at] = sum(1 << b for b in range(12) if b % step == (d * nh + h) % step)
            lane += size
    return table, nf


def feature_kernel(n, nrow, bk, lengths, table, out, sc, seg_ref, place_ref):
    block = pl.program_id(0)
    width = out.shape[1]
    seq_pos, head_pos = lax.axis_index("seq"), lax.axis_index("head")
    ends, end, row_begin = [], 0, 0
    for r in range(nrow):
        end = end + lengths[r]
        ends.append(end)
        row_begin = jnp.where(end <= seq_pos * bk, end, row_begin)

    @pl.when(block == 0)
    def _():
        sc[0] = seq_pos
        sc[1] = row_begin
        for r in range(4):
            sc[2 + r] = head_pos ^ r
        pos = sum(jnp.where(seq_pos == d, k, 0) for k, d in enumerate(RING))
        for k in range(n):
            if n == 8:
                at = (pos + (0, 7, 1, 6, 2, 5, 3, 4)[k]) & 7
                sc[SC + k] = sum(jnp.where(at == m, d, 0) for m, d in enumerate(RING))
            else:
                sc[SC + k] = k

    shift, mask, first, own = (table[k : k + 1, :] for k in range(4))
    residues = table[pl.ds(4 + head_pos, 1), :]
    pieces = [(lengths[r] + mask) >> shift for r in range(nrow)]

    def one(k, carry):
        tile = block * (out.shape[0] // bk) + k

        @pl.when((tile <= seq_pos) & ((tile + 1) * bk > row_begin))
        def _():
            pos = tile * bk + lax.broadcasted_iota(jnp.int32, (bk, width), 0)
            start, base = 0, first
            for r in range(nrow):
                passed = ends[r] <= tile * bk
                start = jnp.where(passed, ends[r], start)
                base = base + jnp.where(passed, pieces[r], 0)
            seg_ref[...] = jnp.broadcast_to(base, (bk, width))
            place_ref[...] = pos - start
            for r in range(nrow):

                @pl.when((ends[r] > tile * bk) & (ends[r] < (tile + 1) * bk))
                def _():
                    past = pos >= ends[r]
                    place_ref[...] = jnp.where(past, pos - ends[r], place_ref[...])
                    seg_ref[...] += jnp.where(past, pieces[r], 0)

            place = place_ref[...]
            seg = seg_ref[...] + (place >> shift)
            part = place & mask
            whole = ((part.astype(f32) + 0.5) * np.float32(1 / 12)).astype(jnp.int32)
            on = (residues >> (part - 12 * whole)) & 1
            out[pl.ds(pl.multiple_of(k * bk, bk), bk), :] = (
                jnp.where(seg == own, on, 0).astype(f32).astype(bf16)
            )

        return carry

    lax.fori_loop(0, out.shape[0] // bk, one, 0)


def features(total, lengths, nh, bk):
    n = total // bk
    nrow = lengths.shape[0]
    table, nf = feature_table(total, nrow, nh, lax.axis_size("head"))
    width = table.shape[1]
    block = 8 * bk if n % 8 == 0 else bk
    feats, sc = pl.pallas_call(
        functools.partial(feature_kernel, n, nrow, bk),
        grid_spec=pltpu.PrefetchScalarGridSpec(
            num_scalar_prefetch=1,
            grid=(total // block,),
            in_specs=[pl.BlockSpec(table.shape, lambda i, s: (0, 0))],
            out_specs=[
                pl.BlockSpec((block, width), lambda i, s: (i, 0)),
                pl.BlockSpec(memory_space=pltpu.SMEM),
            ],
            scratch_shapes=[pltpu.VMEM((bk, width), jnp.int32)] * 2,
        ),
        out_shape=[
            jax.ShapeDtypeStruct((total, width), bf16),
            jax.ShapeDtypeStruct((SC + n,), jnp.int32),
        ],
        compiler_params=pltpu.CompilerParams(
            dimension_semantics=("arbitrary",), vmem_limit_bytes=16 << 20
        ),
        name="features",
    )(lengths, jnp.asarray(table))
    return feats, nf, sc


def head_pad(x, h, upper):
    part = x[:, HEAD_DIM * h : HEAD_DIM * (h + 1)]
    zero = jnp.zeros_like(part)
    return jnp.concatenate([zero, part] if upper else [part, zero], axis=1)


def count_tile(fk, fq, h, nf, first_key, first_row):
    lane = lax.broadcasted_iota(jnp.int32, fq.shape, 1)
    fqh = jnp.where((lane >= h * nf) & (lane < (h + 1) * nf), fq.astype(f32), 0.0).astype(bf16)
    count = dot(fk, fqh, NT)
    keys = first_key + lax.broadcasted_iota(jnp.int32, (count.shape[0], 1), 0)
    rows = first_row + lax.broadcasted_iota(jnp.int32, (1, count.shape[1]), 1)
    return jnp.where(keys <= rows, count, 0.0)


def fwd_tile(nh, nf, q, fq, kv, fk, first_key, first_row, acc, m, l):
    kv_t = kv[...].astype(f32).T.astype(bf16)
    qs = (q[...].astype(f32) * HEAD_DIM**-0.5).astype(bf16)
    for h in range(nh):
        s = dot(kv[:, 128 * h : 128 * h + 128], head_pad(qs, h, False), NT)
        count = count_tile(fk[...], fq[...], h, nf, first_key, first_row)
        s = jnp.where(count > 0, s, -1e30)
        old = m[h : h + 1, :]
        new = jnp.maximum(old, jnp.max(s, axis=0, keepdims=True))
        p = count * jnp.exp(s - new)
        factor = jnp.exp(old - new)
        l[h : h + 1, :] = l[h : h + 1, :] * factor + jnp.sum(p, axis=0, keepdims=True)
        o = dot(kv_t[128 * h : 128 * h + 128], p.astype(bf16))
        acc[64 * h : 64 * h + 64, :] = acc[64 * h : 64 * h + 64, :] * factor + o[64:, :]
        m[h : h + 1, :] = new


def bwd_tile(nh, nf, q, fq, do, lse, dterm, kv, fk, first_key, first_row, dq_t):
    kv_t = kv[...].astype(f32).T.astype(bf16)
    qs = (q[...].astype(f32) * HEAD_DIM**-0.5).astype(bf16)
    out = []
    for h in range(nh):
        kvh = kv[:, 128 * h : 128 * h + 128]
        qh = head_pad(qs, h, False)
        doh = head_pad(do[...], h, True)
        count = count_tile(fk[...], fq[...], h, nf, first_key, first_row)
        p = count * jnp.exp(jnp.minimum(dot(kvh, qh, NT) - lse[h : h + 1, :], 1.0))
        ds = (p * (dot(kvh, doh, NT) - dterm[h : h + 1, :])).astype(bf16)
        out.append((dot(ds, qh) + dot(p.astype(bf16), doh)).astype(bf16))
        o = dot(kv_t[128 * h : 128 * h + 128], ds)
        dq_t[64 * h : 64 * h + 64, :] += o[:64, :]
    return out


def fwd_start(acc, m, l):
    acc[...] = jnp.zeros_like(acc)
    m[...] = jnp.full_like(m, -1e30)
    l[...] = jnp.zeros_like(l)


def fwd_end(nh, quarters, acc, m, l, out, lse, msgs):
    for h in range(nh):
        out[:, 64 * h : 64 * h + 64] = (acc[64 * h : 64 * h + 64, :] / l[h : h + 1, :]).T
    lse[...] = m[...] + jnp.log(jnp.maximum(l[...], 1e-30))
    rows = msgs[0].shape[0]
    for at, msg in zip(quarters, msgs):
        msg[...] = out[pl.ds(pl.multiple_of(at * rows, rows), rows), :].astype(bf16)


def bwd_start(nh, quarters, pieces, att, do, dterm, dq_t):
    dq_t[...] = jnp.zeros_like(dq_t)
    rows = pieces[0].shape[0]
    for at, piece in zip(quarters, pieces):
        do[pl.ds(pl.multiple_of(at * rows, rows), rows), :] = piece[...]
    prod = do[...].astype(f32) * att[...]
    r = lax.broadcasted_iota(jnp.int32, (8, prod.shape[1]), 0)
    c = lax.broadcasted_iota(jnp.int32, (8, prod.shape[1]), 1)
    pick = jnp.where(c // HEAD_DIM == r, 1.0, 0.0).astype(f32)
    dterm[...] = lax.dot_general(
        pick, prod, NT, precision=lax.Precision.HIGHEST, preferred_element_type=f32
    )


def tile_needed(tile, sc, bk):
    return (tile <= sc[0]) & ((tile + 1) * bk > sc[1])


def fwd_grid(nh, nf, n, sc, q, fq, kv, fk, out, lse, m0, m1, m2, m3, acc, m, l):
    i = pl.program_id(0)
    bk = kv.shape[1]

    @pl.when(i == 0)
    def _():
        fwd_start(acc, m, l)

    @pl.when(tile_needed(sc[SC + i], sc, bk))
    def _():
        fwd_tile(nh, nf, q, fq, kv.at[0], fk, sc[SC + i] * bk, sc[0] * q.shape[0], acc, m, l)

    @pl.when(i == n - 1)
    def _():
        fwd_end(nh, [sc[2 + r] for r in range(4)], acc, m, l, out, lse, (m0, m1, m2, m3))


def bwd_grid(nh, nf, n, sc, q, fq, d0, d1, d2, d3, att, lse, kv, fk, dq, dkv, do, dterm, dq_t):
    i = pl.program_id(0)
    bk = kv.shape[1]

    @pl.when(i == 0)
    def _():
        bwd_start(nh, [sc[2 + r] for r in range(4)], (d0, d1, d2, d3), att, do, dterm, dq_t)

    need = tile_needed(sc[SC + i], sc, bk)

    @pl.when(jnp.logical_not(need))
    def _():
        dkv[...] = jnp.zeros_like(dkv)

    @pl.when(need)
    def _():
        out = bwd_tile(
            nh, nf, q, fq, do, lse, dterm, kv.at[0], fk, sc[SC + i] * bk, sc[0] * q.shape[0], dq_t
        )
        for h in range(nh):
            dkv[0, :, 128 * h : 128 * h + 128] = out[h]

    @pl.when(i == n - 1)
    def _():
        dq[...] = (dq_t[...].T * HEAD_DIM**-0.5).astype(dq.dtype)


def whole_block(*shape):
    return pl.BlockSpec(shape, lambda i, s: (0,) * len(shape))


def struct(shape, dtype):
    return jax.ShapeDtypeStruct(shape, dtype)


def params(mib=16):
    return pltpu.CompilerParams(
        dimension_semantics=("arbitrary",), vmem_limit_bytes=mib << 20
    )


def fwd_outs(tq, wd):
    return [struct((tq, wd), f32), struct((8, tq), f32)] + [struct((tq // 4, wd), bf16)] * 4


def attend_fwd(q, feats, nf, kv, sc, n):
    tq, wd = q.shape
    bk, width = kv.shape[1], feats.shape[1]
    outs = fwd_outs(tq, wd)
    return pl.pallas_call(
        functools.partial(fwd_grid, wd // HEAD_DIM, nf, n),
        grid_spec=pltpu.PrefetchScalarGridSpec(
            num_scalar_prefetch=1,
            grid=(n,),
            in_specs=[
                whole_block(tq, wd),
                pl.BlockSpec((tq, width), lambda i, s: (s[0], 0)),
                pl.BlockSpec((1, bk, 2 * wd), lambda i, s: (i, 0, 0)),
                pl.BlockSpec((bk, width), lambda i, s: (s[SC + i], 0)),
            ],
            out_specs=[whole_block(*o.shape) for o in outs],
            scratch_shapes=[
                pltpu.VMEM((wd, tq), f32),
                pltpu.VMEM((8, tq), f32),
                pltpu.VMEM((8, tq), f32),
            ],
        ),
        out_shape=outs,
        compiler_params=params(),
        name="attend_fwd",
    )(sc, q, feats, kv, feats)


def attend_bwd(q, feats, nf, pieces, att, lse, kv, sc, n):
    tq, wd = q.shape
    bk, width = kv.shape[1], feats.shape[1]
    return pl.pallas_call(
        functools.partial(bwd_grid, wd // HEAD_DIM, nf, n),
        grid_spec=pltpu.PrefetchScalarGridSpec(
            num_scalar_prefetch=1,
            grid=(n,),
            in_specs=[whole_block(tq, wd), pl.BlockSpec((tq, width), lambda i, s: (s[0], 0))]
            + [whole_block(tq // 4, wd)] * 4
            + [
                whole_block(tq, wd),
                whole_block(8, tq),
                pl.BlockSpec((1, bk, 2 * wd), lambda i, s: (i, 0, 0)),
                pl.BlockSpec((bk, width), lambda i, s: (s[SC + i], 0)),
            ],
            out_specs=[whole_block(tq, wd), pl.BlockSpec((1, bk, 2 * wd), lambda i, s: (i, 0, 0))],
            scratch_shapes=[
                pltpu.VMEM((tq, wd), bf16),
                pltpu.VMEM((8, tq), f32),
                pltpu.VMEM((wd, tq), f32),
            ],
        ),
        out_shape=[struct((tq, wd), bf16), struct(kv.shape, bf16)],
        compiler_params=params(),
        name="attend_bwd",
    )(sc, q, feats, *pieces, att, lse, kv, feats)


def fwd_part(nh, nf, tiles, bk, first, last, sc, *refs):
    q, fq = refs[:2]
    n = len(tiles)
    kvs, fks = refs[2 : 2 + n], refs[2 + n : 2 + 2 * n]
    rest = refs[2 + 2 * n :]
    if not first:
        rest = rest[3:]
    if last:
        out, lse, *msgs = rest[:6]
        acc, m, l = rest[6:9]
    else:
        acc, m, l = rest[:3]
    if first:
        fwd_start(acc, m, l)
    for (place, rows, offset), kv, fk in zip(tiles, kvs, fks):

        @pl.when(tile_needed(sc[SC + place], sc, bk))
        def _():
            fwd_tile(
                nh, nf, q, fq, kv, fk, sc[SC + place] * bk + offset, sc[0] * q.shape[0], acc, m, l
            )

    if last:
        fwd_end(nh, [sc[2 + r] for r in range(4)], acc, m, l, out, lse, msgs)


def attend_fwd_part(q, feats, nf, kvs, tiles, state, sc, last):
    tq, wd = q.shape
    width = feats.shape[1]
    n = len(tiles)
    sums = [struct((wd, tq), f32), struct((8, tq), f32), struct((8, tq), f32)]
    ins = [whole_block(tq, wd), pl.BlockSpec((tq, width), lambda i, s: (s[0], 0))]
    ins += [whole_block(*kv.shape) for kv in kvs]
    for place, rows, offset in tiles:
        at = lambda i, s, p=place, k=tq // rows, o=offset // rows: (s[SC + p] * k + o, 0)
        ins.append(pl.BlockSpec((rows, width), at))
    args = [sc, q, feats, *kvs, *([feats] * n)]
    outs = (fwd_outs(tq, wd) if last else []) + sums
    alias = {}
    if state is not None:
        ins += [whole_block(*o.shape) for o in sums]
        alias = {len(args) + k: len(outs) - 3 + k for k in range(3)}
        args += state

    def kernel(sc_ref, *refs):
        if state is not None:
            olds = refs[2 + 2 * n : 5 + 2 * n]
            news = refs[len(refs) - 3 :]
            for old, new in zip(olds, news):
                new[...] = old[...]
        fwd_part(wd // HEAD_DIM, nf, tiles, tq, state is None, last, sc_ref, *refs)

    got = pl.pallas_call(
        kernel,
        grid_spec=pltpu.PrefetchScalarGridSpec(
            num_scalar_prefetch=1,
            grid=(1,),
            in_specs=ins,
            out_specs=[whole_block(*o.shape) for o in outs],
        ),
        out_shape=outs,
        input_output_aliases=alias,
        compiler_params=params(),
        cost_estimate=pl.CostEstimate(flops=n << 31, bytes_accessed=n << 20, transcendentals=0),
        name="fwd_part",
    )(*args)
    return got[:6] if last else got


def attend_bwd_part(q, feats, nf, kvs, tiles, lse, sc, start, state, last):
    tq, wd = q.shape
    nh = wd // HEAD_DIM
    width = feats.shape[1]
    n = len(tiles)
    held = [struct((tq, wd), bf16), struct((8, tq), f32), struct((wd, tq), f32)]
    ins = [whole_block(tq, wd), pl.BlockSpec((tq, width), lambda i, s: (s[0], 0)), whole_block(8, tq)]
    ins += [whole_block(*kv.shape) for kv in kvs]
    for place, rows, offset in tiles:
        at = lambda i, s, p=place, k=tq // rows, o=offset // rows: (s[SC + p] * k + o, 0)
        ins.append(pl.BlockSpec((rows, width), at))
    args = [sc, q, feats, lse, *kvs, *([feats] * n)]
    outs = [struct(kv.shape, bf16) for kv in kvs]
    more = start if start is not None else state
    ins += [whole_block(*v.shape) for v in more]
    args += more
    if start is not None:
        outs = outs + held
    elif not last:
        outs = outs + held[2:]
    if last:
        outs = outs + [struct((tq, wd), bf16)]
    scratch = [pltpu.VMEM((wd, tq), f32)] if last else []

    def kernel(sc_ref, *refs):
        q_ref, fq, lse_ref = refs[:3]
        kv_refs, fks = refs[3 : 3 + n], refs[3 + n : 3 + 2 * n]
        given = refs[3 + 2 * n : 3 + 2 * n + len(more)]
        rest = refs[3 + 2 * n + len(more) :]
        dkvs, rest = rest[:n], rest[n:]
        if start is not None:
            do, dterm, dq_t = rest[:3]
            bwd_start(nh, [sc_ref[2 + r] for r in range(4)], given[:4], given[4], do, dterm, dq_t)
        else:
            do, dterm, old = given
            dq_t = rest[-1] if last else rest[0]
            dq_t[...] = old[...]
        for (place, rows, offset), kv, fk, dkv in zip(tiles, kv_refs, fks, dkvs):
            need = tile_needed(sc_ref[SC + place], sc_ref, tq)

            @pl.when(jnp.logical_not(need))
            def _():
                dkv[...] = jnp.zeros_like(dkv)

            @pl.when(need)
            def _():
                got = bwd_tile(
                    nh, nf, q_ref, fq, do, lse_ref, dterm, kv, fk,
                    sc_ref[SC + place] * tq + offset, sc_ref[0] * tq, dq_t,
                )
                for h in range(nh):
                    dkv[:, 128 * h : 128 * h + 128] = got[h]

        if last:
            rest[0][...] = (dq_t[...].T * HEAD_DIM**-0.5).astype(bf16)

    return pl.pallas_call(
        kernel,
        grid_spec=pltpu.PrefetchScalarGridSpec(
            num_scalar_prefetch=1,
            grid=(1,),
            in_specs=ins,
            out_specs=[whole_block(*o.shape) for o in outs],
            scratch_shapes=scratch,
        ),
        out_shape=outs,
        compiler_params=params(56 if start is not None else 16),
        cost_estimate=pl.CostEstimate(flops=n << 31, bytes_accessed=n << 20, transcendentals=0),
        name="bwd_part",
    )(*args)


def ring_attend(q, feats, nf, kv, sc, g, pack_in, head_pos):
    rows = kv.shape[0]
    half = rows // 2
    a = b = kv
    tiles, state = [kv], None
    whole = lambda p: (p, rows, 0)
    part = functools.partial(attend_fwd_part, q, feats, nf)
    for step in range(3):
        a2, b2 = lax.ppermute(a, "seq", FWD), lax.ppermute(b, "seq", BWD)
        if step == 0:
            state = part([kv], [whole(0)], None, sc, False)
        else:
            state = part([a, b], [whole(2 * step - 1), whole(2 * step)], state, sc, False)
        a, b, state = lax.optimization_barrier((a2, b2, state))
        if step == 0:
            a, b, g, pack_in = lax.optimization_barrier((a, b, g, pack_in))
            pack = out_pack(*pack_in)
            far_g, far_pack = (lax.ppermute(v, "head", CROSS) for v in (g, pack))
        if step == 2:
            a, b, far_g, far_pack = lax.optimization_barrier((a, b, far_g, far_pack))
            gs, packs = (
                [v, lax.ppermute(v, "head", CORE), w, lax.ppermute(w, "head", CORE)]
                for v, w in ((g, far_g), (pack, far_pack))
            )
        tiles += [a, b]
    c, d = lax.ppermute(a[:half], "seq", FWD), lax.ppermute(b[half:], "seq", BWD)
    g = head_columns(gs, head_pos)
    state = part([a, b], [whole(5), whole(6)], state, sc, False)
    tiles += [c, d]
    c, d, g, state = lax.optimization_barrier((c, d, g, state))
    return part([c, d], [(7, half, 0), (7, half, half)], state, sc, True), tiles, g, packs


def ring_attend_back(q, feats, nf, tiles, pieces, att, lse, sc, beside):
    rows = tiles[0].shape[0]
    half = rows // 2
    whole = lambda p: (p, rows, 0)
    part = functools.partial(attend_bwd_part, q, feats, nf)
    c, d, do, dterm, dq_t = part(
        tiles[7:9], [(7, half, 0), (7, half, half)], lse, sc, [*pieces, att], None, False
    )
    c, d, dq_t, (dbr, sub) = lax.optimization_barrier((c, d, dq_t, beside))
    a, b = lax.ppermute(c, "seq", FWD), lax.ppermute(d, "seq", BWD)
    for place in (5, 3, 1):
        given, at = tiles[place : place + 2], [whole(place), whole(place + 1)]
        if place == 3:
            t, u, own, dq_t = part(
                given + tiles[:1], at + [whole(0)], lse, sc, None, [do, dterm, dq_t], False
            )
        elif place == 5:
            t, u, dq_t = part(given, at, lse, sc, None, [do, dterm, dq_t], False)
        else:
            t, u, dq = part(given, at, lse, sc, None, [do, dterm, dq_t], True)
        if place == 5:
            up = jnp.concatenate([add_low(u[:half], a), u[half:]], axis=0)
            down = jnp.concatenate([t[:half], add_low(t[half:], b)], axis=0)
        else:
            up, down = add_low(u, a), add_low(t, b)
        if place == 1:
            up, down, beside = lax.optimization_barrier((up, down, beside))
        elif place == 3:
            up, down, dq_t = lax.optimization_barrier((up, down, dq_t))
        else:
            up, down, dq_t = lax.optimization_barrier((up, down, dq_t))
            beside = head_whole(dbr), head_pieces(*sub)
        a, b = lax.ppermute(up, "seq", FWD), lax.ppermute(down, "seq", BWD)
    return dq, (own.astype(f32) + a.astype(f32) + b.astype(f32)).astype(bf16), beside


VEC_ROWS = 16


def out_pack(w_out, sub_gain, sub_bias):
    width = w_out.shape[1]
    share = sub_gain.shape[0]
    room = width // 3
    pad = lambda v: jnp.concatenate([v, jnp.zeros((room - share,), f32)])
    vec = jnp.concatenate([pad(sub_gain), pad(sub_bias), jnp.zeros((room,), f32)]).reshape(1, width)
    high = vec.astype(bf16)
    rest = vec - lax.optimization_barrier(high).astype(f32)
    middle = rest.astype(bf16)
    low = (rest - lax.optimization_barrier(middle).astype(f32)).astype(bf16)
    top = jnp.concatenate([high, middle, low, jnp.zeros((VEC_ROWS - 3, width), bf16)], axis=0)
    return jnp.concatenate([top, w_out], axis=0)


def unpack_vec(w, row):
    v = w[0:VEC_ROWS, :].astype(f32)
    return v[row : row + 1] + v[row + 1 : row + 2] + v[row + 2 : row + 3]


def sub_parts(pieces, width):
    total = sum(jnp.sum(p, axis=1, keepdims=True) for p in pieces)
    square = sum(jnp.sum(p * p, axis=1, keepdims=True) for p in pieces)
    mean = total / width
    inv = lax.rsqrt(square / width - mean * mean + eps)
    return [(p - mean) * inv for p in pieces], inv


def norm_parts(x):
    center = x - jnp.mean(x, axis=1, keepdims=True)
    rs = lax.rsqrt(jnp.mean(center * center, axis=1, keepdims=True) + eps)
    return center * rs, rs


def norm_back(g, hat, rs):
    return rs * (
        g - jnp.mean(g, axis=1, keepdims=True) - hat * jnp.mean(g * hat, axis=1, keepdims=True)
    )


def mid1_kernel(sc, p0, p1, p2, p3, w0, w1, w2, w3, x, b_out, gain2, bias2, nm, middle, sub):
    share = p0.shape[1]
    room = w0.shape[1] // 3
    cen, _ = sub_parts([p[...].astype(f32) for p in (p0, p1, p2, p3)], w0.shape[1])
    acc = x[...].astype(f32) + b_out[...]
    for r, w in enumerate((w0, w1, w2, w3)):
        vec = unpack_vec(w, 0)
        s = (cen[r] * vec[:, :share] + vec[:, room : room + share]).astype(bf16)
        sub[r] = s
        acc = acc + dot(s, w[VEC_ROWS : VEC_ROWS + share, :])
    middle[...] = acc
    hat, _ = norm_parts(acc)
    nm[...] = (hat * gain2[...] + bias2[...]).astype(bf16)


def gelu_parts(z):
    half = 0.5 * (1.0 + lax.erf(z * np.float32(np.sqrt(0.5))))
    slope = half + z * (np.float32(1.0 / np.sqrt(2.0 * np.pi)) * jnp.exp(-0.5 * z * z))
    return z * half, slope


def ffn_kernel(pair, sc, n0, n1, g, w_up, w_down, b_up, *refs):
    nm, act, d_inner, *outs = refs[len(refs) - 7 :]
    rows = n0.shape[0]
    for k, piece in enumerate((n0, n1)):
        quarter = sc[2 * pair + k]
        at = pl.ds(pl.multiple_of((quarter & 1) * rows, rows), rows)
        x = piece[...]
        nm[at, :] = x
        a, slope = gelu_parts(dot(x, w_up[...]) + b_up[...])
        a = a.astype(bf16)
        g_rows = g[pl.ds(pl.multiple_of(quarter * rows, rows), rows), :]
        d = (dot(g_rows, w_down[...], NT) * slope).astype(bf16)
        act[at, :] = a
        d_inner[at, :] = d
        outs[k][...] = dot(a, w_down[...]).astype(bf16)
        outs[2 + k][...] = dot(d, w_up[...], NT).astype(bf16)


def mid2_kernel(sc, p0, p1, p2, p3, w0, w1, w2, w3, middle, g, gain2, t0, t1, t2, t3, *refs):
    d_mid, dbr, d0, d1, d2, d3, vec768, vec192 = refs
    share = p0.shape[1]
    width = w0.shape[1]
    dn = sum(t[...].astype(f32) for t in (t0, t1, t2, t3))
    hat, rs = norm_parts(middle[...])
    vec768[0:1, :] = jnp.sum(dn * hat, axis=0, keepdims=True)
    vec768[1:2, :] = jnp.sum(dn, axis=0, keepdims=True)
    dm = g[...].astype(f32) + norm_back(dn * gain2[...], hat, rs)
    d_mid[...] = dm
    branch = dm.astype(bf16)
    dbr[...] = branch
    cen, inv = sub_parts([p[...].astype(f32) for p in (p0, p1, p2, p3)], width)
    hats = []
    for r, w in enumerate((w0, w1, w2, w3)):
        ds = dot(branch, w[VEC_ROWS : VEC_ROWS + share, :], NT)
        vec192[r : r + 1, :] = jnp.sum(ds * cen[r], axis=0, keepdims=True)
        vec192[r + 4 : r + 5, :] = jnp.sum(ds, axis=0, keepdims=True)
        hats.append(ds * unpack_vec(w, 0)[:, :share])
    s1 = sum(jnp.sum(t, axis=1, keepdims=True) for t in hats) / width
    s2 = sum(jnp.sum(t * c, axis=1, keepdims=True) for t, c in zip(hats, cen)) / width
    for o, t, c in zip((d0, d1, d2, d3), hats, cen):
        o[...] = (inv * (t - s1 - c * s2)).astype(bf16)


def one_step(kernel, ins, in_specs, outs, name, flops, mib=16):
    return pl.pallas_call(
        kernel,
        grid_spec=pltpu.PrefetchScalarGridSpec(
            num_scalar_prefetch=1,
            grid=(1,),
            in_specs=in_specs,
            out_specs=[whole_block(*o.shape) for o in outs],
        ),
        out_shape=outs,
        compiler_params=params(mib),
        cost_estimate=pl.CostEstimate(flops=flops, bytes_accessed=12 << 20, transcendentals=0),
        name=name,
    )(*ins)


def mid1(head_no, pieces, packs, x, b_out, gain2, bias2):
    quarter, share = pieces[0].shape
    rows, width = packs[0].shape
    at_quarter = pl.BlockSpec((quarter, width), lambda i, s: (s[0], 0))
    return one_step(
        mid1_kernel,
        (head_no, *pieces, *packs, x, b_out, gain2, bias2),
        [whole_block(quarter, share)] * 4
        + [whole_block(rows, width)] * 4
        + [at_quarter]
        + [whole_block(1, width)] * 3,
        [struct((quarter, width), bf16), struct((quarter, width), f32), struct((4, quarter, share), bf16)],
        "mid1",
        2 * quarter * width * width,
    )


def ffn(head_no, pair, pieces, g, w_up, w_down, b_up, held):
    quarter, width = pieces[0].shape
    hidden = w_up.shape[1]
    ins = (head_no, *pieces, g, w_up, w_down, b_up)
    specs = [whole_block(*v.shape) for v in ins[1:]]
    outs = [struct((4 * quarter, k), bf16) for k in (width, hidden, hidden)]
    outs += [struct((quarter, width), bf16)] * 4
    at_chip = lambda k: pl.BlockSpec((2 * quarter, k), lambda i, s: (s[2 * pair] // 2, 0))
    return pl.pallas_call(
        functools.partial(ffn_kernel, pair),
        grid_spec=pltpu.PrefetchScalarGridSpec(
            num_scalar_prefetch=1,
            grid=(1,),
            in_specs=specs + [pl.BlockSpec(memory_space=pl.ANY)] * len(held),
            out_specs=[at_chip(o.shape[1]) for o in outs[:3]] + [whole_block(quarter, width)] * 4,
        ),
        out_shape=outs,
        input_output_aliases={len(ins) + k: k for k in range(len(held))},
        compiler_params=params(),
        cost_estimate=pl.CostEstimate(
            flops=16 * quarter * width * hidden, bytes_accessed=8 << 20, transcendentals=0
        ),
        name="ffn",
    )(*ins, *held)


def mid2(head_no, pieces, packs, middle, g, gain2, terms):
    quarter, share = pieces[0].shape
    rows, width = packs[0].shape
    at_quarter = pl.BlockSpec((quarter, width), lambda i, s: (s[0], 0))
    return one_step(
        mid2_kernel,
        (head_no, *pieces, *packs, middle, g, gain2, *terms),
        [whole_block(quarter, share)] * 4
        + [whole_block(rows, width)] * 4
        + [whole_block(quarter, width), at_quarter, whole_block(1, width)]
        + [whole_block(*t.shape) for t in terms],
        [struct((quarter, width), f32), struct((quarter, width), bf16)]
        + [struct((quarter, share), bf16)] * 4
        + [struct((8, width), f32), struct((8, share), f32)],
        "mid2",
        2 * quarter * width * width,
        56,
    )


def spread_kernel(sc, *refs):
    parts, (gq, gk, gv, go, gu, gd) = refs[:18], refs[18:]
    rows = 2 * parts[0].shape[0] // 3

    def put(out, at, value):
        out[pl.ds(pl.multiple_of(at, 8), value.shape[0]), :] = value

    def place(d, first, value):
        last = first + value.shape[0]
        for m in range(3):
            lo, hi = max(first, m * rows), min(last, (m + 1) * rows)
            if lo >= hi:
                continue
            some = value[lo - first : hi - first]
            if m:
                put((gu, gd)[m - 1], d * rows + lo - m * rows, some)
                continue
            which = (d & 1) * 2 + ((d >> 1) & 1)
            for k, out in enumerate((gq, gk, gv, go)):

                @pl.when(which == k)
                def _():
                    put(out, (d >> 2) * rows + lo, some)

    for k in range(7):
        for m in range(2):
            part = parts[2 * k + m]
            place(sc[SC + k], m * part.shape[0], part[...].astype(f32))
    size = parts[14].shape[0]
    for n, first in enumerate((0, 2, 1, 3)):
        place(sc[SC + 7], first * size, parts[14 + n][...].astype(f32))


def spread(sc, tiles, hidden):
    tiles = [part for tile in tiles for part in tile]
    width = tiles[0].shape[1]
    share = width // 4
    outs = [struct((share, width), f32)] * 4 + [
        struct((width, hidden), f32),
        struct((hidden, width), f32),
    ]
    return one_step(
        spread_kernel,
        (sc, *tiles),
        [whole_block(*t.shape) for t in tiles],
        outs,
        "spread",
        1 << 30,
    )


def shards(
    layer_input, ln1_gain, ln1_bias, w_query, b_query, w_key, w_value, b_value, sub_gain, sub_bias,
    w_out, b_out, ln2_gain, ln2_bias, w_up, b_up, w_down, b_down, cotangent, row_lengths,
):
    rows_local, slice_width = layer_input.shape
    head_share = w_query.shape[1]
    local_heads = head_share // HEAD_DIM
    head_pos = lax.axis_index("head")
    seq_pos = lax.axis_index("seq")
    n_seq = lax.axis_size("seq")
    width = head_share * lax.axis_size("head")
    quarter = rows_local // 4
    relative = jnp.stack([head_pos, head_pos ^ 1, head_pos ^ 2, head_pos ^ 3]).astype(jnp.int32)
    row2 = lambda v: v.reshape(1, -1)

    input_whole = lax.all_gather(layer_input, "head", axis=1, tiled=True)
    hat1, rs1 = norm_parts(input_whole.astype(f32))
    normed = (hat1 * ln1_gain + ln1_bias).astype(bf16)
    pair = lambda a, b: jnp.stack(
        [a.reshape(-1, local_heads, HEAD_DIM), b.reshape(-1, local_heads, HEAD_DIM)], axis=2
    ).reshape(-1, 2 * head_share)
    w_kv = pair(w_key, w_value)
    b_kv = pair(jnp.zeros_like(b_value), b_value)
    kv = (dot(normed, w_kv) + b_kv).astype(bf16)
    queries = (dot(normed, w_query) + b_query).astype(bf16)

    feats, nf, sc = features(rows_local * n_seq, row_lengths, local_heads, rows_local)
    kv, cotangent, pack_in = lax.optimization_barrier((kv, cotangent, (w_out, sub_gain, sub_bias)))
    if n_seq == 8:
        (att, lse, *msgs), kv_tiles, g_whole, packs = ring_attend(
            queries, feats, nf, kv, sc, cotangent, pack_in, head_pos
        )
    else:
        kv_tiles = lax.all_gather(kv, "seq", axis=0)
        att, lse, *msgs = attend_fwd(queries, feats, nf, kv_tiles, sc, n_seq)
        g_whole, packs = head_columns(head_whole(cotangent), head_pos), head_whole(out_pack(*pack_in))

    pieces = head_pieces(*msgs)
    nm, middle, sub = mid1(
        relative, pieces, packs, input_whole, row2(b_out), row2(ln2_gain), row2(ln2_bias)
    )
    nms = head_pieces(nm, nm, nm, nm)
    *held, out0, out1, dn0, dn1 = ffn(
        relative, 0, nms[:2], g_whole, w_up, w_down, row2(b_up), []
    )
    nm_all, act, d_inner, out2, out3, dn2, dn3 = ffn(
        relative, 1, nms[2:], g_whole, w_up, w_down, row2(b_up), held
    )
    outs, dn = (out0, out1, out2, out3), head_pieces(dn0, dn1, dn2, dn3)
    gw_up = dot(nm_all, d_inner, TN).astype(bf16)
    gw_down = dot(act, g_whole, TN).astype(bf16)
    early = jnp.concatenate([v.reshape(8, -1, v.shape[1]) for v in (gw_up, gw_down)], axis=1)
    early = early.reshape(-1, early.shape[2])
    early, dn = lax.optimization_barrier((early, dn))
    if n_seq == 8:
        early = lax.psum_scatter(early, "seq", scatter_dimension=0, tiled=True)
    d_mid, dbr, *d_msgs, vec768, vec192 = mid2(
        relative, pieces, packs, middle, g_whole, row2(ln2_gain), dn
    )
    d_pieces = head_pieces(*d_msgs)
    beside = (dbr, [sub[r] for r in range(4)])

    if n_seq == 8:
        dq, dkv, beside = ring_attend_back(
            queries, feats, nf, kv_tiles, d_pieces, att, lse, sc, beside
        )
    else:
        dq, dkv_tiles = attend_bwd(queries, feats, nf, d_pieces, att, lse, kv_tiles, sc, n_seq)
        dkv = lax.psum_scatter(dkv_tiles, "seq", scatter_dimension=0, tiled=False)
        beside = head_pieces(*[beside[0]] * 4), head_pieces(*beside[1])
        early = lax.psum(early, "seq")
    dbr_all, sub_all = (jnp.concatenate(v, axis=0) for v in beside)

    gw_out = dot(sub_all, dbr_all, TN).astype(bf16)
    gw_query = dot(dq, normed, TN).astype(bf16)
    gb_out = jnp.sum(dbr_all.astype(f32), axis=0)
    gb_up = jnp.sum(d_inner.astype(f32), axis=0)
    gb_down = jnp.sum(g_whole.astype(f32), axis=0)
    gw_kv = dot(dkv, normed, TN).astype(bf16).reshape(local_heads, 2, HEAD_DIM, width)
    gw_kv = jnp.concatenate([gw_kv[:, k].reshape(head_share, width) for k in range(2)], axis=0)
    late = jnp.concatenate([gw_query, gw_kv, gw_out], axis=0)
    late, dkv = lax.optimization_barrier((late, dkv))
    dn = dot(dq, w_query, NT) + dot(dkv, w_kv, NT)
    gb_kv = jnp.sum(dkv.astype(f32), axis=0)
    gb_qkv = jnp.concatenate([jnp.sum(dq.astype(f32), axis=0), gb_kv])
    split = lambda v: jnp.sum(
        jnp.where(relative[:, None, None] == jnp.arange(4)[None, :, None], v[:, None, :], 0.0), axis=0
    ).reshape(-1)
    fill = lambda v: jnp.concatenate([v, jnp.zeros((width - v.shape[0],), f32)])
    small = jnp.stack(
        [
            jnp.sum(dn * hat1, axis=0),
            jnp.sum(dn, axis=0),
            vec768[0],
            vec768[1],
            split(vec192[:4]),
            split(vec192[4:]),
        ]
    )
    more = jnp.stack([gb_up, gb_down, gb_out, fill(gb_qkv)])
    dn = dn.astype(bf16).reshape(2, 2, quarter, width)
    core, chip = head_pos % 2, head_pos // 2
    mine = lax.dynamic_index_in_dim(dn, core, 1, False)
    mate = lax.dynamic_index_in_dim(dn, 1 - core, 1, False)
    hold = lax.optimization_barrier

    if n_seq == 8:
        late = halve(late, 1)
        small = small + lax.ppermute(small, "head", CORE)
        small = small + lax.ppermute(small, "head", CROSS)
        late, small, more, mine, mate = hold((late, small, more, mine, mate))
        mate = lax.ppermute(mate, "head", CORE)
        small = jnp.concatenate([small, more], axis=0)
        small = small + lax.ppermute(small, "seq", exchange(1))
        late = halve(late, 2)
        mine = add_low(mine, mate)
        late, mine, small = hold((late, mine, small))
        far = lax.ppermute(lax.dynamic_index_in_dim(mine, 1 - chip, 0, False), "head", CROSS)
        small = small + lax.ppermute(small, "seq", exchange(2))
        late = halve(late, 4)
        tile = jnp.concatenate([late, early], axis=0)
        half = tile.shape[0] // 2
        tile, small, outs = hold((tile, small, outs))
        a = [tile[:half], tile[half:]]
        b, tiles = a, [a]
        for step in range(3):
            if step == 1:
                a[1], small, outs = hold((a[1], small, outs))
                small = small + lax.ppermute(small, "seq", exchange(4))
                core_terms = [lax.ppermute(outs[k], "head", CORE) for k in (1, 3)]
                cross_term = lax.ppermute(add_low(outs[2], core_terms[1]), "head", CROSS)
                outs = outs[0], core_terms[0], cross_term
            a = [lax.ppermute(v, "seq", FWD) for v in a]
            b = [lax.ppermute(v, "seq", BWD) for v in b]
            tiles += [a, b]
        tiles.append([lax.ppermute(v[: half // 2], "seq", FWD) for v in a])
        tiles.append([lax.ppermute(v[half // 2 :], "seq", BWD) for v in b])
        gw_query, gw_key, gw_value, gw_out, gw_up, gw_down = spread(sc, tiles, w_up.shape[1])
    else:
        mine = add_low(mine, lax.ppermute(mate, "head", CORE))
        far = lax.ppermute(lax.dynamic_index_in_dim(mine, 1 - chip, 0, False), "head", CROSS)
        small = small + lax.ppermute(small, "head", CORE)
        small = small + lax.ppermute(small, "head", CROSS)
        small = lax.psum(jnp.concatenate([small, more], axis=0), "seq")
        outs = head_pieces(*outs)
        late = lax.psum(late, "seq").astype(f32)
        gw_query, gw_key, gw_value, gw_out = (
            late[k * head_share : (k + 1) * head_share] for k in range(4)
        )
        early = early.astype(f32).reshape(8, 2, -1, width)
        gw_up, gw_down = early[:, 0].reshape(-1, width), early[:, 1].reshape(-1, width)

    y = middle + (sum(t.astype(f32) for t in outs) + b_down)
    dn = lax.dynamic_index_in_dim(mine, chip, 0, False).astype(f32) + far.astype(f32)
    cut = lambda v: lax.dynamic_slice_in_dim(v, head_pos * quarter, quarter, 0)
    d_in = d_mid + norm_back(dn * ln1_gain, cut(hat1), cut(rs1))
    both = lax.all_to_all(jnp.stack([y, d_in]).astype(bf16), "head", 2, 1, tiled=True)
    layer_output, grad_input = both[0], both[1].astype(f32)

    gb_qkv = small[9]
    own = lambda v: lax.dynamic_slice_in_dim(v, head_pos * head_share, head_share, 0)
    gb_value = gb_qkv[head_share : 3 * head_share].reshape(local_heads, 2, HEAD_DIM)[:, 1].reshape(-1)
    return (
        layer_output,
        grad_input,
        small[0],
        small[1],
        gw_query.T,
        gb_qkv[:head_share],
        gw_key.T,
        gw_value.T,
        gb_value,
        own(small[4]),
        own(small[5]),
        gw_out,
        small[8],
        small[2],
        small[3],
        gw_up,
        small[6],
        gw_down,
        small[7],
    )


def solution(mesh):
    cols, rows, both, shared, vec = P(None, "head"), P("head", None), P("seq", "head"), P(), P("head")
    in_specs = (
        both, shared, shared, cols, vec, cols, cols, vec, vec, vec,
        rows, shared, shared, shared, cols, vec, rows, shared, both, shared,
    )
    out_specs = (
        both, both, shared, shared, cols, vec, cols, cols, vec, vec,
        vec, rows, shared, shared, shared, cols, vec, rows, shared,
    )
    return jax.shard_map(shards, mesh=mesh, in_specs=in_specs, out_specs=out_specs, check_vma=False)
```
